32 devices in a mesh: level: 8 (over y, x, core), slab: 4 (over z).
Axes of the slice: x: 2, y: 2, z: 4, core: 2. Of those that a mesh axis runs over, the one named last changes fastest.
Arguments:
- right_side: float32 [16, 128, 512], P('slab', 'level'), may hold values from -6 to 6
- scale_field: float32 [16, 128, 512], P('slab', 'level'), may hold values from 0.7 to 1.4
- mass_field: float32 [16, 128, 512], P('slab', 'level'), may hold values from 0.05 to 0.5
- degrees: int32 [3], replicated, may hold values from 2 to 6, as said below
- lower_bound: float32 [3], replicated, may hold values from 0.05 to 0.3
- upper_bound: float32 [3], replicated, may hold values from 2 to 2.6
Outputs:
- solution: float32 [16, 128, 512], P('slab', 'level')
- final_res: float32 [16, 128, 512], P('slab', 'level')
The draws below stay inside these ranges and needn't reach their ends.
Inputs may be any that keep to these rules, and one draw needn't show every extreme that they name: `degrees`: degree of each grid; in every draw at least one grid has degree exactly 6.
All inputs are finite; a program needn't handle non-finite values.
Results may differ from the reference program's by a relative error of at most 0.0001.
Values sent between devices are 32-bit elements; how exact they have to be, the bound alone decides.
No kernel may reach another device: no remote copies, remote signals or barrier semaphores. Data moves between devices by JAX's collectives and lax.ppermute only.
A program may use at most 128 MiB of HBM per device.

```python
import math
import jax
import jax.numpy as jnp

NY = 512
GRIDS = 3
CYCLES = 3
MAXDEG = 6
NZ = 16
NX = 128


def draw_degrees(key, part):
    first_key, second_key = jax.random.split(jax.random.fold_in(key, 17))
    values = jax.random.randint(first_key, (GRIDS,), 2, MAXDEG + 1)
    chosen = jax.random.randint(second_key, (), 0, GRIDS)
    return jnp.where(jnp.arange(GRIDS) == chosen, MAXDEG, values).astype(jnp.int32)


def levels(key, extent, shards, least, largest):
    level, own = 1.0, jax.random.fold_in(key, 6)
    for axis_at, parts in shards:
        steps = jnp.exp(jax.random.uniform(jax.random.fold_in(own, axis_at), (parts,), jnp.float32, least / len(shards), largest / len(shards)))
        level = level * jnp.repeat(steps, extent[axis_at] // parts).reshape([-1 if axis == axis_at else 1 for axis in range(len(extent))])
    return level


def bell_draw(key, dims, scale, limit, pieces=(), held_as=jnp.bfloat16):
    level = levels(key, dims, pieces, -0.22, 0.18) if pieces else 1.0
    result = jax.random.normal(key, dims, jnp.float32) * scale * level
    return jnp.minimum(jnp.maximum(result, -limit), limit).astype(held_as)


def setup_inputs(seed: int = 0) -> dict:
    seeds = jax.random.split(jax.random.key(seed), 7)
    right_side = bell_draw(seeds[0], (NZ, NX, NY), 1.0, 6.0, ((0, 4), (1, 8)), jnp.float32)
    scale_field = jnp.clip(jnp.exp(math.log(1.4) - 0.6931472 * jax.random.uniform(seeds[1], (NZ, NX, NY), jnp.float32) ** levels(seeds[1], (NZ, NX, NY), ((0, 4), (1, 8)), -0.2, 0.2)), 0.7, 1.4)
    mass_field = jnp.clip(jnp.exp(math.log(0.5) - 2.3025851 * jax.random.uniform(seeds[2], (NZ, NX, NY), jnp.float32) ** levels(seeds[2], (NZ, NX, NY), ((0, 4), (1, 8)), -0.2, 0.2)), 0.05, 0.5)
    degrees = draw_degrees(jax.random.fold_in(seeds[6], 71), 0)
    lower_bound = jnp.clip(jax.random.uniform(seeds[4], (GRIDS,), jnp.float32, 0.05, 0.3), 0.05, 0.3)
    upper_bound = jnp.clip(jax.random.uniform(seeds[5], (GRIDS,), jnp.float32, 2.0, 2.6), 2.0, 2.6)
    return dict(right_side=right_side, scale_field=scale_field, mass_field=mass_field, degrees=degrees, lower_bound=lower_bound, upper_bound=upper_bound)


def box_sum(padded):
    summed = padded[:-2] + padded[1:-1] + padded[2:]
    summed = summed[:, :-2] + summed[:, 1:-1] + summed[:, 2:]
    return summed[:, :, :-2] + summed[:, :, 1:-1] + summed[:, :, 2:]


def operate(field, coeff, mass_term):
    weighted = coeff * field
    padded = jnp.pad(weighted, 1)
    return coeff * ((27.0 / 26.0) * weighted - box_sum(padded) / 26.0) + mass_term * field


def average_cells(field):
    size_z, size_x, size_y = field.shape
    blocks = field.reshape(size_z // 2, 2, size_x // 2, 2, size_y // 2, 2)
    return jnp.mean(blocks, axis=(1, 3, 5))


def prolong(field):
    size_z, size_x, size_y = field.shape
    spread_out = jnp.broadcast_to(field[:, None, :, None, :, None], (size_z, 2, size_x, 2, size_y, 2))
    return spread_out.reshape(2 * size_z, 2 * size_x, 2 * size_y)


def smooth(source, coeff, mass_term, degree, bound_low, bound_high):
    inverse = 1.0 / (coeff * coeff + mass_term)
    centre = (bound_high + bound_low) * 0.5
    radius = (bound_high - bound_low) * 0.5
    spread_ratio = centre / radius
    direction = inverse * source / centre
    approx = direction
    rho_now = 1.0 / spread_ratio
    for step_no in range(1, MAXDEG):
        defect = source - operate(approx, coeff, mass_term)
        rho_new = 1.0 / (2.0 * spread_ratio - rho_now)
        new_dir = rho_new * rho_now * direction + (2.0 * rho_new / radius) * inverse * defect
        active = step_no < degree
        approx = jnp.where(active, approx + new_dir, approx)
        direction = jnp.where(active, new_dir, direction)
        rho_now = jnp.where(active, rho_new, rho_now)
    return approx


def reference(right_side, scale_field, mass_field, degrees, lower_bound, upper_bound):
    scale_mid = average_cells(scale_field)
    mass_mid = average_cells(mass_field)
    scale_low = average_cells(scale_mid)
    mass_low = average_cells(mass_mid)
    solution = jnp.zeros_like(right_side)
    for cycle_no in range(CYCLES):
        if cycle_no == 0:
            resid = right_side
        else:
            resid = right_side - operate(solution, scale_field, mass_field)
        resid_mid = 4.0 * average_cells(resid)
        resid_low = 4.0 * average_cells(resid_mid)
        fine_corr = smooth(resid, scale_field, mass_field, degrees[0], lower_bound[0], upper_bound[0])
        mid_corr = smooth(resid_mid, scale_mid, mass_mid, degrees[1], lower_bound[1], upper_bound[1])
        low_corr = smooth(resid_low, scale_low, mass_low, degrees[2], lower_bound[2], upper_bound[2])
        solution = solution + 0.5 * (fine_corr + prolong(mid_corr + prolong(low_corr)))
    final_res = right_side - operate(solution, scale_field, mass_field)
    return solution, final_res
```

```python
import jax
import jax.numpy as jnp
from jax import lax
from jax.experimental import pallas as pl
from jax.experimental.pallas import tpu as pltpu
from jax.sharding import PartitionSpec as P

CYCLES = 3
MAXDEG = 6
INTERPRET = False

F32 = jnp.float32
CH = 4
OUT = 12
XH = 9
MH = 6
LH = 6
YH = 64


def dot(a, b):
    return jnp.dot(a, b, precision=lax.Precision.HIGHEST, preferred_element_type=F32)


def blocks(ref, rows):
    return jnp.concatenate([ref[b, rows, :] for b in range(ref.shape[0])], axis=1)


def put_blocks(ref, rows, value):
    for b in range(ref.shape[0]):
        ref[b, rows, :] = value[:, 128 * b : 128 * b + 128]


def iota(shape, dim):
    return lax.broadcasted_iota(jnp.int32, shape, dim)


def zy_sum(w, nz):
    rows, lanes = w.shape
    at_z = iota(w.shape, 0) & (nz - 1)
    at_y = iota(w.shape, 1)
    up = jnp.where(at_z == 0, 0.0, pltpu.roll(w, 1, 0))
    down = jnp.where(at_z == nz - 1, 0.0, pltpu.roll(w, rows - 1, 0))
    s = w + up + down
    left = jnp.where(at_y == 0, 0.0, pltpu.roll(s, 1, 1))
    right = jnp.where(at_y == lanes - 1, 0.0, pltpu.roll(s, lanes - 1, 1))
    return s + left + right


class Geometry:
    def __init__(self, shape, ns, nl):
        self.nz, self.nx, self.NY = shape
        self.ns, self.nl = ns, nl
        self.NZ = self.nz * ns
        self.ny = self.NY // ns
        self.WY = min(self.NY, -(-(self.ny + 2 * YH) // 128) * 128)
        self.PW = -(-self.ny // 128) * 128
        self.nxm, self.nxl = self.nx // 2, self.nx // 4
        self.NZm, self.NZl = self.NZ // 2, self.NZ // 4
        self.WYm, self.NYm, self.NYl = self.WY // 2, self.NY // 2, self.NY // 4
        self.PF = self.nx + 2 * OUT
        self.PM = self.nxm + 2 * MH
        self.PL = self.nxl + 2 * LH
        assert self.nx % CH == 0 and OUT % CH == 0 and XH <= self.nx
        assert self.nxl < LH <= 2 * self.nxl and MH <= self.nxm
        assert (self.nxl * self.nz // 4) % 4 == 0 and self.WYm % 128 == 0 and self.NYl % 128 == 0
        self.lowrows = self.nxl * (self.nz // 4)
        self.packrows = 3 * self.nz * self.nx + -(-3 * self.lowrows // 8) * 8

    def start(self, s):
        return jnp.clip(s * self.ny - (self.WY - self.ny) // 2, 0, self.NY - self.WY)


def vmem_call(kernel, outs, scratch, smem, args):
    specs = [pl.BlockSpec(memory_space=pltpu.SMEM)] * smem
    specs += [pl.BlockSpec(memory_space=pltpu.VMEM)] * (len(args) - smem)
    return pl.pallas_call(
        kernel,
        out_shape=[jax.ShapeDtypeStruct(o, F32) for o in outs],
        in_specs=specs,
        out_specs=[pl.BlockSpec(memory_space=pltpu.VMEM)] * len(outs),
        scratch_shapes=[pltpu.VMEM(o, F32) for o in scratch],
        interpret=INTERPRET,
    )(*args)


def pack_kernel(g, idx, b, c, q, *outs):
    s = idx[0]
    lane_pick = jnp.where(
        iota((g.NY, g.NYl), 0) // 4 == iota((g.NY, g.NYl), 1), 1.0, 0.0
    ).astype(F32)
    row_pick = jnp.where(
        iota((g.nxl, g.nx), 1) // 4 == iota((g.nxl, g.nx), 0), 1.0 / 64.0, 0.0
    ).astype(F32)
    base = 3 * g.nz * g.nx
    for k in range(g.ns):
        outs[k][base:, :] = jnp.zeros((g.packrows - base, g.WY), F32)
    for a, arr in enumerate((b, c, q)):
        for zl in range(g.nz // 4):
            col = arr[4 * zl] + arr[4 * zl + 1] + arr[4 * zl + 2] + arr[4 * zl + 3]
            low = dot(row_pick, dot(col, lane_pick))
            at = base + a * g.lowrows + zl * g.nxl
            for k in range(g.ns):
                outs[k][at : at + g.nxl, : g.NYl] = low
    for k in range(g.ns):
        partner = lax.rem(s - k + g.ns, g.ns)
        turn = lax.rem(g.NY - g.start(partner), g.NY)
        for a, arr in enumerate((b, c, q)):
            for z in range(g.nz):
                at = (a * g.nz + z) * g.nx
                outs[k][at : at + g.nx, :] = pltpu.roll(arr[z], turn, 1)[:, : g.WY]


def fine_to_mid(src, row, planes, nz, scale):
    n = planes * nz // 2
    lanes = src.shape[0] * 128
    v = blocks(src, pl.ds(row, n, stride=2)) + blocks(src, pl.ds(row + 1, n, stride=2))
    v = v.reshape(planes // 2, 2, nz // 2, lanes)
    v = (v[:, 0] + v[:, 1]).reshape(planes // 2 * (nz // 2), lanes)
    half = (lanes, lanes // 2)
    pick = jnp.where(iota(half, 0) // 2 == iota(half, 1), scale / 8.0, 0.0).astype(F32)
    return dot(v, pick)


def assemble_kernel(g, idx, *refs):
    s = idx[0]
    recv = refs[: g.ns]
    f_out, m_out, l_out, to_left, to_right, fs = refs[g.ns :]
    base = 3 * g.nz * g.nx
    for j in range(g.ns):
        src = lax.rem(s + j, g.ns)
        for a in range(3):
            for z in range(g.nz):
                at = (a * g.nz + z) * g.nx
                rows = pl.ds(src * g.nz + z, g.nx, stride=g.NZ)
                put_blocks(fs.at[a], rows, recv[j][at : at + g.nx, :])
            for zl in range(g.nz // 4):
                at = base + a * g.lowrows + zl * g.nxl
                for x in range(g.nxl):
                    l_out[a, pl.ds(x * g.NZl + src * (g.nz // 4) + zl, 1), :] = recv[j][
                        at + x : at + x + 1, : g.NYl
                    ]
    nxz = g.nx * g.NZ
    for a in range(3):
        f_out[a] = blocks(fs.at[a], slice(0, nxz))
        m_out[a] = fine_to_mid(fs.at[a], 0, g.nx, g.NZ, 1.0)
    n = XH * g.NZ
    at = 0
    for a in range(3):
        for y in range(0, g.WY, 128):
            to_left[at : at + n, :] = f_out[a, 0:n, y : y + 128]
            to_right[at : at + n, :] = f_out[a, nxz - n :, y : y + 128]
            at += n
    n, total = MH * g.NZm, g.nxm * g.NZm
    for a in range(3):
        for y in range(0, g.WYm, 128):
            to_left[at : at + n, :] = m_out[a, 0:n, y : y + 128]
            to_right[at : at + n, :] = m_out[a, total - n :, y : y + 128]
            at += n
    n = g.nxl * g.NZl
    for a in range(3):
        for y in range(0, g.NYl, 128):
            to_left[at : at + n, :] = l_out[a, :, y : y + 128]
            to_right[at : at + n, :] = l_out[a, :, y : y + 128]
            at += n


def edge_rows(g):
    return (
        3 * XH * g.NZ * (g.WY // 128)
        + 3 * MH * g.NZm * (g.WYm // 128)
        + 3 * g.nxl * g.NZl * (g.NYl // 128)
    )


def coefficients(b, c, q):
    diag = c * c + q
    inv = 1.0 / diag
    scaled = (27.0 / 26.0 * (c * c) + q) * inv
    return diag, inv, scaled, c * inv / 26.0


def small_smooth(level, degs, tab, nz, gi, c, D, K, y, d, t):
    rows = c.shape[0]
    first = gi[...] * tab[level, 0]
    y[...] = first
    d[...] = first

    def turn(j, carry):
        t[nz : nz + rows, :] = zy_sum(c[...] * y[...], nz)
        box = t[0:rows, :] + t[nz : nz + rows, :] + t[2 * nz : 2 * nz + rows, :]
        e = gi[...] - D[...] * y[...] + K[...] * box
        nd = tab[level, j] * d[...] + tab[level, MAXDEG + j] * e
        d[...] = nd
        y[...] = y[...] + nd
        return carry

    lax.fori_loop(1, degs[level], turn, 0)


def fine_boxes(g, first, last, c, x, t):
    n = CH * g.NZ

    def turn(k, carry):
        r = pl.ds(pl.multiple_of(k * n, n), n)
        t[pl.ds(pl.multiple_of(g.NZ + k * n, g.NZ), n), :] = zy_sum(c[r, :] * x[r, :], g.NZ)
        return carry

    lax.fori_loop(first, last, turn, 0)


def box_at(g, t, k):
    n = CH * g.NZ
    parts = [t[pl.ds(pl.multiple_of(k * n + o * g.NZ, g.NZ), n), :] for o in range(3)]
    return parts[0] + parts[1] + parts[2]


def fine_smooth(g, reach, degs, tab, gi, c, D, K, y, d, t):
    n = CH * g.NZ
    side, own = OUT // CH, g.nx // CH
    inner = slice((side - 2) * n, (side + own + 2) * n)
    y[inner, :] = gi[inner, :] * tab[0, 0]
    d[inner, :] = y[inner, :]

    def turn(j, carry):
        radius = reach + degs[0] - 1 - j
        ht = (radius + 1 + CH - 1) // CH
        h = (radius + CH - 1) // CH
        fine_boxes(g, side - ht, side + own + ht, c, y, t)

        def chunk(k, inner_carry):
            r = pl.ds(pl.multiple_of(k * n, n), n)
            old = y[r, :]
            e = gi[r, :] - D[r, :] * old + K[r, :] * box_at(g, t, k)
            nd = tab[0, j] * d[r, :] + tab[0, MAXDEG + j] * e
            d[r, :] = nd
            y[r, :] = old + nd
            return inner_carry

        lax.fori_loop(side - h, side + own + h, chunk, 0)
        return carry

    lax.fori_loop(1, degs[0], turn, 0)


def clear_box_edges(g, t, tm, tl):
    zeros = jnp.zeros((g.NZ + CH * g.NZ, g.WY), F32)
    t[0 : zeros.shape[0], :] = zeros
    t[t.shape[0] - zeros.shape[0] :, :] = zeros
    for ref, nz in ((tm, g.NZm), (tl, g.NZl)):
        zeros = jnp.zeros((nz, ref.shape[1]), F32)
        ref[0:nz, :] = zeros
        ref[ref.shape[0] - nz :, :] = zeros


def coarse_correction(g, s, ym, yl, zd):
    planes = g.nxm + 2
    rows = planes * g.NZm
    shape = (rows, g.PL * g.NZl)
    row, col = iota(shape, 0), iota(shape, 1)
    plane = row // g.NZm + (2 * LH - 1)
    want = (plane // 2) * g.NZl + (row % g.NZm) // 2
    up_rows = jnp.where(col == want, 1.0, 0.0).astype(F32)
    shape = (g.NYl, g.WYm)
    off = g.start(s) // 4
    up_lanes = jnp.where(
        iota(shape, 0) == off + iota(shape, 1) // 2, 1.0, 0.0
    ).astype(F32)
    low = dot(dot(up_rows, yl[...]), up_lanes)
    at = (MH - 1) * g.NZm
    both = ym[at : at + rows, :] + low
    shape = (g.WYm, g.WY)
    wide = jnp.where(iota(shape, 0) == iota(shape, 1) // 2, 1.0, 0.0).astype(F32)
    v = dot(both, wide)
    put_blocks(zd, pl.ds(0, rows, stride=2), v)
    put_blocks(zd, pl.ds(1, rows, stride=2), v)


def doubled(g, zd, plane, planes):
    at = (plane // 2 + 1) * g.NZ
    v = blocks(zd, slice(at, at + planes // 2 * g.NZ)).reshape(planes // 2, 1, g.NZ, g.WY)
    v = jnp.broadcast_to(v, (planes // 2, 2, g.NZ, g.WY))
    return v.reshape(planes * g.NZ, g.WY)


def first_kernel(g, idx, degs, tab, f, m, l, from_l, from_r, from_l2, from_r2, *refs):
    (c, D, K, bi, diag, cm, Dm, Km, im, cl, Dl, Kl, il, x, xl, xr) = refs[:16]
    (y, d, t, gm, ym, dm, tm, gl, yl, dl, tl, zd) = refs[16:]
    s, li = idx[0], idx[1]
    clear_box_edges(g, t, tm, tl)
    fill = (0.0, 0.0, 1.0)

    def kept(ok, v, a):
        return jnp.where(ok, v, fill[a])

    n, own = XH * g.NZ, g.nx * g.NZ
    lo, hi = OUT * g.NZ, (OUT + g.nx) * g.NZ
    at = 0
    region = (bi, c, diag)
    for a in range(3):
        region[a][0 : lo - n, :] = jnp.full((lo - n, g.WY), fill[a], F32)
        region[a][hi + n :, :] = jnp.full((lo - n, g.WY), fill[a], F32)
        region[a][lo:hi, :] = f[a]
        for yy in range(0, g.WY, 128):
            region[a][lo - n : lo, yy : yy + 128] = kept(li > 0, from_l[at : at + n, :], a)
            region[a][hi : hi + n, yy : yy + 128] = kept(
                li < g.nl - 1, from_r[at : at + n, :], a
            )
            at += n
    step = CH * g.NZ

    def build(k, carry):
        r = pl.ds(pl.multiple_of(k * step, step), step)
        b0, c0, q0 = bi[r, :], c[r, :], diag[r, :]
        dg, inv, sc, kk = coefficients(b0, c0, q0)
        diag[r, :] = dg
        bi[r, :] = b0 * inv
        D[r, :] = sc
        K[r, :] = kk
        return carry

    lax.fori_loop(0, g.PF // CH, build, 0)

    n = MH * g.NZm
    parts = []
    for a in range(3):
        halves = []
        for yy in range(0, g.WYm, 128):
            halves.append(
                (
                    kept(li > 0, from_l[at : at + n, :], a),
                    kept(li < g.nl - 1, from_r[at : at + n, :], a),
                )
            )
            at += n
        left = jnp.concatenate([v[0] for v in halves], axis=1)
        right = jnp.concatenate([v[1] for v in halves], axis=1)
        parts.append(jnp.concatenate([left, m[a], right], axis=0))
    _, inv, sc, kk = coefficients(*parts)
    cm[...] = parts[1]
    Dm[...] = sc
    Km[...] = kk
    im[...] = inv
    gm[...] = 4.0 * parts[0] * inv

    n = g.nxl * g.NZl
    far = (LH - g.nxl) * g.NZl
    store = (gl, cl, il)
    at2 = 0
    for a in range(3):
        for yy in range(0, g.NYl, 128):
            lanes = slice(yy, yy + 128)
            ref = store[a]
            ref[0:far, lanes] = kept(li > 1, from_l2[at2 : at2 + far, :], a)
            ref[far : far + n, lanes] = kept(li > 0, from_l[at : at + n, :], a)
            ref[far + n : far + 2 * n, lanes] = l[a, :, lanes]
            ref[far + 2 * n : far + 3 * n, lanes] = kept(
                li < g.nl - 1, from_r[at : at + n, :], a
            )
            ref[far + 3 * n :, lanes] = kept(li < g.nl - 2, from_r2[at2 : at2 + far, :], a)
            at += n
            at2 += far
    _, inv, sc, kk = coefficients(gl[...], cl[...], il[...])
    Dl[...] = sc
    Kl[...] = kk
    il[...] = inv
    gl[...] = 16.0 * gl[...] * inv

    fine_smooth(g, 0, degs, tab, bi, c, D, K, y, d, t)
    small_smooth(1, degs, tab, g.NZm, gm, cm, Dm, Km, ym, dm, tm)
    small_smooth(2, degs, tab, g.NZl, gl, cl, Dl, Kl, yl, dl, tl)
    coarse_correction(g, s, ym, yl, zd)
    for p in range(0, g.nx, CH):
        r = slice(p * g.NZ, (p + CH) * g.NZ)
        rr = slice((OUT + p) * g.NZ, (OUT + p + CH) * g.NZ)
        x[r, :] = 0.5 * (y[rr, :] + doubled(g, zd, p, CH))
    n = XH * g.NZ
    xl[...] = x[0:n, :]
    xr[...] = x[own - n :, :]


def defect_kernel(g, idx, x, xl, xr, c, D, K, bi, diag, *refs):
    gi, rm, rl, to_left, to_right, xs, t, res = refs
    s = idx[0]
    n, own = XH * g.NZ, g.nx * g.NZ
    lo, hi = OUT * g.NZ, (OUT + g.nx) * g.NZ
    zeros = jnp.zeros((lo - n, g.WY), F32)
    xs[0 : lo - n, :] = zeros
    xs[hi + n :, :] = zeros
    xs[lo - n : lo, :] = xl[...]
    xs[lo:hi, :] = x[...]
    xs[hi : hi + n, :] = xr[...]
    side, chunks = OUT // CH, g.nx // CH
    fine_boxes(g, 0, g.PF // CH, c, xs, t)
    step = CH * g.NZ

    def turn(k, carry):
        r = pl.ds(pl.multiple_of(k * step, step), step)
        v = bi[r, :] - D[r, :] * xs[r, :] + K[r, :] * box_at(g, t, k)
        gi[r, :] = v
        put_blocks(res, r, v * diag[r, :])
        return carry

    lax.fori_loop(side - 2, side + chunks + 2, turn, 0)
    planes = g.nx + 4 * CH
    mid = fine_to_mid(res, (OUT - 2 * CH) * g.NZ, planes, g.NZ, 4.0)
    rm[...] = mid
    lowp = planes // 4
    shape = (lowp * g.NZl, planes // 2 * g.NZm)
    row, col = iota(shape, 0), iota(shape, 1)
    same_x = col // (2 * g.NZm) == row // g.NZl
    same_z = (col % g.NZm) // 2 == row % g.NZl
    rows = jnp.where(same_x & same_z, 0.5, 0.0).astype(F32)
    shape = (g.WYm, g.NYl)
    off = g.start(s) // 4
    lanes = jnp.where(iota(shape, 0) // 2 + off == iota(shape, 1), 1.0, 0.0).astype(F32)
    low = dot(dot(rows, mid), lanes)
    rl[...] = low
    a = 2 * g.NZm
    w = g.WYm
    q = (CH + g.nxm - MH) * g.NZm
    to_right[0:a, 0:w] = rm[q : q + a, :]
    q = (CH + MH - 2) * g.NZm
    to_left[0:a, 0:w] = rm[q : q + a, :]
    e = (LH - 2) * g.NZl
    q = (2 + g.nxl - LH) * g.NZl
    to_right[a : a + e, 0 : g.NYl] = rl[q : q + e, :]
    q = (2 + 2) * g.NZl
    to_left[a : a + e, 0 : g.NYl] = rl[q : q + e, :]


def fine_kernel(g, reach, degs, tab, gi, c, D, K, yo, y, d, t):
    zeros = jnp.zeros((g.NZ + CH * g.NZ, g.WY), F32)
    t[0 : zeros.shape[0], :] = zeros
    t[t.shape[0] - zeros.shape[0] :, :] = zeros
    fine_smooth(g, reach, degs, tab, gi, c, D, K, y, d, t)
    yo[...] = y[(OUT - 2) * g.NZ : (OUT + g.nx + 2) * g.NZ, :]


def coarse_parts(g, degs, tab, rm, rl, from_l, from_r, coefs, scr):
    cm, Dm, Km, im, cl, Dl, Kl, il = coefs
    gm, ym, dm, tm, gl, yl, dl, tl = scr
    for ref, nz in ((tm, g.NZm), (tl, g.NZl)):
        zeros = jnp.zeros((nz, ref.shape[1]), F32)
        ref[0:nz, :] = zeros
        ref[ref.shape[0] - nz :, :] = zeros
    a, n = 2 * g.NZm, rm.shape[0]
    gm[0:a, :] = from_l[0:a, 0 : g.WYm]
    gm[a : a + n, :] = rm[...]
    gm[a + n :, :] = from_r[0:a, 0 : g.WYm]
    gm[...] = gm[...] * im[...]
    e, n = (LH - 2) * g.NZl, rl.shape[0]
    gl[0:e, :] = from_l[a : a + e, 0 : g.NYl]
    gl[e : e + n, :] = rl[...]
    gl[e + n :, :] = from_r[a : a + e, 0 : g.NYl]
    gl[...] = gl[...] * il[...]
    small_smooth(1, degs, tab, g.NZm, gm, cm, Dm, Km, ym, dm, tm)
    small_smooth(2, degs, tab, g.NZl, gl, cl, Dl, Kl, yl, dl, tl)


def combine_kernel(g, idx, degs, tab, rm, rl, from_l, from_r, yf, xo, *refs):
    coefs, outs, scr = refs[:8], refs[8:11], refs[11:]
    x, xl, xr = outs
    zd = scr[8]
    coarse_parts(g, degs, tab, rm, rl, from_l, from_r, coefs, scr[:8])
    coarse_correction(g, idx[0], scr[1], scr[5], zd)
    for p in range(0, g.nx, CH):
        r = slice(p * g.NZ, (p + CH) * g.NZ)
        rr = slice((2 + p) * g.NZ, (2 + p + CH) * g.NZ)
        x[r, :] = xo[r, :] + 0.5 * (yf[rr, :] + doubled(g, zd, p, CH))
    n, own = XH * g.NZ, g.nx * g.NZ
    xl[...] = x[0:n, :]
    xr[...] = x[own - n :, :]


def last_kernel(g, idx, degs, tab, rm, rl, from_l, from_r, yf, xo, xlo, xro, *refs):
    coefs, refs = refs[:8], refs[8:]
    c, D, K, bi, diag = refs[:5]
    packs, scr = refs[5 : 5 + g.ns], refs[5 + g.ns :]
    zd, xs, t, fin, xb = scr[8:]
    s = idx[0]
    coarse_parts(g, degs, tab, rm, rl, from_l, from_r, coefs, scr[:8])
    coarse_correction(g, s, scr[1], scr[5], zd)
    two = 2 * g.NZ
    nh, own = XH * g.NZ, g.nx * g.NZ
    xs[0:two, :] = xlo[nh - two :, :] + 0.5 * (yf[0:two, :] + doubled(g, zd, -2, 2))
    for p in range(0, g.nx, CH):
        r = slice(p * g.NZ, (p + CH) * g.NZ)
        rr = slice((2 + p) * g.NZ, (2 + p + CH) * g.NZ)
        v = xo[r, :] + 0.5 * (yf[rr, :] + doubled(g, zd, p, CH))
        xs[rr, :] = v
        put_blocks(xb, r, v)
    xs[two + own :, :] = xro[0:two, :] + 0.5 * (
        yf[two + own :, :] + doubled(g, zd, g.nx, 2)
    )
    base = (OUT - 2) * g.NZ
    part = (g.nx + 4) * g.NZ // 5
    for at in range(0, 5 * part, part):
        r = slice(at, at + part)
        t[r, :] = zy_sum(c[base + at : base + at + part, :] * xs[r, :], g.NZ)
    lo = OUT * g.NZ
    step = CH * g.NZ
    for at in range(0, own, step):
        up = two + at
        box = (
            t[up - g.NZ : up - g.NZ + step, :]
            + t[up : up + step, :]
            + t[up + g.NZ : up + g.NZ + step, :]
        )
        r = slice(lo + at, lo + at + step)
        v = bi[r, :] - D[r, :] * xs[up : up + step, :] + K[r, :] * box
        put_blocks(fin, slice(at, at + step), v * diag[r, :])
    shift = lax.rem(g.WY - (s * g.ny - g.start(s)), g.WY)
    for k in range(g.ns):
        partner = lax.rem(s - k + g.ns, g.ns)
        for o, ref in enumerate((xb, fin)):
            for z in range(g.nz):
                v = blocks(ref, pl.ds(partner * g.nz + z, g.nx, stride=g.NZ))
                at = (o * g.nz + z) * g.nx
                packs[k][at : at + g.nx, :] = pltpu.roll(v, shift, 1)[:, : g.PW]


def unpack_kernel(g, idx, *refs):
    s = idx[0]
    recv, outs = refs[: g.ns], refs[g.ns :]
    for o in range(2):
        for z in range(g.nz):
            at = (o * g.nz + z) * g.nx
            total = None
            if g.ny % 128 == 0:
                wide = jnp.concatenate(
                    [recv[j][at : at + g.nx, : g.ny] for j in range(g.ns)], axis=1
                )
                total = pltpu.roll(wide, s * g.ny, 1)
            else:
                mine = iota((g.nx, g.NY), 1) < g.ny
                for j in range(g.ns):
                    src = lax.rem(s + j, g.ns)
                    v = recv[j][at : at + g.nx, :]
                    pad = jnp.zeros((g.nx, g.NY - g.PW), F32)
                    v = jnp.where(mine, jnp.concatenate([v, pad], axis=1), 0.0)
                    v = pltpu.roll(v, src * g.ny, 1)
                    total = v if total is None else total + v
            outs[o][z] = total


def ring(value, axis, by):
    peers = lax.axis_size(axis)
    if by % peers == 0:
        return value
    return lax.ppermute(value, axis, [(i, (i - by) % peers) for i in range(peers)])


def sweep_tables(lower, upper):
    centre = (upper + lower) * 0.5
    radius = (upper - lower) * 0.5
    ratio = centre / radius
    rho = 1.0 / ratio
    alphas, betas = [], []
    for _ in range(1, MAXDEG):
        new = 1.0 / (2.0 * ratio - rho)
        alphas.append(new * rho)
        betas.append(2.0 * new / radius)
        rho = new
    zero = jnp.zeros_like(rho)
    return jnp.stack([1.0 / centre] + alphas + [zero] + betas, axis=1)


def shards(right_side, scale_field, mass_field, degrees, lower_bound, upper_bound):
    g = Geometry(right_side.shape, lax.axis_size("slab"), lax.axis_size("level"))
    idx = jnp.stack([lax.axis_index("slab"), lax.axis_index("level")]).astype(jnp.int32)
    tab = sweep_tables(lower_bound, upper_bound)

    def call(kernel, outs, scratch, smem, *args):
        return vmem_call(
            lambda *refs: kernel(g, *refs), outs, scratch, smem, args
        )

    packs = call(
        pack_kernel, [(g.packrows, g.WY)] * g.ns, [], 1,
        idx, right_side, scale_field, mass_field,
    )
    packs = [ring(v, "slab", k) for k, v in enumerate(packs)]

    fine = (g.PF * g.NZ, g.WY)
    boxes = (fine[0] + 2 * g.NZ, g.WY)
    own = (g.nx * g.NZ, g.WY)
    edge = (XH * g.NZ, g.WY)
    mid = (g.PM * g.NZm, g.WYm)
    low = (g.PL * g.NZl, g.NYl)
    coarse_scr = [
        mid, mid, mid, (mid[0] + 2 * g.NZm, g.WYm),
        low, low, low, (low[0] + 2 * g.NZl, g.NYl),
    ]
    in_blocks = (g.WY // 128, fine[0], 128)
    own_blocks = (g.WY // 128, own[0], 128)
    zd = (g.WY // 128, (g.nxm + 2) * g.NZ, 128)

    f, m, l, to_left, to_right = call(
        assemble_kernel,
        [
            (3, *own), (3, g.nxm * g.NZm, g.WYm), (3, g.nxl * g.NZl, g.NYl),
            (edge_rows(g), 128), (edge_rows(g), 128),
        ],
        [(3, g.WY // 128, g.nx * g.NZ, 128)], 1, idx, *packs,
    )
    far = (LH - g.nxl) * g.NZl
    lanes = g.NYl // 128

    def far_rows(part):
        pieces = part.reshape(3, part.shape[1], lanes, 128)
        return pieces.transpose(0, 2, 1, 3).reshape(3 * lanes * far, 128)

    from_l = ring(to_right, "level", -1)
    from_r = ring(to_left, "level", 1)
    from_l2 = ring(far_rows(l[:, l.shape[1] - far :]), "level", -2)
    from_r2 = ring(far_rows(l[:, :far]), "level", 2)

    outs = call(
        first_kernel,
        [fine] * 5 + [mid] * 4 + [low] * 4 + [own, edge, edge],
        [fine, fine, boxes] + coarse_scr + [zd], 3,
        idx, degrees, tab, f, m, l, from_l, from_r, from_l2, from_r2,
    )
    c, D, K, bi, diag = outs[:5]
    coefs = outs[5:13]
    x, xl, xr = outs[13:]

    planes = g.nx + 4 * CH
    wide = max(g.WYm, g.NYl)
    payload = (2 * g.NZm + (LH - 2) * g.NZl, wide)
    for cycle_no in range(1, CYCLES):
        last = cycle_no == CYCLES - 1
        halo_l = ring(xr, "level", -1)
        halo_r = ring(xl, "level", 1)
        gi, rm, rl, to_left, to_right = call(
            defect_kernel,
            [
                fine, (planes // 2 * g.NZm, g.WYm), (planes // 4 * g.NZl, g.NYl),
                payload, payload,
            ],
            [fine, boxes, in_blocks], 1,
            idx, x, halo_l, halo_r, c, D, K, bi, diag,
        )
        from_l = ring(to_right, "level", -1)
        from_r = ring(to_left, "level", 1)
        reach = 1 if last else 0
        (yf,) = vmem_call(
            lambda *refs, reach=reach: fine_kernel(g, reach, *refs),
            [((g.nx + 4) * g.NZ, g.WY)], [fine, fine, boxes], 2,
            (degrees, tab, gi, c, D, K),
        )
        if not last:
            x, xl, xr = call(
                combine_kernel, [own, edge, edge], coarse_scr + [zd], 3,
                idx, degrees, tab, rm, rl, from_l, from_r, yf, x, *coefs,
            )
        else:
            packs = call(
                last_kernel,
                [(2 * g.nz * g.nx, g.PW)] * g.ns,
                coarse_scr
                + [zd, ((g.nx + 4) * g.NZ, g.WY), ((g.nx + 4) * g.NZ, g.WY)]
                + [own_blocks, own_blocks],
                3,
                idx, degrees, tab, rm, rl, from_l, from_r, yf, x, halo_l, halo_r,
                *coefs, c, D, K, bi, diag,
            )
    packs = [ring(v, "slab", k) for k, v in enumerate(packs)]
    shape = right_side.shape
    return tuple(call(unpack_kernel, [shape, shape], [], 1, idx, *packs))


def solution(mesh):
    spread = P("slab", "level", None)
    return jax.shard_map(
        shards,
        mesh=mesh,
        in_specs=(spread, spread, spread, P(), P(), P()),
        out_specs=(spread, spread),
        check_vma=False,
    )
```

```python
import math

import jax
import jax.numpy as jnp
from jax import lax
from jax.experimental import pallas as pl
from jax.experimental.pallas import tpu as pltpu
from jax.sharding import PartitionSpec as P

CYCLES = 3
MAXDEG = 6
INTERPRET = False

F32 = jnp.float32
CH = 4
OUT = 12
XH = 9
MH = 6
LH = 6
YH = 64


def dot(a, b):
    return jnp.dot(a, b, precision=lax.Precision.HIGHEST, preferred_element_type=F32)


def blocks(ref, rows):
    return jnp.concatenate([ref[b, rows, :] for b in range(ref.shape[0])], axis=1)


def put_blocks(ref, rows, value):
    for b in range(ref.shape[0]):
        ref[b, rows, :] = value[:, 128 * b : 128 * b + 128]


def iota(shape, dim):
    return lax.broadcasted_iota(jnp.int32, shape, dim)


def zy_sum(w, nz):
    rows, lanes = w.shape
    at_z = iota(w.shape, 0) & (nz - 1)
    at_y = iota(w.shape, 1)
    up = jnp.where(at_z == 0, 0.0, pltpu.roll(w, 1, 0))
    down = jnp.where(at_z == nz - 1, 0.0, pltpu.roll(w, rows - 1, 0))
    s = w + up + down
    left = jnp.where(at_y == 0, 0.0, pltpu.roll(s, 1, 1))
    right = jnp.where(at_y == lanes - 1, 0.0, pltpu.roll(s, lanes - 1, 1))
    return s + left + right


class Geometry:
    def __init__(self, shape, ns, nl):
        self.nz, self.nx, self.NY = shape
        self.ns, self.nl = ns, nl
        self.NZ = self.nz * ns
        self.ny = self.NY // ns
        self.WY = min(self.NY, -(-(self.ny + 2 * YH) // 128) * 128)
        self.PW = -(-self.ny // 128) * 128
        self.nxm, self.nxl = self.nx // 2, self.nx // 4
        self.NZm, self.NZl = self.NZ // 2, self.NZ // 4
        self.WYm, self.NYm, self.NYl = self.WY // 2, self.NY // 2, self.NY // 4
        self.PF = self.nx + 2 * OUT
        self.PM = self.nxm + 2 * MH
        self.PL = self.nxl + 2 * LH
        assert self.nx % CH == 0 and OUT % CH == 0 and XH <= self.nx
        assert self.nxl < LH <= 2 * self.nxl and MH <= self.nxm
        assert (self.nxl * self.nz // 4) % 4 == 0 and self.WYm % 128 == 0 and self.NYl % 128 == 0
        self.lowrows = self.nxl * (self.nz // 4)
        self.packrows = 3 * self.nz * self.nx + -(-3 * self.lowrows // 8) * 8

    def start(self, s):
        return jnp.clip(s * self.ny - (self.WY - self.ny) // 2, 0, self.NY - self.WY)


def vmem_call(kernel, outs, scratch, smem, args):
    specs = [pl.BlockSpec(memory_space=pltpu.SMEM)] * smem
    specs += [pl.BlockSpec(memory_space=pltpu.VMEM)] * (len(args) - smem)
    shapes = list(outs) + list(scratch) + [a.shape for a in args[smem:]]
    held = sum(4 * math.prod(o) for o in shapes)
    return pl.pallas_call(
        kernel,
        out_shape=[jax.ShapeDtypeStruct(o, F32) for o in outs],
        in_specs=specs,
        out_specs=[pl.BlockSpec(memory_space=pltpu.VMEM)] * len(outs),
        scratch_shapes=[pltpu.VMEM(o, F32) for o in scratch],
        compiler_params=pltpu.CompilerParams(vmem_limit_bytes=min(held * 3 // 2 + (4 << 20), 60 << 20)),
        interpret=INTERPRET,
    )(*args)


def pack_kernel(g, idx, b, c, q, *outs):
    s = idx[0]
    lane_pick = jnp.where(
        iota((g.NY, g.NYl), 0) // 4 == iota((g.NY, g.NYl), 1), 1.0, 0.0
    ).astype(F32)
    row_pick = jnp.where(
        iota((g.nxl, g.nx), 1) // 4 == iota((g.nxl, g.nx), 0), 1.0 / 64.0, 0.0
    ).astype(F32)
    base = 3 * g.nz * g.nx
    for k in range(g.ns):
        outs[k][base:, :] = jnp.zeros((g.packrows - base, g.WY), F32)
    for a, arr in enumerate((b, c, q)):
        for zl in range(g.nz // 4):
            col = arr[4 * zl] + arr[4 * zl + 1] + arr[4 * zl + 2] + arr[4 * zl + 3]
            low = dot(row_pick, dot(col, lane_pick))
            at = base + a * g.lowrows + zl * g.nxl
            for k in range(g.ns):
                outs[k][at : at + g.nxl, : g.NYl] = low
    for k in range(g.ns):
        partner = lax.rem(s - k + g.ns, g.ns)
        turn = lax.rem(g.NY - g.start(partner), g.NY)
        for a, arr in enumerate((b, c, q)):
            for z in range(g.nz):
                at = (a * g.nz + z) * g.nx
                outs[k][at : at + g.nx, :] = pltpu.roll(arr[z], turn, 1)[:, : g.WY]


def fine_to_mid(src, row, planes, nz, scale):
    n = planes * nz // 2
    lanes = src.shape[0] * 128
    v = blocks(src, pl.ds(row, n, stride=2)) + blocks(src, pl.ds(row + 1, n, stride=2))
    v = v.reshape(planes // 2, 2, nz // 2, lanes)
    v = (v[:, 0] + v[:, 1]).reshape(planes // 2 * (nz // 2), lanes)
    half = (lanes, lanes // 2)
    pick = jnp.where(iota(half, 0) // 2 == iota(half, 1), scale / 8.0, 0.0).astype(F32)
    return dot(v, pick)


def assemble_kernel(g, idx, *refs):
    s = idx[0]
    recv = refs[: g.ns]
    f_out, m_out, l_out, to_left, to_right, fs = refs[g.ns :]
    base = 3 * g.nz * g.nx
    for j in range(g.ns):
        src = lax.rem(s + j, g.ns)
        for a in range(3):
            for z in range(g.nz):
                at = (a * g.nz + z) * g.nx
                rows = pl.ds(src * g.nz + z, g.nx, stride=g.NZ)
                put_blocks(fs.at[a], rows, recv[j][at : at + g.nx, :])
            for zl in range(g.nz // 4):
                at = base + a * g.lowrows + zl * g.nxl
                for x in range(g.nxl):
                    l_out[a, pl.ds(x * g.NZl + src * (g.nz // 4) + zl, 1), :] = recv[j][
                        at + x : at + x + 1, : g.NYl
                    ]
    nxz = g.nx * g.NZ
    for a in range(3):
        f_out[a] = blocks(fs.at[a], slice(0, nxz))
        m_out[a] = fine_to_mid(fs.at[a], 0, g.nx, g.NZ, 1.0)
    n = XH * g.NZ
    at = 0
    for a in range(3):
        for y in range(0, g.WY, 128):
            to_left[at : at + n, :] = f_out[a, 0:n, y : y + 128]
            to_right[at : at + n, :] = f_out[a, nxz - n :, y : y + 128]
            at += n
    n, total = MH * g.NZm, g.nxm * g.NZm
    for a in range(3):
        for y in range(0, g.WYm, 128):
            to_left[at : at + n, :] = m_out[a, 0:n, y : y + 128]
            to_right[at : at + n, :] = m_out[a, total - n :, y : y + 128]
            at += n
    n = g.nxl * g.NZl
    for a in range(3):
        for y in range(0, g.NYl, 128):
            to_left[at : at + n, :] = l_out[a, :, y : y + 128]
            to_right[at : at + n, :] = l_out[a, :, y : y + 128]
            at += n


def edge_rows(g):
    return (
        3 * XH * g.NZ * (g.WY // 128)
        + 3 * MH * g.NZm * (g.WYm // 128)
        + 3 * g.nxl * g.NZl * (g.NYl // 128)
    )


def coefficients(b, c, q):
    diag = c * c + q
    inv = 1.0 / diag
    scaled = (27.0 / 26.0 * (c * c) + q) * inv
    return diag, inv, scaled, c * inv / 26.0


def small_smooth(level, degs, tab, nz, gi, c, D, K, y, d, t):
    rows = c.shape[0]
    first = gi[...] * tab[level, 0]
    y[...] = first
    d[...] = first

    def turn(j, carry):
        t[nz : nz + rows, :] = zy_sum(c[...] * y[...], nz)
        box = t[0:rows, :] + t[nz : nz + rows, :] + t[2 * nz : 2 * nz + rows, :]
        e = gi[...] - D[...] * y[...] + K[...] * box
        nd = tab[level, j] * d[...] + tab[level, MAXDEG + j] * e
        d[...] = nd
        y[...] = y[...] + nd
        return carry

    lax.fori_loop(1, degs[level], turn, 0)


def fine_boxes(g, first, last, c, x, t):
    n = CH * g.NZ

    def turn(k, carry):
        r = pl.ds(pl.multiple_of(k * n, n), n)
        t[pl.ds(pl.multiple_of(g.NZ + k * n, g.NZ), n), :] = zy_sum(c[r, :] * x[r, :], g.NZ)
        return carry

    lax.fori_loop(first, last, turn, 0)


def box_at(g, t, k):
    n = CH * g.NZ
    parts = [t[pl.ds(pl.multiple_of(k * n + o * g.NZ, g.NZ), n), :] for o in range(3)]
    return parts[0] + parts[1] + parts[2]


def fine_smooth(g, reach, degs, tab, gi, c, D, K, y, d, t):
    n = CH * g.NZ
    side, own = OUT // CH, g.nx // CH
    inner = slice((side - 2) * n, (side + own + 2) * n)
    y[inner, :] = gi[inner, :] * tab[0, 0]
    d[inner, :] = y[inner, :]

    def turn(j, carry):
        radius = reach + degs[0] - 1 - j
        ht = (radius + 1 + CH - 1) // CH
        h = (radius + CH - 1) // CH
        fine_boxes(g, side - ht, side + own + ht, c, y, t)

        def chunk(k, inner_carry):
            r = pl.ds(pl.multiple_of(k * n, n), n)
            old = y[r, :]
            e = gi[r, :] - D[r, :] * old + K[r, :] * box_at(g, t, k)
            nd = tab[0, j] * d[r, :] + tab[0, MAXDEG + j] * e
            d[r, :] = nd
            y[r, :] = old + nd
            return inner_carry

        lax.fori_loop(side - h, side + own + h, chunk, 0)
        return carry

    lax.fori_loop(1, degs[0], turn, 0)


def clear_box_edges(g, t, tm, tl):
    zeros = jnp.zeros((g.NZ + CH * g.NZ, g.WY), F32)
    t[0 : zeros.shape[0], :] = zeros
    t[t.shape[0] - zeros.shape[0] :, :] = zeros
    for ref, nz in ((tm, g.NZm), (tl, g.NZl)):
        zeros = jnp.zeros((nz, ref.shape[1]), F32)
        ref[0:nz, :] = zeros
        ref[ref.shape[0] - nz :, :] = zeros


def coarse_correction(g, s, ym, yl, zd):
    planes = g.nxm + 2
    rows = planes * g.NZm
    shape = (rows, g.PL * g.NZl)
    row, col = iota(shape, 0), iota(shape, 1)
    plane = row // g.NZm + (2 * LH - 1)
    want = (plane // 2) * g.NZl + (row % g.NZm) // 2
    up_rows = jnp.where(col == want, 1.0, 0.0).astype(F32)
    shape = (g.NYl, g.WYm)
    off = g.start(s) // 4
    up_lanes = jnp.where(
        iota(shape, 0) == off + iota(shape, 1) // 2, 1.0, 0.0
    ).astype(F32)
    low = dot(dot(up_rows, yl[...]), up_lanes)
    at = (MH - 1) * g.NZm
    both = ym[at : at + rows, :] + low
    shape = (g.WYm, g.WY)
    wide = jnp.where(iota(shape, 0) == iota(shape, 1) // 2, 1.0, 0.0).astype(F32)
    v = dot(both, wide)
    put_blocks(zd, pl.ds(0, rows, stride=2), v)
    put_blocks(zd, pl.ds(1, rows, stride=2), v)


def doubled(g, zd, plane, planes):
    at = (plane // 2 + 1) * g.NZ
    v = blocks(zd, slice(at, at + planes // 2 * g.NZ)).reshape(planes // 2, 1, g.NZ, g.WY)
    v = jnp.broadcast_to(v, (planes // 2, 2, g.NZ, g.WY))
    return v.reshape(planes * g.NZ, g.WY)


def first_kernel(g, idx, degs, tab, f, m, l, from_l, from_r, from_l2, from_r2, *refs):
    (c, D, K, bi, diag, cm, Dm, Km, im, cl, Dl, Kl, il, x, xl, xr) = refs[:16]
    (y, d, t, gm, ym, dm, tm, gl, yl, dl, tl, zd) = refs[16:]
    s, li = idx[0], idx[1]
    clear_box_edges(g, t, tm, tl)
    fill = (0.0, 0.0, 1.0)

    def kept(ok, v, a):
        return jnp.where(ok, v, fill[a])

    n, own = XH * g.NZ, g.nx * g.NZ
    lo, hi = OUT * g.NZ, (OUT + g.nx) * g.NZ
    at = 0
    region = (bi, c, diag)
    for a in range(3):
        region[a][0 : lo - n, :] = jnp.full((lo - n, g.WY), fill[a], F32)
        region[a][hi + n :, :] = jnp.full((lo - n, g.WY), fill[a], F32)
        region[a][lo:hi, :] = f[a]
        for yy in range(0, g.WY, 128):
            region[a][lo - n : lo, yy : yy + 128] = kept(li > 0, from_l[at : at + n, :], a)
            region[a][hi : hi + n, yy : yy + 128] = kept(
                li < g.nl - 1, from_r[at : at + n, :], a
            )
            at += n
    step = CH * g.NZ

    def build(k, carry):
        r = pl.ds(pl.multiple_of(k * step, step), step)
        b0, c0, q0 = bi[r, :], c[r, :], diag[r, :]
        dg, inv, sc, kk = coefficients(b0, c0, q0)
        diag[r, :] = dg
        bi[r, :] = b0 * inv
        D[r, :] = sc
        K[r, :] = kk
        return carry

    lax.fori_loop(0, g.PF // CH, build, 0)

    n = MH * g.NZm
    parts = []
    for a in range(3):
        halves = []
        for yy in range(0, g.WYm, 128):
            halves.append(
                (
                    kept(li > 0, from_l[at : at + n, :], a),
                    kept(li < g.nl - 1, from_r[at : at + n, :], a),
                )
            )
            at += n
        left = jnp.concatenate([v[0] for v in halves], axis=1)
        right = jnp.concatenate([v[1] for v in halves], axis=1)
        parts.append(jnp.concatenate([left, m[a], right], axis=0))
    _, inv, sc, kk = coefficients(*parts)
    cm[...] = parts[1]
    Dm[...] = sc
    Km[...] = kk
    im[...] = inv
    gm[...] = 4.0 * parts[0] * inv

    n = g.nxl * g.NZl
    far = (LH - g.nxl) * g.NZl
    store = (gl, cl, il)
    at2 = 0
    for a in range(3):
        for yy in range(0, g.NYl, 128):
            lanes = slice(yy, yy + 128)
            ref = store[a]
            ref[0:far, lanes] = kept(li > 1, from_l2[at2 : at2 + far, :], a)
            ref[far : far + n, lanes] = kept(li > 0, from_l[at : at + n, :], a)
            ref[far + n : far + 2 * n, lanes] = l[a, :, lanes]
            ref[far + 2 * n : far + 3 * n, lanes] = kept(
                li < g.nl - 1, from_r[at : at + n, :], a
            )
            ref[far + 3 * n :, lanes] = kept(li < g.nl - 2, from_r2[at2 : at2 + far, :], a)
            at += n
            at2 += far
    _, inv, sc, kk = coefficients(gl[...], cl[...], il[...])
    Dl[...] = sc
    Kl[...] = kk
    il[...] = inv
    gl[...] = 16.0 * gl[...] * inv

    fine_smooth(g, 0, degs, tab, bi, c, D, K, y, d, t)
    small_smooth(1, degs, tab, g.NZm, gm, cm, Dm, Km, ym, dm, tm)
    small_smooth(2, degs, tab, g.NZl, gl, cl, Dl, Kl, yl, dl, tl)
    coarse_correction(g, s, ym, yl, zd)
    for p in range(0, g.nx, CH):
        r = slice(p * g.NZ, (p + CH) * g.NZ)
        rr = slice((OUT + p) * g.NZ, (OUT + p + CH) * g.NZ)
        x[r, :] = 0.5 * (y[rr, :] + doubled(g, zd, p, CH))
    n = XH * g.NZ
    xl[...] = x[0:n, :]
    xr[...] = x[own - n :, :]


def defect_kernel(g, idx, x, xl, xr, c, D, K, bi, diag, *refs):
    gi, rm, rl, to_left, to_right, xs, t, res = refs
    s = idx[0]
    n, own = XH * g.NZ, g.nx * g.NZ
    lo, hi = OUT * g.NZ, (OUT + g.nx) * g.NZ
    zeros = jnp.zeros((lo - n, g.WY), F32)
    xs[0 : lo - n, :] = zeros
    xs[hi + n :, :] = zeros
    xs[lo - n : lo, :] = xl[...]
    xs[lo:hi, :] = x[...]
    xs[hi : hi + n, :] = xr[...]
    side, chunks = OUT // CH, g.nx // CH
    fine_boxes(g, 0, g.PF // CH, c, xs, t)
    step = CH * g.NZ

    def turn(k, carry):
        r = pl.ds(pl.multiple_of(k * step, step), step)
        v = bi[r, :] - D[r, :] * xs[r, :] + K[r, :] * box_at(g, t, k)
        gi[r, :] = v
        put_blocks(res, r, v * diag[r, :])
        return carry

    lax.fori_loop(side - 2, side + chunks + 2, turn, 0)
    planes = g.nx + 4 * CH
    mid = fine_to_mid(res, (OUT - 2 * CH) * g.NZ, planes, g.NZ, 4.0)
    rm[...] = mid
    lowp = planes // 4
    shape = (lowp * g.NZl, planes // 2 * g.NZm)
    row, col = iota(shape, 0), iota(shape, 1)
    same_x = col // (2 * g.NZm) == row // g.NZl
    same_z = (col % g.NZm) // 2 == row % g.NZl
    rows = jnp.where(same_x & same_z, 0.5, 0.0).astype(F32)
    shape = (g.WYm, g.NYl)
    off = g.start(s) // 4
    lanes = jnp.where(iota(shape, 0) // 2 + off == iota(shape, 1), 1.0, 0.0).astype(F32)
    low = dot(dot(rows, mid), lanes)
    rl[...] = low
    a = 2 * g.NZm
    w = g.WYm
    q = (CH + g.nxm - MH) * g.NZm
    to_right[0:a, 0:w] = rm[q : q + a, :]
    q = (CH + MH - 2) * g.NZm
    to_left[0:a, 0:w] = rm[q : q + a, :]
    e = (LH - 2) * g.NZl
    q = (2 + g.nxl - LH) * g.NZl
    to_right[a : a + e, 0 : g.NYl] = rl[q : q + e, :]
    q = (2 + 2) * g.NZl
    to_left[a : a + e, 0 : g.NYl] = rl[q : q + e, :]


def fine_kernel(g, reach, degs, tab, gi, c, D, K, yo, y, d, t):
    zeros = jnp.zeros((g.NZ + CH * g.NZ, g.WY), F32)
    t[0 : zeros.shape[0], :] = zeros
    t[t.shape[0] - zeros.shape[0] :, :] = zeros
    fine_smooth(g, reach, degs, tab, gi, c, D, K, y, d, t)
    yo[...] = y[(OUT - 2) * g.NZ : (OUT + g.nx + 2) * g.NZ, :]


def coarse_parts(g, degs, tab, rm, rl, from_l, from_r, coefs, scr):
    cm, Dm, Km, im, cl, Dl, Kl, il = coefs
    gm, ym, dm, tm, gl, yl, dl, tl = scr
    for ref, nz in ((tm, g.NZm), (tl, g.NZl)):
        zeros = jnp.zeros((nz, ref.shape[1]), F32)
        ref[0:nz, :] = zeros
        ref[ref.shape[0] - nz :, :] = zeros
    a, n = 2 * g.NZm, rm.shape[0]
    gm[0:a, :] = from_l[0:a, 0 : g.WYm]
    gm[a : a + n, :] = rm[...]
    gm[a + n :, :] = from_r[0:a, 0 : g.WYm]
    gm[...] = gm[...] * im[...]
    e, n = (LH - 2) * g.NZl, rl.shape[0]
    gl[0:e, :] = from_l[a : a + e, 0 : g.NYl]
    gl[e : e + n, :] = rl[...]
    gl[e + n :, :] = from_r[a : a + e, 0 : g.NYl]
    gl[...] = gl[...] * il[...]
    small_smooth(1, degs, tab, g.NZm, gm, cm, Dm, Km, ym, dm, tm)
    small_smooth(2, degs, tab, g.NZl, gl, cl, Dl, Kl, yl, dl, tl)


def combine_kernel(g, idx, degs, tab, rm, rl, from_l, from_r, yf, xo, *refs):
    coefs, outs, scr = refs[:8], refs[8:11], refs[11:]
    x, xl, xr = outs
    zd = scr[8]
    coarse_parts(g, degs, tab, rm, rl, from_l, from_r, coefs, scr[:8])
    coarse_correction(g, idx[0], scr[1], scr[5], zd)
    for p in range(0, g.nx, CH):
        r = slice(p * g.NZ, (p + CH) * g.NZ)
        rr = slice((2 + p) * g.NZ, (2 + p + CH) * g.NZ)
        x[r, :] = xo[r, :] + 0.5 * (yf[rr, :] + doubled(g, zd, p, CH))
    n, own = XH * g.NZ, g.nx * g.NZ
    xl[...] = x[0:n, :]
    xr[...] = x[own - n :, :]


def last_kernel(g, idx, degs, tab, rm, rl, from_l, from_r, yf, xo, xlo, xro, *refs):
    coefs, refs = refs[:8], refs[8:]
    c, D, K, bi, diag = refs[:5]
    packs, scr = refs[5 : 5 + g.ns], refs[5 + g.ns :]
    zd, xs, t, fin, xb = scr[8:]
    s = idx[0]
    coarse_parts(g, degs, tab, rm, rl, from_l, from_r, coefs, scr[:8])
    coarse_correction(g, s, scr[1], scr[5], zd)
    two = 2 * g.NZ
    nh, own = XH * g.NZ, g.nx * g.NZ
    xs[0:two, :] = xlo[nh - two :, :] + 0.5 * (yf[0:two, :] + doubled(g, zd, -2, 2))
    for p in range(0, g.nx, CH):
        r = slice(p * g.NZ, (p + CH) * g.NZ)
        rr = slice((2 + p) * g.NZ, (2 + p + CH) * g.NZ)
        v = xo[r, :] + 0.5 * (yf[rr, :] + doubled(g, zd, p, CH))
        xs[rr, :] = v
        put_blocks(xb, r, v)
    xs[two + own :, :] = xro[0:two, :] + 0.5 * (
        yf[two + own :, :] + doubled(g, zd, g.nx, 2)
    )
    base = (OUT - 2) * g.NZ
    part = (g.nx + 4) * g.NZ // 5
    for at in range(0, 5 * part, part):
        r = slice(at, at + part)
        t[r, :] = zy_sum(c[base + at : base + at + part, :] * xs[r, :], g.NZ)
    lo = OUT * g.NZ
    step = CH * g.NZ
    for at in range(0, own, step):
        up = two + at
        box = (
            t[up - g.NZ : up - g.NZ + step, :]
            + t[up : up + step, :]
            + t[up + g.NZ : up + g.NZ + step, :]
        )
        r = slice(lo + at, lo + at + step)
        v = bi[r, :] - D[r, :] * xs[up : up + step, :] + K[r, :] * box
        put_blocks(fin, slice(at, at + step), v * diag[r, :])
    shift = lax.rem(g.WY - (s * g.ny - g.start(s)), g.WY)
    for k in range(g.ns):
        partner = lax.rem(s - k + g.ns, g.ns)
        for o, ref in enumerate((xb, fin)):
            for z in range(g.nz):
                v = blocks(ref, pl.ds(partner * g.nz + z, g.nx, stride=g.NZ))
                at = (o * g.nz + z) * g.nx
                packs[k][at : at + g.nx, :] = pltpu.roll(v, shift, 1)[:, : g.PW]


def unpack_kernel(g, idx, *refs):
    s = idx[0]
    recv, outs = refs[: g.ns], refs[g.ns :]
    for o in range(2):
        for z in range(g.nz):
            at = (o * g.nz + z) * g.nx
            total = None
            if g.ny % 128 == 0:
                wide = jnp.concatenate(
                    [recv[j][at : at + g.nx, : g.ny] for j in range(g.ns)], axis=1
                )
                total = pltpu.roll(wide, s * g.ny, 1)
            else:
                mine = iota((g.nx, g.NY), 1) < g.ny
                for j in range(g.ns):
                    src = lax.rem(s + j, g.ns)
                    v = recv[j][at : at + g.nx, :]
                    pad = jnp.zeros((g.nx, g.NY - g.PW), F32)
                    v = jnp.where(mine, jnp.concatenate([v, pad], axis=1), 0.0)
                    v = pltpu.roll(v, src * g.ny, 1)
                    total = v if total is None else total + v
            outs[o][z] = total


def ring(value, axis, by):
    peers = lax.axis_size(axis)
    if by % peers == 0:
        return value
    return lax.ppermute(value, axis, [(i, (i - by) % peers) for i in range(peers)])


def sweep_tables(lower, upper):
    centre = (upper + lower) * 0.5
    radius = (upper - lower) * 0.5
    ratio = centre / radius
    rho = 1.0 / ratio
    alphas, betas = [], []
    for _ in range(1, MAXDEG):
        new = 1.0 / (2.0 * ratio - rho)
        alphas.append(new * rho)
        betas.append(2.0 * new / radius)
        rho = new
    zero = jnp.zeros_like(rho)
    return jnp.stack([1.0 / centre] + alphas + [zero] + betas, axis=1)


def shards(right_side, scale_field, mass_field, degrees, lower_bound, upper_bound):
    g = Geometry(right_side.shape, lax.axis_size("slab"), lax.axis_size("level"))
    idx = jnp.stack([lax.axis_index("slab"), lax.axis_index("level")]).astype(jnp.int32)
    tab = sweep_tables(lower_bound, upper_bound)

    def call(kernel, outs, scratch, smem, *args):
        return vmem_call(
            lambda *refs: kernel(g, *refs), outs, scratch, smem, args
        )

    packs = call(
        pack_kernel, [(g.packrows, g.WY)] * g.ns, [], 1,
        idx, right_side, scale_field, mass_field,
    )
    packs = [ring(v, "slab", k) for k, v in enumerate(packs)]

    fine = (g.PF * g.NZ, g.WY)
    boxes = (fine[0] + 2 * g.NZ, g.WY)
    own = (g.nx * g.NZ, g.WY)
    edge = (XH * g.NZ, g.WY)
    mid = (g.PM * g.NZm, g.WYm)
    low = (g.PL * g.NZl, g.NYl)
    coarse_scr = [
        mid, mid, mid, (mid[0] + 2 * g.NZm, g.WYm),
        low, low, low, (low[0] + 2 * g.NZl, g.NYl),
    ]
    in_blocks = (g.WY // 128, fine[0], 128)
    own_blocks = (g.WY // 128, own[0], 128)
    zd = (g.WY // 128, (g.nxm + 2) * g.NZ, 128)

    f, m, l, to_left, to_right = call(
        assemble_kernel,
        [
            (3, *own), (3, g.nxm * g.NZm, g.WYm), (3, g.nxl * g.NZl, g.NYl),
            (edge_rows(g), 128), (edge_rows(g), 128),
        ],
        [(3, g.WY // 128, g.nx * g.NZ, 128)], 1, idx, *packs,
    )
    far = (LH - g.nxl) * g.NZl
    lanes = g.NYl // 128

    def far_rows(part):
        pieces = part.reshape(3, part.shape[1], lanes, 128)
        return pieces.transpose(0, 2, 1, 3).reshape(3 * lanes * far, 128)

    from_l = ring(to_right, "level", -1)
    from_r = ring(to_left, "level", 1)
    from_l2 = ring(far_rows(l[:, l.shape[1] - far :]), "level", -2)
    from_r2 = ring(far_rows(l[:, :far]), "level", 2)

    outs = call(
        first_kernel,
        [fine] * 5 + [mid] * 4 + [low] * 4 + [own, edge, edge],
        [fine, fine, boxes] + coarse_scr + [zd], 3,
        idx, degrees, tab, f, m, l, from_l, from_r, from_l2, from_r2,
    )
    c, D, K, bi, diag = outs[:5]
    coefs = outs[5:13]
    x, xl, xr = outs[13:]

    planes = g.nx + 4 * CH
    wide = max(g.WYm, g.NYl)
    payload = (2 * g.NZm + (LH - 2) * g.NZl, wide)
    for cycle_no in range(1, CYCLES):
        last = cycle_no == CYCLES - 1
        halo_l = ring(xr, "level", -1)
        halo_r = ring(xl, "level", 1)
        gi, rm, rl, to_left, to_right = call(
            defect_kernel,
            [
                fine, (planes // 2 * g.NZm, g.WYm), (planes // 4 * g.NZl, g.NYl),
                payload, payload,
            ],
            [fine, boxes, in_blocks], 1,
            idx, x, halo_l, halo_r, c, D, K, bi, diag,
        )
        from_l = ring(to_right, "level", -1)
        from_r = ring(to_left, "level", 1)
        reach = 1 if last else 0
        (yf,) = vmem_call(
            lambda *refs, reach=reach: fine_kernel(g, reach, *refs),
            [((g.nx + 4) * g.NZ, g.WY)], [fine, fine, boxes], 2,
            (degrees, tab, gi, c, D, K),
        )
        if not last:
            x, xl, xr = call(
                combine_kernel, [own, edge, edge], coarse_scr + [zd], 3,
                idx, degrees, tab, rm, rl, from_l, from_r, yf, x, *coefs,
            )
        else:
            packs = call(
                last_kernel,
                [(2 * g.nz * g.nx, g.PW)] * g.ns,
                coarse_scr
                + [zd, ((g.nx + 4) * g.NZ, g.WY), ((g.nx + 4) * g.NZ, g.WY)]
                + [own_blocks, own_blocks],
                3,
                idx, degrees, tab, rm, rl, from_l, from_r, yf, x, halo_l, halo_r,
                *coefs, c, D, K, bi, diag,
            )
    packs = [ring(v, "slab", k) for k, v in enumerate(packs)]
    shape = right_side.shape
    return tuple(call(unpack_kernel, [shape, shape], [], 1, idx, *packs))


def solution(mesh):
    spread = P("slab", "level", None)
    return jax.shard_map(
        shards,
        mesh=mesh,
        in_specs=(spread, spread, spread, P(), P(), P()),
        out_specs=(spread, spread),
        check_vma=False,
    )
```

```python
import math

import jax
import jax.numpy as jnp
from jax import lax
from jax.experimental import pallas as pl
from jax.experimental.pallas import tpu as pltpu
from jax.sharding import PartitionSpec as P

CYCLES = 3
MAXDEG = 6
INTERPRET = False

F32 = jnp.float32
OUT = 8
XH = 6
MH = 6
LH = 6
YH = 64


def dot(a, b):
    return jnp.dot(a, b, precision=lax.Precision.HIGHEST, preferred_element_type=F32)


def blocks(ref, rows):
    return jnp.concatenate([ref[b, rows, :] for b in range(ref.shape[0])], axis=1)


def put_blocks(ref, rows, value):
    for b in range(ref.shape[0]):
        ref[b, rows, :] = value[:, 128 * b : 128 * b + 128]


def iota(shape, dim):
    return lax.broadcasted_iota(jnp.int32, shape, dim)


def zy_sum(w, nz):
    rows, lanes = w.shape
    at_z = iota(w.shape, 0) & (nz - 1)
    at_y = iota(w.shape, 1)
    up = jnp.where(at_z == 0, 0.0, pltpu.roll(w, 1, 0))
    down = jnp.where(at_z == nz - 1, 0.0, pltpu.roll(w, rows - 1, 0))
    s = w + up + down
    left = jnp.where(at_y == 0, 0.0, pltpu.roll(s, 1, 1))
    right = jnp.where(at_y == lanes - 1, 0.0, pltpu.roll(s, lanes - 1, 1))
    return s + left + right


class Geometry:
    def __init__(self, shape, ns, nl):
        self.nz, self.nx, self.NY = shape
        self.ns, self.nl = ns, nl
        self.NZ = self.nz * ns
        self.ny = self.NY // ns
        self.WY = min(self.NY, -(-(self.ny + 2 * YH) // 128) * 128)
        self.PW = -(-self.ny // 128) * 128
        self.nxm, self.nxl = self.nx // 2, self.nx // 4
        self.NZm, self.NZl = self.NZ // 2, self.NZ // 4
        self.WYm, self.NYm, self.NYl = self.WY // 2, self.NY // 2, self.NY // 4
        self.CH = max(1, min(4, 64 // self.NZ))
        self.PF = self.nx + 2 * OUT
        self.PM = self.nxm + 2 * MH
        self.PL = self.nxl + 2 * LH
        assert self.nx % self.CH == 0 and OUT % self.CH == 0 and XH <= self.nx
        assert self.nxl < LH <= 2 * self.nxl and MH <= self.nxm
        assert (self.nxl * self.nz // 4) % 4 == 0 and self.WYm % 128 == 0 and self.NYl % 128 == 0
        self.lowrows = self.nxl * (self.nz // 4)
        self.packrows = 3 * self.nz * self.nx + -(-3 * self.lowrows // 8) * 8

    def start(self, s):
        return jnp.clip(s * self.ny - (self.WY - self.ny) // 2, 0, self.NY - self.WY)


def vmem_call(kernel, outs, scratch, smem, args, away=False):
    place = pl.ANY if away else pltpu.VMEM
    specs = [pl.BlockSpec(memory_space=pltpu.SMEM)] * smem
    specs += [pl.BlockSpec(memory_space=place)] * (len(args) - smem)
    shapes = list(outs) + list(scratch) + [a.shape for a in args[smem:]]
    held = sum(4 * math.prod(o) for o in shapes)
    return pl.pallas_call(
        kernel,
        out_shape=[jax.ShapeDtypeStruct(o, F32) for o in outs],
        in_specs=specs,
        out_specs=[pl.BlockSpec(memory_space=pltpu.VMEM)] * len(outs),
        scratch_shapes=[pltpu.VMEM(o, F32) for o in scratch]
        + [pltpu.SemaphoreType.DMA((3,))] * away,
        compiler_params=pltpu.CompilerParams(vmem_limit_bytes=min(held * 3 // 2 + (4 << 20), 60 << 20)),
        interpret=INTERPRET,
    )(*args)


def repeat(g, n, body):
    if g.ns <= 4:
        for i in range(n):
            body(i)
    else:
        lax.fori_loop(0, n, lambda i, carry: (body(i), carry)[1], 0)


def pack_kernel(g, idx, *refs):
    far, outs = refs[:3], refs[3 : 3 + g.ns]
    near, sems = refs[3 + g.ns : 6 + g.ns], refs[6 + g.ns]
    copies = [
        pltpu.make_async_copy(far[a], near[a], sems.at[a]) for a in range(3)
    ]
    for copy in copies:
        copy.start()
    s = idx[0]
    lane_pick = jnp.where(
        iota((g.NY, g.NYl), 0) // 4 == iota((g.NY, g.NYl), 1), 1.0, 0.0
    ).astype(F32)
    row_pick = jnp.where(
        iota((g.nxl, g.nx), 1) // 4 == iota((g.nxl, g.nx), 0), 1.0 / 64.0, 0.0
    ).astype(F32)
    base = 3 * g.nz * g.nx
    for k in range(g.ns):
        outs[k][base:, :] = jnp.zeros((g.packrows - base, g.WY), F32)
    turns = []
    for k in range(g.ns):
        partner = lax.rem(s - k + g.ns, g.ns)
        turns.append(lax.rem(g.NY - g.start(partner), g.NY))
    for a in range(3):
        copies[a].wait()
        arr = near[a]
        for k in range(g.ns):

            def row(z, a=a, k=k, arr=arr):
                at = (a * g.nz + z) * g.nx
                if not isinstance(at, int):
                    at = pl.multiple_of(at, 8)
                v = pltpu.roll(arr[z], turns[k], 1)[:, : g.WY]
                outs[k][pl.ds(at, g.nx), :] = v

            repeat(g, g.nz, row)
    for a in range(3):
        arr = near[a]
        for zl in range(g.nz // 4):
            col = arr[4 * zl] + arr[4 * zl + 1] + arr[4 * zl + 2] + arr[4 * zl + 3]
            low = dot(row_pick, dot(col, lane_pick))
            at = base + a * g.lowrows + zl * g.nxl
            for k in range(g.ns):
                outs[k][at : at + g.nxl, : g.NYl] = low


def fine_to_mid(src, row, planes, nz, scale):
    n = planes * nz // 2
    lanes = src.shape[0] * 128
    v = blocks(src, pl.ds(row, n, stride=2)) + blocks(src, pl.ds(row + 1, n, stride=2))
    v = v.reshape(planes // 2, 2, nz // 2, lanes)
    v = (v[:, 0] + v[:, 1]).reshape(planes // 2 * (nz // 2), lanes)
    half = (lanes, lanes // 2)
    pick = jnp.where(iota(half, 0) // 2 == iota(half, 1), scale / 8.0, 0.0).astype(F32)
    return dot(v, pick)


def assemble_kernel(g, idx, *refs):
    s = idx[0]
    recv = refs[: g.ns]
    f_out, m_out, l_out, to_left, to_right, fs = refs[g.ns :]
    base = 3 * g.nz * g.nx
    for j in range(g.ns):
        src = lax.rem(s + j, g.ns)
        for a in range(3):

            def row(z, a=a, j=j, src=src):
                at = (a * g.nz + z) * g.nx
                if not isinstance(at, int):
                    at = pl.multiple_of(at, 8)
                rows = pl.ds(src * g.nz + z, g.nx, stride=g.NZ)
                put_blocks(fs.at[a], rows, recv[j][pl.ds(at, g.nx), :])

            repeat(g, g.nz, row)
            for zl in range(g.nz // 4):
                at = base + a * g.lowrows + zl * g.nxl
                for x in range(g.nxl):
                    l_out[a, pl.ds(x * g.NZl + src * (g.nz // 4) + zl, 1), :] = recv[j][
                        at + x : at + x + 1, : g.NYl
                    ]
    nxz = g.nx * g.NZ
    for a in range(3):
        f_out[a] = blocks(fs.at[a], slice(0, nxz))
        m_out[a] = fine_to_mid(fs.at[a], 0, g.nx, g.NZ, 1.0)
    n = XH * g.NZ
    at = 0
    for a in range(3):
        for y in range(0, g.WY, 128):
            to_left[at : at + n, :] = f_out[a, 0:n, y : y + 128]
            to_right[at : at + n, :] = f_out[a, nxz - n :, y : y + 128]
            at += n
    n, total = MH * g.NZm, g.nxm * g.NZm
    for a in range(3):
        for y in range(0, g.WYm, 128):
            to_left[at : at + n, :] = m_out[a, 0:n, y : y + 128]
            to_right[at : at + n, :] = m_out[a, total - n :, y : y + 128]
            at += n
    n = g.nxl * g.NZl
    for a in range(3):
        for y in range(0, g.NYl, 128):
            to_left[at : at + n, :] = l_out[a, :, y : y + 128]
            to_right[at : at + n, :] = l_out[a, :, y : y + 128]
            at += n


def edge_rows(g):
    return (
        3 * XH * g.NZ * (g.WY // 128)
        + 3 * MH * g.NZm * (g.WYm // 128)
        + 3 * g.nxl * g.NZl * (g.NYl // 128)
    )


def coefficients(b, c, q):
    diag = c * c + q
    inv = 1.0 / diag
    scaled = (27.0 / 26.0 * (c * c) + q) * inv
    return diag, inv, scaled, c * inv / 26.0


def coarse_smooth(g, idx, tab, mid, low):
    for level, (gi, c, D, K, y, d, t) in ((1, mid), (2, low)):
        y[...] = gi[...] * tab[level, 0]
        d[...] = y[...]

    def turn(j, carry):
        for level, nz, (gi, c, D, K, y, d, t) in ((1, g.NZm, mid), (2, g.NZl, low)):
            rows = c.shape[0]
            t[nz : nz + rows, :] = zy_sum(c[...] * y[...], nz)
        for level, nz, (gi, c, D, K, y, d, t) in ((1, g.NZm, mid), (2, g.NZl, low)):
            rows = c.shape[0]
            box = t[0:rows, :] + t[nz : nz + rows, :] + t[2 * nz : 2 * nz + rows, :]
            e = gi[...] - D[...] * y[...] + K[...] * box
            nd = tab[level, j] * d[...] + tab[level, MAXDEG + j] * e
            d[...] = nd
            y[...] = y[...] + nd
        return carry

    lax.fori_loop(1, jnp.maximum(idx[3], idx[4]), turn, 0)


def fine_smooth(g, idx, tab, gi, c, D, K, y, d, t):
    n = g.CH * g.NZ
    side, own = OUT // g.CH, g.nx // g.CH
    y[...] = gi[...] * tab[0, 0]
    d[...] = y[...]

    def turn(j, carry):
        radius = idx[2] - j
        ht = (radius + 1 + g.CH - 1) // g.CH
        h = (radius + g.CH - 1) // g.CH
        fine_boxes(g, side - ht, side + own + ht, c, y, t)

        def chunk(k, inner_carry):
            r = pl.ds(pl.multiple_of(k * n, n), n)
            old = y[r, :]
            e = gi[r, :] - D[r, :] * old + K[r, :] * box_at(g, t, k)
            nd = tab[0, j] * d[r, :] + tab[0, MAXDEG + j] * e
            d[r, :] = nd
            y[r, :] = old + nd
            return inner_carry

        lax.fori_loop(side - h, side + own + h, chunk, 0)
        return carry

    lax.fori_loop(1, idx[2], turn, 0)


def clear_box_edges(g, t, tm, tl):
    for ref, nz in ((t, g.NZ), (tm, g.NZm), (tl, g.NZl)):
        zeros = jnp.zeros((nz, ref.shape[1]), F32)
        ref[0:nz, :] = zeros
        ref[ref.shape[0] - nz :, :] = zeros


def fine_boxes(g, first, last, c, x, t):
    n = g.CH * g.NZ

    def turn(k, carry):
        r = pl.ds(pl.multiple_of(k * n, n), n)
        t[pl.ds(pl.multiple_of(g.NZ + k * n, g.NZ), n), :] = zy_sum(c[r, :] * x[r, :], g.NZ)
        return carry

    lax.fori_loop(first, last, turn, 0)


def box_at(g, t, k):
    n = g.CH * g.NZ
    parts = [t[pl.ds(pl.multiple_of(k * n + o * g.NZ, g.NZ), n), :] for o in range(3)]
    return parts[0] + parts[1] + parts[2]


def coarse_correction(g, s, ym, yl, zd):
    planes = g.nxm + 2
    rows = planes * g.NZm
    shape = (rows, g.PL * g.NZl)
    row, col = iota(shape, 0), iota(shape, 1)
    plane = row // g.NZm + (2 * LH - 1)
    want = (plane // 2) * g.NZl + (row % g.NZm) // 2
    up_rows = jnp.where(col == want, 1.0, 0.0).astype(F32)
    shape = (g.NYl, g.WYm)
    off = g.start(s) // 4
    up_lanes = jnp.where(
        iota(shape, 0) == off + iota(shape, 1) // 2, 1.0, 0.0
    ).astype(F32)
    low = dot(dot(up_rows, yl[...]), up_lanes)
    at = (MH - 1) * g.NZm
    both = ym[at : at + rows, :] + low
    shape = (g.WYm, g.WY)
    wide = jnp.where(iota(shape, 0) == iota(shape, 1) // 2, 1.0, 0.0).astype(F32)
    v = dot(both, wide)
    put_blocks(zd, pl.ds(0, rows, stride=2), v)
    put_blocks(zd, pl.ds(1, rows, stride=2), v)


def doubled(g, zd, plane, planes):
    at = (plane + 2) // 2 * g.NZ
    if planes == 1:
        return blocks(zd, slice(at, at + g.NZ))
    v = blocks(zd, slice(at, at + planes // 2 * g.NZ)).reshape(planes // 2, 1, g.NZ, g.WY)
    v = jnp.broadcast_to(v, (planes // 2, 2, g.NZ, g.WY))
    return v.reshape(planes * g.NZ, g.WY)


def pieces(g):
    return [(-1, 1)] + [(p, g.CH) for p in range(0, g.nx, g.CH)] + [(g.nx, 1)]


def cycle(g, idx, tab, fine, mid, low, x_old, x, bi, diag, zd, keep, xb=None):
    gi, c, D, K, y, d, t = fine
    fine_smooth(g, idx, tab, *fine)
    coarse_smooth(g, idx, tab, mid, low)
    coarse_correction(g, idx[0], mid[4], low[4], zd)
    for p, planes in pieces(g):
        n = planes * g.NZ
        rr = slice((OUT + p) * g.NZ, (OUT + p) * g.NZ + n)
        r = slice((1 + p) * g.NZ, (1 + p) * g.NZ + n)
        v = 0.5 * (y[rr, :] + doubled(g, zd, p, planes))
        if x_old is not None:
            v = x_old[r, :] + v
        x[r, :] = v
        if xb is not None and planes == g.CH and 0 <= p < g.nx:
            put_blocks(xb, slice(p * g.NZ, p * g.NZ + n), v)
        t[r, :] = zy_sum(c[rr, :] * v, g.NZ)
    step = g.CH * g.NZ
    for p in range(0, g.nx, g.CH):
        at = p * g.NZ
        box = (
            t[at : at + step, :]
            + t[at + g.NZ : at + g.NZ + step, :]
            + t[at + 2 * g.NZ : at + 2 * g.NZ + step, :]
        )
        r = slice(at, at + step)
        rr = slice(OUT * g.NZ + at, OUT * g.NZ + at + step)
        v = bi[r, :] - D[rr, :] * x[at + g.NZ : at + g.NZ + step, :] + K[rr, :] * box
        keep(r, v, v * diag[r, :])


def send_defect(g, s, gi, rm, rl, res, to_l, to_r, to_l2, to_r2):
    rm[...] = fine_to_mid(res, 0, g.nx, g.NZ, 4.0)
    shape = (g.nxl * g.NZl, g.nxm * g.NZm)
    row, col = iota(shape, 0), iota(shape, 1)
    same_x = col // (2 * g.NZm) == row // g.NZl
    same_z = (col % g.NZm) // 2 == row % g.NZl
    rows = jnp.where(same_x & same_z, 0.5, 0.0).astype(F32)
    shape = (g.WYm, g.NYl)
    off = g.start(s) // 4
    lanes = jnp.where(iota(shape, 0) // 2 + off == iota(shape, 1), 1.0, 0.0).astype(F32)
    rl[...] = dot(dot(rows, rm[...]), lanes)
    at = 0
    for ref, n in ((gi, XH * g.NZ), (rm, MH * g.NZm), (rl, g.nxl * g.NZl)):
        total = ref.shape[0]
        for y in range(0, ref.shape[1], 128):
            to_l[at : at + n, :] = ref[0:n, y : y + 128]
            to_r[at : at + n, :] = ref[total - n :, y : y + 128]
            at += n
    far = (LH - g.nxl) * g.NZl
    total = rl.shape[0]
    for b in range(g.NYl // 128):
        lanes = slice(128 * b, 128 * b + 128)
        to_l2[b * far : b * far + far, :] = rl[0:far, lanes]
        to_r2[b * far : b * far + far, :] = rl[total - far :, lanes]


def first_kernel(g, idx, tab, f, m, l, from_l, from_r, from_l2, from_r2, *refs):
    (c, D, K, bi, diag, cm, Dm, Km, im, cl, Dl, Kl, il) = refs[:13]
    x, gi_own, rm, rl, to_l, to_r, to_l2, to_r2 = refs[13:21]
    (gi, y, d, t, gm, ym, dm, tm, gl, yl, dl, tl, zd, res) = refs[21:]
    s, li = idx[0], idx[1]
    clear_box_edges(g, t, tm, tl)
    fill = (0.0, 0.0, 1.0)

    def kept(ok, v, a):
        return jnp.where(ok, v, fill[a])

    n, own = XH * g.NZ, g.nx * g.NZ
    lo, hi = OUT * g.NZ, (OUT + g.nx) * g.NZ
    at = 0
    region = (gi, c, y)
    for a in range(3):
        region[a][0 : lo - n, :] = jnp.full((lo - n, g.WY), fill[a], F32)
        region[a][hi + n :, :] = jnp.full((lo - n, g.WY), fill[a], F32)
        region[a][lo:hi, :] = f[a]
        for yy in range(0, g.WY, 128):
            region[a][lo - n : lo, yy : yy + 128] = kept(li > 0, from_l[at : at + n, :], a)
            region[a][hi : hi + n, yy : yy + 128] = kept(
                li < g.nl - 1, from_r[at : at + n, :], a
            )
            at += n
    step = g.CH * g.NZ
    side = OUT // g.CH

    def build(k, carry):
        r = pl.ds(pl.multiple_of(k * step, step), step)
        b0 = gi[r, :]
        dg, inv, sc, kk = coefficients(b0, c[r, :], y[r, :])
        gi[r, :] = b0 * inv
        D[r, :] = sc
        K[r, :] = kk
        y[r, :] = dg
        return carry

    lax.fori_loop(0, g.PF // g.CH, build, 0)
    bi[...] = gi[lo:hi, :]
    diag[...] = y[lo:hi, :]

    n = MH * g.NZm
    parts = []
    for a in range(3):
        halves = []
        for yy in range(0, g.WYm, 128):
            halves.append(
                (
                    kept(li > 0, from_l[at : at + n, :], a),
                    kept(li < g.nl - 1, from_r[at : at + n, :], a),
                )
            )
            at += n
        left = jnp.concatenate([v[0] for v in halves], axis=1)
        right = jnp.concatenate([v[1] for v in halves], axis=1)
        parts.append(jnp.concatenate([left, m[a], right], axis=0))
    _, inv, sc, kk = coefficients(*parts)
    cm[...] = parts[1]
    Dm[...] = sc
    Km[...] = kk
    im[...] = inv
    gm[...] = 4.0 * parts[0] * inv

    n = g.nxl * g.NZl
    far = (LH - g.nxl) * g.NZl
    store = (gl, cl, il)
    at2 = 0
    for a in range(3):
        for yy in range(0, g.NYl, 128):
            lanes = slice(yy, yy + 128)
            ref = store[a]
            ref[0:far, lanes] = kept(li > 1, from_l2[at2 : at2 + far, :], a)
            ref[far : far + n, lanes] = kept(li > 0, from_l[at : at + n, :], a)
            ref[far + n : far + 2 * n, lanes] = l[a, :, lanes]
            ref[far + 2 * n : far + 3 * n, lanes] = kept(
                li < g.nl - 1, from_r[at : at + n, :], a
            )
            ref[far + 3 * n :, lanes] = kept(li < g.nl - 2, from_r2[at2 : at2 + far, :], a)
            at += n
            at2 += far
    _, inv, sc, kk = coefficients(gl[...], cl[...], il[...])
    Dl[...] = sc
    Kl[...] = kk
    il[...] = inv
    gl[...] = 16.0 * gl[...] * inv

    def keep(r, scaled, plain):
        gi_own[r, :] = scaled
        put_blocks(res, r, plain)

    fine = (gi, c, D, K, y, d, t)
    mid = (gm, cm, Dm, Km, ym, dm, tm)
    low = (gl, cl, Dl, Kl, yl, dl, tl)
    cycle(g, idx, tab, fine, mid, low, None, x, bi, diag, zd, keep)
    send_defect(g, s, gi_own, rm, rl, res, to_l, to_r, to_l2, to_r2)


def gather_defect(g, gi_own, rm, rl, from_l, from_r, from_l2, from_r2, gi, gm, im, gl, il):
    lo, hi = OUT * g.NZ, (OUT + g.nx) * g.NZ
    n = XH * g.NZ
    zeros = jnp.zeros((lo - n, g.WY), F32)
    gi[0 : lo - n, :] = zeros
    gi[hi + n :, :] = zeros
    gi[lo:hi, :] = gi_own[...]
    at = 0
    for y in range(0, g.WY, 128):
        gi[lo - n : lo, y : y + 128] = from_l[at : at + n, :]
        gi[hi : hi + n, y : y + 128] = from_r[at : at + n, :]
        at += n
    n, own = MH * g.NZm, rm.shape[0]
    for y in range(0, g.WYm, 128):
        lanes = slice(y, y + 128)
        gm[0:n, lanes] = from_l[at : at + n, :] * im[0:n, lanes]
        gm[n + own :, lanes] = from_r[at : at + n, :] * im[n + own :, lanes]
        at += n
    gm[n : n + own, :] = rm[...] * im[n : n + own, :]
    n = g.nxl * g.NZl
    far = (LH - g.nxl) * g.NZl
    for b in range(g.NYl // 128):
        lanes = slice(128 * b, 128 * b + 128)
        rows = slice(b * far, b * far + far)
        gl[0:far, lanes] = from_l2[rows, :]
        gl[far : far + n, lanes] = from_l[at : at + n, :]
        gl[far + n : far + 2 * n, lanes] = rl[:, lanes]
        gl[far + 2 * n : far + 3 * n, lanes] = from_r[at : at + n, :]
        gl[far + 3 * n :, lanes] = from_r2[rows, :]
        at += n
    gl[...] = gl[...] * il[...]


def cycle_kernel(g, n_outs, idx, tab, *refs):
    gi_own, rm, rl, x_old = refs[:4]
    received = refs[4:8]
    (c, D, K, bi, diag, cm, Dm, Km, im, cl, Dl, Kl, il) = refs[8:21]
    outs = refs[21 : 21 + n_outs]
    scr = refs[21 + n_outs :]
    (gi, y, d, t, gm, ym, dm, tm, gl, yl, dl, tl, zd, res) = scr[:14]
    clear_box_edges(g, t, tm, tl)
    gather_defect(g, gi_own, rm, rl, *received, gi, gm, im, gl, il)
    fine = (gi, c, D, K, y, d, t)
    mid = (gm, cm, Dm, Km, ym, dm, tm)
    low = (gl, cl, Dl, Kl, yl, dl, tl)
    s = idx[0]
    if len(scr) == 14:
        x, gi_new, rm_new, rl_new = outs[:4]

        def keep(r, scaled, plain):
            gi_new[r, :] = scaled
            put_blocks(res, r, plain)

        cycle(g, idx, tab, fine, mid, low, x_old, x, bi, diag, zd, keep)
        send_defect(g, s, gi_new, rm_new, rl_new, res, *outs[4:])
        return
    x, xb = scr[14:]

    def keep_plain(r, scaled, plain):
        put_blocks(res, r, plain)

    cycle(g, idx, tab, fine, mid, low, x_old, x, bi, diag, zd, keep_plain, xb)
    shift = lax.rem(g.WY - (s * g.ny - g.start(s)), g.WY)
    for k in range(g.ns):
        partner = lax.rem(s - k + g.ns, g.ns)
        for o, ref in enumerate((xb, res)):

            def row(z, o=o, ref=ref, k=k, partner=partner):
                v = blocks(ref, pl.ds(partner * g.nz + z, g.nx, stride=g.NZ))
                at = (o * g.nz + z) * g.nx
                if not isinstance(at, int):
                    at = pl.multiple_of(at, 8)
                outs[k][pl.ds(at, g.nx), :] = pltpu.roll(v, shift, 1)[:, : g.PW]

            repeat(g, g.nz, row)


def unpack_kernel(g, idx, *refs):
    s = idx[0]
    recv, outs = refs[: g.ns], refs[g.ns :]
    for o in range(2):
        for z in range(g.nz):
            at = (o * g.nz + z) * g.nx
            total = None
            if g.ny % 128 == 0:
                wide = jnp.concatenate(
                    [recv[j][at : at + g.nx, : g.ny] for j in range(g.ns)], axis=1
                )
                total = pltpu.roll(wide, s * g.ny, 1)
            else:
                mine = iota((g.nx, g.NY), 1) < g.ny
                for j in range(g.ns):
                    src = lax.rem(s + j, g.ns)
                    v = recv[j][at : at + g.nx, :]
                    pad = jnp.zeros((g.nx, g.NY - g.PW), F32)
                    v = jnp.where(mine, jnp.concatenate([v, pad], axis=1), 0.0)
                    v = pltpu.roll(v, src * g.ny, 1)
                    total = v if total is None else total + v
            outs[o][z] = total


def ring(value, axis, by):
    peers = lax.axis_size(axis)
    if by % peers == 0:
        return value
    return lax.ppermute(value, axis, [(i, (i - by) % peers) for i in range(peers)])


def sweep_tables(degrees, lower, upper):
    centre = (upper + lower) * 0.5
    radius = (upper - lower) * 0.5
    ratio = centre / radius
    rho = 1.0 / ratio
    alphas, betas = [], []
    for j in range(1, MAXDEG):
        new = 1.0 / (2.0 * ratio - rho)
        active = j < degrees
        alphas.append(jnp.where(active, new * rho, 0.0))
        betas.append(jnp.where(active, 2.0 * new / radius, 0.0))
        rho = new
    zero = jnp.zeros_like(rho)
    return jnp.stack([1.0 / centre] + alphas + [zero] + betas, axis=1)


def shards(right_side, scale_field, mass_field, degrees, lower_bound, upper_bound):
    g = Geometry(right_side.shape, lax.axis_size("slab"), lax.axis_size("level"))
    place = jnp.stack([lax.axis_index("slab"), lax.axis_index("level")])
    idx = jnp.concatenate([place.astype(jnp.int32), degrees])
    tab = sweep_tables(degrees, lower_bound, upper_bound)

    def call(kernel, outs, scratch, smem, *args, away=False):
        return vmem_call(
            lambda *refs: kernel(g, *refs), outs, scratch, smem, args, away
        )

    shape = right_side.shape
    packs = call(
        pack_kernel, [(g.packrows, g.WY)] * g.ns, [shape] * 3, 1,
        idx, right_side, scale_field, mass_field, away=True,
    )
    packs = [ring(v, "slab", k) for k, v in enumerate(packs)]

    fine = (g.PF * g.NZ, g.WY)
    own = (g.nx * g.NZ, g.WY)
    mid = (g.PM * g.NZm, g.WYm)
    low = (g.PL * g.NZl, g.NYl)
    own_blocks = (g.WY // 128, own[0], 128)
    scratch = [
        fine, fine, fine, (fine[0] + 2 * g.NZ, g.WY),
        mid, mid, mid, (mid[0] + 2 * g.NZm, g.WYm),
        low, low, low, (low[0] + 2 * g.NZl, g.NYl),
        (g.WY // 128, (g.nxm + 2) * g.NZ, 128), own_blocks,
    ]

    f, m, l, to_left, to_right = call(
        assemble_kernel,
        [
            (3, *own), (3, g.nxm * g.NZm, g.WYm), (3, g.nxl * g.NZl, g.NYl),
            (edge_rows(g), 128), (edge_rows(g), 128),
        ],
        [(3, *own_blocks)], 1, idx, *packs,
    )
    far = (LH - g.nxl) * g.NZl
    lanes = g.NYl // 128

    def far_rows(part):
        parts = part.reshape(3, part.shape[1], lanes, 128)
        return parts.transpose(0, 2, 1, 3).reshape(3 * lanes * far, 128)

    from_l = ring(to_right, "level", -1)
    from_r = ring(to_left, "level", 1)
    from_l2 = ring(far_rows(l[:, l.shape[1] - far :]), "level", -2)
    from_r2 = ring(far_rows(l[:, :far]), "level", 2)

    x_shape = ((g.nx + 2) * g.NZ, g.WY)
    rm_shape, rl_shape = (g.nxm * g.NZm, g.WYm), (g.nxl * g.NZl, g.NYl)
    sent = (
        XH * g.NZ * (g.WY // 128) + MH * g.NZm * (g.WYm // 128) + rl_shape[0] * lanes,
        128,
    )
    sent2 = (lanes * far, 128)
    state = [x_shape, own, rm_shape, rl_shape, sent, sent, sent2, sent2]
    outs = call(
        first_kernel, [fine] * 3 + [own] * 2 + [mid] * 4 + [low] * 4 + state, scratch, 2,
        idx, tab, f, m, l, from_l, from_r, from_l2, from_r2,
    )
    coefs, outs = outs[:13], outs[13:]
    for cycle_no in range(1, CYCLES):
        x, gi, rm, rl, to_l, to_r, to_l2, to_r2 = outs
        received = (
            ring(to_r, "level", -1),
            ring(to_l, "level", 1),
            ring(to_r2, "level", -2),
            ring(to_l2, "level", 2),
        )
        if cycle_no < CYCLES - 1:
            shapes, more = state, []
        else:
            shapes, more = [(2 * g.nz * g.nx, g.PW)] * g.ns, [x_shape, own_blocks]
        outs = vmem_call(
            lambda *refs, n=len(shapes): cycle_kernel(g, n, *refs),
            shapes, scratch + more, 2,
            (idx, tab, gi, rm, rl, x, *received, *coefs),
        )
    packs = [ring(v, "slab", k) for k, v in enumerate(outs)]
    return tuple(call(unpack_kernel, [shape, shape], [], 1, idx, *packs))


def solution(mesh):
    spread = P("slab", "level", None)
    return jax.shard_map(
        shards,
        mesh=mesh,
        in_specs=(spread, spread, spread, P(), P(), P()),
        out_specs=(spread, spread),
        check_vma=False,
    )
```

```python
import math

import jax
import jax.numpy as jnp
from jax import lax
from jax.experimental import pallas as pl
from jax.experimental.pallas import tpu as pltpu
from jax.sharding import PartitionSpec as P

CYCLES = 3
MAXDEG = 6
INTERPRET = False

F32 = jnp.float32
OUT = 8
XH = 6
MH = 6
LH = 6
YH = 64


def dot(a, b):
    return jnp.dot(a, b, precision=lax.Precision.HIGHEST, preferred_element_type=F32)


def blocks(ref, rows):
    return jnp.concatenate([ref[b, rows, :] for b in range(ref.shape[0])], axis=1)


def put_blocks(ref, rows, value):
    for b in range(ref.shape[0]):
        ref[b, rows, :] = value[:, 128 * b : 128 * b + 128]


def iota(shape, dim):
    return lax.broadcasted_iota(jnp.int32, shape, dim)


def zy_sum(w, nz):
    rows, lanes = w.shape
    if nz % 8 == 0:
        v = w.reshape(rows // nz, nz // 8, 8, lanes)
        at = iota(v.shape, 2)
        edge = jnp.zeros_like(v[:, :1])
        up = pltpu.roll(w.reshape(rows // 8, 8, lanes), 1, 1).reshape(v.shape)
        down = pltpu.roll(w.reshape(rows // 8, 8, lanes), 7, 1).reshape(v.shape)
        up_over = down_over = edge
        if nz > 8:
            up_over = jnp.concatenate([edge, up[:, :-1]], axis=1)
            down_over = jnp.concatenate([down[:, 1:], edge], axis=1)
        s = v + jnp.where(at == 0, up_over, up) + jnp.where(at == 7, down_over, down)
        s = s.reshape(rows, lanes)
    else:
        at = iota(w.shape, 0) & (nz - 1)
        up = jnp.where(at == 0, 0.0, pltpu.roll(w, 1, 0))
        down = jnp.where(at == nz - 1, 0.0, pltpu.roll(w, rows - 1, 0))
        s = w + up + down
    at = iota((rows, 128), 1)
    n = lanes // 128
    part = [s[:, 128 * b : 128 * b + 128] for b in range(n)]
    left = [pltpu.roll(p, 1, 1) for p in part]
    right = [pltpu.roll(p, 127, 1) for p in part]
    out = []
    for b in range(n):
        before = left[b - 1] if b else 0.0
        after = right[b + 1] if b < n - 1 else 0.0
        out.append(
            part[b] + jnp.where(at == 0, before, left[b]) + jnp.where(at == 127, after, right[b])
        )
    return jnp.concatenate(out, axis=1)


class Geometry:
    def __init__(self, shape, ns, nl):
        self.nz, self.nx, self.NY = shape
        self.ns, self.nl = ns, nl
        self.NZ = self.nz * ns
        self.ny = self.NY // ns
        self.WY = min(self.NY, -(-(self.ny + 2 * YH) // 128) * 128)
        self.PW = -(-self.ny // 128) * 128
        self.nxm, self.nxl = self.nx // 2, self.nx // 4
        self.NZm, self.NZl = self.NZ // 2, self.NZ // 4
        self.WYm, self.NYm, self.NYl = self.WY // 2, self.NY // 2, self.NY // 4
        self.CH = max(1, min(4, 64 // self.NZ))
        self.PF = self.nx + 2 * OUT
        self.PM = self.nxm + 2 * MH
        self.PL = self.nxl + 2 * LH
        assert self.nx % self.CH == 0 and OUT % self.CH == 0 and XH <= self.nx
        assert self.nxl < LH <= 2 * self.nxl and MH <= self.nxm
        assert (self.nxl * self.nz // 4) % 4 == 0 and self.WYm % 128 == 0 and self.NYl % 128 == 0
        self.lowrows = self.nxl * (self.nz // 4)
        self.packrows = 3 * self.nz * self.nx + -(-3 * self.lowrows // 8) * 8

    def start(self, s):
        return jnp.clip(s * self.ny - (self.WY - self.ny) // 2, 0, self.NY - self.WY)


def vmem_call(kernel, outs, scratch, smem, args):
    specs = [pl.BlockSpec(memory_space=pltpu.SMEM)] * smem
    specs += [pl.BlockSpec(memory_space=pltpu.VMEM)] * (len(args) - smem)
    shapes = list(outs) + list(scratch) + [a.shape for a in args[smem:]]
    held = sum(4 * math.prod(o) for o in shapes)
    return pl.pallas_call(
        kernel,
        out_shape=[jax.ShapeDtypeStruct(o, F32) for o in outs],
        in_specs=specs,
        out_specs=[pl.BlockSpec(memory_space=pltpu.VMEM)] * len(outs),
        scratch_shapes=[pltpu.VMEM(o, F32) for o in scratch],
        compiler_params=pltpu.CompilerParams(vmem_limit_bytes=min(held * 3 // 2 + (4 << 20), 60 << 20)),
        interpret=INTERPRET,
    )(*args)


def repeat(g, n, body):
    if g.ns <= 4:
        for i in range(n):
            body(i)
    else:
        lax.fori_loop(0, n, lambda i, carry: (body(i), carry)[1], 0)


def pack_kernel(g, idx, near, *outs):
    s = idx[0]
    lane_pick = jnp.where(
        iota((g.NY, g.NYl), 0) // 4 == iota((g.NY, g.NYl), 1), 1.0, 0.0
    ).astype(F32)
    row_pick = jnp.where(
        iota((g.nxl, g.nx), 1) // 4 == iota((g.nxl, g.nx), 0), 1.0 / 64.0, 0.0
    ).astype(F32)
    base = 3 * g.nz * g.nx
    for k in range(g.ns):
        outs[k][base:, :] = jnp.zeros((g.packrows - base, g.WY), F32)
    turns = []
    for k in range(g.ns):
        partner = lax.rem(s - k + g.ns, g.ns)
        turns.append(lax.rem(g.NY - g.start(partner), g.NY))
    for a in range(3):
        arr = near.at[a]
        for k in range(g.ns):

            def row(z, a=a, k=k, arr=arr):
                at = (a * g.nz + z) * g.nx
                if not isinstance(at, int):
                    at = pl.multiple_of(at, 8)
                v = pltpu.roll(arr[z], turns[k], 1)[:, : g.WY]
                outs[k][pl.ds(at, g.nx), :] = v

            repeat(g, g.nz, row)
    for a in range(3):
        arr = near.at[a]
        for zl in range(g.nz // 4):
            col = arr[4 * zl] + arr[4 * zl + 1] + arr[4 * zl + 2] + arr[4 * zl + 3]
            low = dot(row_pick, dot(col, lane_pick))
            at = base + a * g.lowrows + zl * g.nxl
            for k in range(g.ns):
                outs[k][at : at + g.nxl, : g.NYl] = low


def fine_to_mid(src, row, planes, nz, scale):
    n = planes * nz // 2
    lanes = src.shape[0] * 128
    v = blocks(src, pl.ds(row, n, stride=2)) + blocks(src, pl.ds(row + 1, n, stride=2))
    v = v.reshape(planes // 2, 2, nz // 2, lanes)
    v = (v[:, 0] + v[:, 1]).reshape(planes // 2 * (nz // 2), lanes)
    half = (lanes, lanes // 2)
    pick = jnp.where(iota(half, 0) // 2 == iota(half, 1), scale / 8.0, 0.0).astype(F32)
    return dot(v, pick)


def assemble_kernel(g, idx, *refs):
    s = idx[0]
    recv = refs[: g.ns]
    f_out, m_out, l_out, to_left, to_right, fs = refs[g.ns :]
    base = 3 * g.nz * g.nx
    for j in range(g.ns):
        src = lax.rem(s + j, g.ns)
        for a in range(3):

            def row(z, a=a, j=j, src=src):
                at = (a * g.nz + z) * g.nx
                if not isinstance(at, int):
                    at = pl.multiple_of(at, 8)
                rows = pl.ds(src * g.nz + z, g.nx, stride=g.NZ)
                put_blocks(fs.at[a], rows, recv[j][pl.ds(at, g.nx), :])

            repeat(g, g.nz, row)
            for zl in range(g.nz // 4):
                at = base + a * g.lowrows + zl * g.nxl
                for x in range(g.nxl):
                    l_out[a, pl.ds(x * g.NZl + src * (g.nz // 4) + zl, 1), :] = recv[j][
                        at + x : at + x + 1, : g.NYl
                    ]
    nxz = g.nx * g.NZ
    for a in range(3):
        f_out[a] = blocks(fs.at[a], slice(0, nxz))
        m_out[a] = fine_to_mid(fs.at[a], 0, g.nx, g.NZ, 1.0)
    n = XH * g.NZ
    at = 0
    for a in range(3):
        for y in range(0, g.WY, 128):
            to_left[at : at + n, :] = f_out[a, 0:n, y : y + 128]
            to_right[at : at + n, :] = f_out[a, nxz - n :, y : y + 128]
            at += n
    n, total = MH * g.NZm, g.nxm * g.NZm
    for a in range(3):
        for y in range(0, g.WYm, 128):
            to_left[at : at + n, :] = m_out[a, 0:n, y : y + 128]
            to_right[at : at + n, :] = m_out[a, total - n :, y : y + 128]
            at += n
    n = g.nxl * g.NZl
    for a in range(3):
        for y in range(0, g.NYl, 128):
            to_left[at : at + n, :] = l_out[a, :, y : y + 128]
            to_right[at : at + n, :] = l_out[a, :, y : y + 128]
            at += n


def edge_rows(g):
    return (
        3 * XH * g.NZ * (g.WY // 128)
        + 3 * MH * g.NZm * (g.WYm // 128)
        + 3 * g.nxl * g.NZl * (g.NYl // 128)
    )


def coefficients(b, c, q):
    diag = c * c + q
    inv = 1.0 / diag
    scaled = (27.0 / 26.0 * (c * c) + q) * inv
    return diag, inv, scaled, c * inv / 26.0


def coarse_smooth(g, idx, tab, mid, low):
    for level, (gi, c, D, K, y, d, t) in ((1, mid), (2, low)):
        y[...] = gi[...] * tab[level, 0]
        d[...] = y[...]

    def turn(j, carry):
        for level, nz, (gi, c, D, K, y, d, t) in ((1, g.NZm, mid), (2, g.NZl, low)):
            rows = c.shape[0]
            t[nz : nz + rows, :] = zy_sum(c[...] * y[...], nz)
        for level, nz, (gi, c, D, K, y, d, t) in ((1, g.NZm, mid), (2, g.NZl, low)):
            rows = c.shape[0]
            box = t[0:rows, :] + t[nz : nz + rows, :] + t[2 * nz : 2 * nz + rows, :]
            e = gi[...] - D[...] * y[...] + K[...] * box
            nd = tab[level, j] * d[...] + tab[level, MAXDEG + j] * e
            d[...] = nd
            y[...] = y[...] + nd
        return carry

    lax.fori_loop(1, jnp.maximum(idx[3], idx[4]), turn, 0)


def fine_sweeps(g, idx, tab, gi, c, D, K, y, d):
    nz = g.NZ

    def rows(p):
        return slice((OUT + p) * nz, (OUT + p + 1) * nz)

    for p in range(-XH, g.nx + XH):
        r = rows(p)
        y[r, :] = gi[r, :] * tab[0, 0]
        d[r, :] = y[r, :]
    for j in range(1, MAXDEG):
        reach = MAXDEG - j

        @pl.when(j < idx[2])
        def _(j=j, reach=reach):
            alpha, beta = tab[0, j], tab[0, MAXDEG + j]
            first, last = -reach - 1, g.nx + reach
            held, sums = {}, {}
            for p in range(first, last + 1):
                held[p] = y[rows(p), :]
                sums[p] = zy_sum(c[rows(p), :] * held[p], nz)
                q = p - 1
                if q <= first:
                    continue
                r = rows(q)
                box = sums[q - 1] + sums[q] + sums[p]
                e = gi[r, :] - D[r, :] * held[q] + K[r, :] * box
                nd = alpha * d[r, :] + beta * e
                d[r, :] = nd
                y[r, :] = held[q] + nd


def fine_smooth(g, idx, tab, gi, c, D, K, y, d, t):
    if g.NZ <= 16:
        fine_sweeps(g, idx, tab, gi, c, D, K, y, d)
        return
    n = g.CH * g.NZ
    side, own = OUT // g.CH, g.nx // g.CH
    y[...] = gi[...] * tab[0, 0]
    d[...] = y[...]

    def turn(j, carry):
        radius = idx[2] - j
        ht = (radius + 1 + g.CH - 1) // g.CH
        h = (radius + g.CH - 1) // g.CH
        fine_boxes(g, side - ht, side + own + ht, c, y, t)

        def chunk(k, inner_carry):
            r = pl.ds(pl.multiple_of(k * n, n), n)
            old = y[r, :]
            e = gi[r, :] - D[r, :] * old + K[r, :] * box_at(g, t, k)
            nd = tab[0, j] * d[r, :] + tab[0, MAXDEG + j] * e
            d[r, :] = nd
            y[r, :] = old + nd
            return inner_carry

        lax.fori_loop(side - h, side + own + h, chunk, 0)
        return carry

    lax.fori_loop(1, idx[2], turn, 0)


def clear_box_edges(g, t, tm, tl):
    for ref, nz in ((t, g.NZ), (tm, g.NZm), (tl, g.NZl)):
        zeros = jnp.zeros((nz, ref.shape[1]), F32)
        ref[0:nz, :] = zeros
        ref[ref.shape[0] - nz :, :] = zeros


def fine_boxes(g, first, last, c, x, t):
    n = g.CH * g.NZ

    def turn(k, carry):
        r = pl.ds(pl.multiple_of(k * n, n), n)
        t[pl.ds(pl.multiple_of(g.NZ + k * n, g.NZ), n), :] = zy_sum(c[r, :] * x[r, :], g.NZ)
        return carry

    lax.fori_loop(first, last, turn, 0)


def box_at(g, t, k):
    n = g.CH * g.NZ
    parts = [t[pl.ds(pl.multiple_of(k * n + o * g.NZ, g.NZ), n), :] for o in range(3)]
    return parts[0] + parts[1] + parts[2]


def coarse_correction(g, s, ym, yl, zd):
    planes = g.nxm + 2
    rows = planes * g.NZm
    shape = (rows, g.PL * g.NZl)
    row, col = iota(shape, 0), iota(shape, 1)
    plane = row // g.NZm + (2 * LH - 1)
    want = (plane // 2) * g.NZl + (row % g.NZm) // 2
    up_rows = jnp.where(col == want, 1.0, 0.0).astype(F32)
    shape = (g.NYl, g.WYm)
    off = g.start(s) // 4
    up_lanes = jnp.where(
        iota(shape, 0) == off + iota(shape, 1) // 2, 1.0, 0.0
    ).astype(F32)
    low = dot(dot(up_rows, yl[...]), up_lanes)
    at = (MH - 1) * g.NZm
    both = ym[at : at + rows, :] + low
    shape = (g.WYm, g.WY)
    wide = jnp.where(iota(shape, 0) == iota(shape, 1) // 2, 1.0, 0.0).astype(F32)
    v = dot(both, wide)
    put_blocks(zd, pl.ds(0, rows, stride=2), v)
    put_blocks(zd, pl.ds(1, rows, stride=2), v)


def doubled(g, zd, plane, planes):
    at = (plane + 2) // 2 * g.NZ
    if planes == 1:
        return blocks(zd, slice(at, at + g.NZ))
    v = blocks(zd, slice(at, at + planes // 2 * g.NZ)).reshape(planes // 2, 1, g.NZ, g.WY)
    v = jnp.broadcast_to(v, (planes // 2, 2, g.NZ, g.WY))
    return v.reshape(planes * g.NZ, g.WY)


def pieces(g):
    return [(-1, 1)] + [(p, g.CH) for p in range(0, g.nx, g.CH)] + [(g.nx, 1)]


def cycle(g, idx, tab, fine, mid, low, x_old, x, bi, diag, zd, keep, xb=None):
    gi, c, D, K, y, d, t = fine
    fine_smooth(g, idx, tab, *fine)
    coarse_smooth(g, idx, tab, mid, low)
    coarse_correction(g, idx[0], mid[4], low[4], zd)
    for p, planes in pieces(g):
        n = planes * g.NZ
        rr = slice((OUT + p) * g.NZ, (OUT + p) * g.NZ + n)
        r = slice((1 + p) * g.NZ, (1 + p) * g.NZ + n)
        v = 0.5 * (y[rr, :] + doubled(g, zd, p, planes))
        if x_old is not None:
            v = x_old[r, :] + v
        x[r, :] = v
        if xb is not None and planes == g.CH and 0 <= p < g.nx:
            put_blocks(xb, slice(p * g.NZ, p * g.NZ + n), v)
        t[r, :] = zy_sum(c[rr, :] * v, g.NZ)
    step = g.CH * g.NZ
    for p in range(0, g.nx, g.CH):
        at = p * g.NZ
        box = (
            t[at : at + step, :]
            + t[at + g.NZ : at + g.NZ + step, :]
            + t[at + 2 * g.NZ : at + 2 * g.NZ + step, :]
        )
        r = slice(at, at + step)
        rr = slice(OUT * g.NZ + at, OUT * g.NZ + at + step)
        v = bi[r, :] - D[rr, :] * x[at + g.NZ : at + g.NZ + step, :] + K[rr, :] * box
        keep(r, v, v * diag[r, :])


def send_defect(g, s, gi, rm, rl, res, to_l, to_r, to_l2, to_r2):
    rm[...] = fine_to_mid(res, 0, g.nx, g.NZ, 4.0)
    shape = (g.nxl * g.NZl, g.nxm * g.NZm)
    row, col = iota(shape, 0), iota(shape, 1)
    same_x = col // (2 * g.NZm) == row // g.NZl
    same_z = (col % g.NZm) // 2 == row % g.NZl
    rows = jnp.where(same_x & same_z, 0.5, 0.0).astype(F32)
    shape = (g.WYm, g.NYl)
    off = g.start(s) // 4
    lanes = jnp.where(iota(shape, 0) // 2 + off == iota(shape, 1), 1.0, 0.0).astype(F32)
    rl[...] = dot(dot(rows, rm[...]), lanes)
    at = 0
    for ref, n in ((gi, XH * g.NZ), (rm, MH * g.NZm), (rl, g.nxl * g.NZl)):
        total = ref.shape[0]
        for y in range(0, ref.shape[1], 128):
            to_l[at : at + n, :] = ref[0:n, y : y + 128]
            to_r[at : at + n, :] = ref[total - n :, y : y + 128]
            at += n
    far = (LH - g.nxl) * g.NZl
    total = rl.shape[0]
    for b in range(g.NYl // 128):
        lanes = slice(128 * b, 128 * b + 128)
        to_l2[b * far : b * far + far, :] = rl[0:far, lanes]
        to_r2[b * far : b * far + far, :] = rl[total - far :, lanes]


def first_kernel(g, idx, tab, f, m, l, from_l, from_r, from_l2, from_r2, *refs):
    (c, D, K, bi, diag, cm, Dm, Km, im, cl, Dl, Kl, il) = refs[:13]
    x, gi_own, rm, rl, to_l, to_r, to_l2, to_r2 = refs[13:21]
    (gi, y, d, t, gm, ym, dm, tm, gl, yl, dl, tl, zd, res) = refs[21:]
    s, li = idx[0], idx[1]
    clear_box_edges(g, t, tm, tl)
    fill = (0.0, 0.0, 1.0)

    def kept(ok, v, a):
        return jnp.where(ok, v, fill[a])

    n, own = XH * g.NZ, g.nx * g.NZ
    lo, hi = OUT * g.NZ, (OUT + g.nx) * g.NZ
    at = 0
    region = (gi, c, y)
    for a in range(3):
        region[a][0 : lo - n, :] = jnp.full((lo - n, g.WY), fill[a], F32)
        region[a][hi + n :, :] = jnp.full((lo - n, g.WY), fill[a], F32)
        region[a][lo:hi, :] = f[a]
        for yy in range(0, g.WY, 128):
            region[a][lo - n : lo, yy : yy + 128] = kept(li > 0, from_l[at : at + n, :], a)
            region[a][hi : hi + n, yy : yy + 128] = kept(
                li < g.nl - 1, from_r[at : at + n, :], a
            )
            at += n
    step = g.CH * g.NZ
    side = OUT // g.CH

    def build(k, carry):
        r = pl.ds(pl.multiple_of(k * step, step), step)
        b0 = gi[r, :]
        dg, inv, sc, kk = coefficients(b0, c[r, :], y[r, :])
        gi[r, :] = b0 * inv
        D[r, :] = sc
        K[r, :] = kk
        y[r, :] = dg
        return carry

    lax.fori_loop(0, g.PF // g.CH, build, 0)
    bi[...] = gi[lo:hi, :]
    diag[...] = y[lo:hi, :]

    n = MH * g.NZm
    parts = []
    for a in range(3):
        halves = []
        for yy in range(0, g.WYm, 128):
            halves.append(
                (
                    kept(li > 0, from_l[at : at + n, :], a),
                    kept(li < g.nl - 1, from_r[at : at + n, :], a),
                )
            )
            at += n
        left = jnp.concatenate([v[0] for v in halves], axis=1)
        right = jnp.concatenate([v[1] for v in halves], axis=1)
        parts.append(jnp.concatenate([left, m[a], right], axis=0))
    _, inv, sc, kk = coefficients(*parts)
    cm[...] = parts[1]
    Dm[...] = sc
    Km[...] = kk
    im[...] = inv
    gm[...] = 4.0 * parts[0] * inv

    n = g.nxl * g.NZl
    far = (LH - g.nxl) * g.NZl
    store = (gl, cl, il)
    at2 = 0
    for a in range(3):
        for yy in range(0, g.NYl, 128):
            lanes = slice(yy, yy + 128)
            ref = store[a]
            ref[0:far, lanes] = kept(li > 1, from_l2[at2 : at2 + far, :], a)
            ref[far : far + n, lanes] = kept(li > 0, from_l[at : at + n, :], a)
            ref[far + n : far + 2 * n, lanes] = l[a, :, lanes]
            ref[far + 2 * n : far + 3 * n, lanes] = kept(
                li < g.nl - 1, from_r[at : at + n, :], a
            )
            ref[far + 3 * n :, lanes] = kept(li < g.nl - 2, from_r2[at2 : at2 + far, :], a)
            at += n
            at2 += far
    _, inv, sc, kk = coefficients(gl[...], cl[...], il[...])
    Dl[...] = sc
    Kl[...] = kk
    il[...] = inv
    gl[...] = 16.0 * gl[...] * inv

    def keep(r, scaled, plain):
        gi_own[r, :] = scaled
        put_blocks(res, r, plain)

    fine = (gi, c, D, K, y, d, t)
    mid = (gm, cm, Dm, Km, ym, dm, tm)
    low = (gl, cl, Dl, Kl, yl, dl, tl)
    cycle(g, idx, tab, fine, mid, low, None, x, bi, diag, zd, keep)
    send_defect(g, s, gi_own, rm, rl, res, to_l, to_r, to_l2, to_r2)


def gather_defect(g, gi_own, rm, rl, from_l, from_r, from_l2, from_r2, gi, gm, im, gl, il):
    lo, hi = OUT * g.NZ, (OUT + g.nx) * g.NZ
    n = XH * g.NZ
    zeros = jnp.zeros((lo - n, g.WY), F32)
    gi[0 : lo - n, :] = zeros
    gi[hi + n :, :] = zeros
    gi[lo:hi, :] = gi_own[...]
    at = 0
    for y in range(0, g.WY, 128):
        gi[lo - n : lo, y : y + 128] = from_l[at : at + n, :]
        gi[hi : hi + n, y : y + 128] = from_r[at : at + n, :]
        at += n
    n, own = MH * g.NZm, rm.shape[0]
    for y in range(0, g.WYm, 128):
        lanes = slice(y, y + 128)
        gm[0:n, lanes] = from_l[at : at + n, :] * im[0:n, lanes]
        gm[n + own :, lanes] = from_r[at : at + n, :] * im[n + own :, lanes]
        at += n
    gm[n : n + own, :] = rm[...] * im[n : n + own, :]
    n = g.nxl * g.NZl
    far = (LH - g.nxl) * g.NZl
    for b in range(g.NYl // 128):
        lanes = slice(128 * b, 128 * b + 128)
        rows = slice(b * far, b * far + far)
        gl[0:far, lanes] = from_l2[rows, :]
        gl[far : far + n, lanes] = from_l[at : at + n, :]
        gl[far + n : far + 2 * n, lanes] = rl[:, lanes]
        gl[far + 2 * n : far + 3 * n, lanes] = from_r[at : at + n, :]
        gl[far + 3 * n :, lanes] = from_r2[rows, :]
        at += n
    gl[...] = gl[...] * il[...]


def cycle_kernel(g, n_outs, idx, tab, *refs):
    gi_own, rm, rl, x_old = refs[:4]
    received = refs[4:8]
    (c, D, K, bi, diag, cm, Dm, Km, im, cl, Dl, Kl, il) = refs[8:21]
    outs = refs[21 : 21 + n_outs]
    scr = refs[21 + n_outs :]
    (gi, y, d, t, gm, ym, dm, tm, gl, yl, dl, tl, zd, res) = scr[:14]
    clear_box_edges(g, t, tm, tl)
    gather_defect(g, gi_own, rm, rl, *received, gi, gm, im, gl, il)
    fine = (gi, c, D, K, y, d, t)
    mid = (gm, cm, Dm, Km, ym, dm, tm)
    low = (gl, cl, Dl, Kl, yl, dl, tl)
    s = idx[0]
    if len(scr) == 14:
        x, gi_new, rm_new, rl_new = outs[:4]

        def keep(r, scaled, plain):
            gi_new[r, :] = scaled
            put_blocks(res, r, plain)

        cycle(g, idx, tab, fine, mid, low, x_old, x, bi, diag, zd, keep)
        send_defect(g, s, gi_new, rm_new, rl_new, res, *outs[4:])
        return
    x, xb = scr[14:]

    def keep_plain(r, scaled, plain):
        put_blocks(res, r, plain)

    cycle(g, idx, tab, fine, mid, low, x_old, x, bi, diag, zd, keep_plain, xb)
    shift = lax.rem(g.WY - (s * g.ny - g.start(s)), g.WY)
    for k in range(g.ns):
        partner = lax.rem(s - k + g.ns, g.ns)
        for o, ref in enumerate((xb, res)):

            def row(z, o=o, ref=ref, k=k, partner=partner):
                v = blocks(ref, pl.ds(partner * g.nz + z, g.nx, stride=g.NZ))
                at = (o * g.nz + z) * g.nx
                if not isinstance(at, int):
                    at = pl.multiple_of(at, 8)
                outs[k][pl.ds(at, g.nx), :] = pltpu.roll(v, shift, 1)[:, : g.PW]

            repeat(g, g.nz, row)


def unpack_kernel(g, idx, *refs):
    s = idx[0]
    recv, outs = refs[: g.ns], refs[g.ns :]
    for o in range(2):
        for z in range(g.nz):
            at = (o * g.nz + z) * g.nx
            total = None
            if g.ny % 128 == 0:
                wide = jnp.concatenate(
                    [recv[j][at : at + g.nx, : g.ny] for j in range(g.ns)], axis=1
                )
                total = pltpu.roll(wide, s * g.ny, 1)
            else:
                mine = iota((g.nx, g.NY), 1) < g.ny
                for j in range(g.ns):
                    src = lax.rem(s + j, g.ns)
                    v = recv[j][at : at + g.nx, :]
                    pad = jnp.zeros((g.nx, g.NY - g.PW), F32)
                    v = jnp.where(mine, jnp.concatenate([v, pad], axis=1), 0.0)
                    v = pltpu.roll(v, src * g.ny, 1)
                    total = v if total is None else total + v
            outs[o][z] = total


def ring(value, axis, by):
    peers = lax.axis_size(axis)
    if by % peers == 0:
        return value
    return lax.ppermute(value, axis, [(i, (i - by) % peers) for i in range(peers)])


def sweep_tables(degrees, lower, upper):
    centre = (upper + lower) * 0.5
    radius = (upper - lower) * 0.5
    ratio = centre / radius
    rho = 1.0 / ratio
    alphas, betas = [], []
    for j in range(1, MAXDEG):
        new = 1.0 / (2.0 * ratio - rho)
        active = j < degrees
        alphas.append(jnp.where(active, new * rho, 0.0))
        betas.append(jnp.where(active, 2.0 * new / radius, 0.0))
        rho = new
    zero = jnp.zeros_like(rho)
    return jnp.stack([1.0 / centre] + alphas + [zero] + betas, axis=1)


def shards(right_side, scale_field, mass_field, degrees, lower_bound, upper_bound):
    g = Geometry(right_side.shape, lax.axis_size("slab"), lax.axis_size("level"))
    place = jnp.stack([lax.axis_index("slab"), lax.axis_index("level")])
    place = place.astype(jnp.int32)
    idx = jnp.concatenate([place, degrees])
    tab = sweep_tables(degrees, lower_bound, upper_bound)

    def call(kernel, outs, scratch, smem, *args):
        return vmem_call(lambda *refs: kernel(g, *refs), outs, scratch, smem, args)

    shape = right_side.shape
    packs = call(
        pack_kernel, [(g.packrows, g.WY)] * g.ns, [], 1,
        place, jnp.stack([right_side, scale_field, mass_field]),
    )
    packs = [ring(v, "slab", k) for k, v in enumerate(packs)]

    fine = (g.PF * g.NZ, g.WY)
    own = (g.nx * g.NZ, g.WY)
    mid = (g.PM * g.NZm, g.WYm)
    low = (g.PL * g.NZl, g.NYl)
    own_blocks = (g.WY // 128, own[0], 128)
    scratch = [
        fine, fine, fine, (fine[0] + 2 * g.NZ, g.WY),
        mid, mid, mid, (mid[0] + 2 * g.NZm, g.WYm),
        low, low, low, (low[0] + 2 * g.NZl, g.NYl),
        (g.WY // 128, (g.nxm + 2) * g.NZ, 128), own_blocks,
    ]

    f, m, l, to_left, to_right = call(
        assemble_kernel,
        [
            (3, *own), (3, g.nxm * g.NZm, g.WYm), (3, g.nxl * g.NZl, g.NYl),
            (edge_rows(g), 128), (edge_rows(g), 128),
        ],
        [(3, *own_blocks)], 1, place, *packs,
    )
    far = (LH - g.nxl) * g.NZl
    lanes = g.NYl // 128

    def far_rows(part):
        parts = part.reshape(3, part.shape[1], lanes, 128)
        return parts.transpose(0, 2, 1, 3).reshape(3 * lanes * far, 128)

    from_l = ring(to_right, "level", -1)
    from_r = ring(to_left, "level", 1)
    from_l2 = ring(far_rows(l[:, l.shape[1] - far :]), "level", -2)
    from_r2 = ring(far_rows(l[:, :far]), "level", 2)

    x_shape = ((g.nx + 2) * g.NZ, g.WY)
    rm_shape, rl_shape = (g.nxm * g.NZm, g.WYm), (g.nxl * g.NZl, g.NYl)
    sent = (
        XH * g.NZ * (g.WY // 128) + MH * g.NZm * (g.WYm // 128) + rl_shape[0] * lanes,
        128,
    )
    sent2 = (lanes * far, 128)
    state = [x_shape, own, rm_shape, rl_shape, sent, sent, sent2, sent2]
    outs = call(
        first_kernel, [fine] * 3 + [own] * 2 + [mid] * 4 + [low] * 4 + state, scratch, 2,
        idx, tab, f, m, l, from_l, from_r, from_l2, from_r2,
    )
    coefs, outs = outs[:13], outs[13:]
    for cycle_no in range(1, CYCLES):
        x, gi, rm, rl, to_l, to_r, to_l2, to_r2 = outs
        received = (
            ring(to_r, "level", -1),
            ring(to_l, "level", 1),
            ring(to_r2, "level", -2),
            ring(to_l2, "level", 2),
        )
        if cycle_no < CYCLES - 1:
            shapes, more = state, []
        else:
            shapes, more = [(2 * g.nz * g.nx, g.PW)] * g.ns, [x_shape, own_blocks]
        outs = vmem_call(
            lambda *refs, n=len(shapes): cycle_kernel(g, n, *refs),
            shapes, scratch + more, 2,
            (idx, tab, gi, rm, rl, x, *received, *coefs),
        )
    packs = [ring(v, "slab", k) for k, v in enumerate(outs)]
    return tuple(call(unpack_kernel, [shape, shape], [], 1, place, *packs))


def solution(mesh):
    spread = P("slab", "level", None)
    return jax.shard_map(
        shards,
        mesh=mesh,
        in_specs=(spread, spread, spread, P(), P(), P()),
        out_specs=(spread, spread),
        check_vma=False,
    )
```

```python
import math

import jax
import jax.numpy as jnp
from jax import lax
from jax.experimental import pallas as pl
from jax.experimental.pallas import tpu as pltpu
from jax.sharding import PartitionSpec as P


CYCLES = 3
MAXDEG = 6
INTERPRET = False

F32 = jnp.float32
OUT = 8
XH = 6
MH = 6
LH = 6
YH = 64


def dot(a, b):
    return jnp.dot(a, b, precision=lax.Precision.HIGHEST, preferred_element_type=F32)


def blocks(ref, rows):
    return jnp.concatenate([ref[b, rows, :] for b in range(ref.shape[0])], axis=1)


def put_blocks(ref, rows, value):
    for b in range(ref.shape[0]):
        ref[b, rows, :] = value[:, 128 * b : 128 * b + 128]


def iota(shape, dim):
    return lax.broadcasted_iota(jnp.int32, shape, dim)


def zy_sum(w, nz):
    rows, lanes = w.shape
    if nz % 8 == 0:
        v = w.reshape(rows // nz, nz // 8, 8, lanes)
        at = iota(v.shape, 2)
        edge = jnp.zeros_like(v[:, :1])
        up = pltpu.roll(w.reshape(rows // 8, 8, lanes), 1, 1).reshape(v.shape)
        down = pltpu.roll(w.reshape(rows // 8, 8, lanes), 7, 1).reshape(v.shape)
        up_over = down_over = edge
        if nz > 8:
            up_over = jnp.concatenate([edge, up[:, :-1]], axis=1)
            down_over = jnp.concatenate([down[:, 1:], edge], axis=1)
        s = v + jnp.where(at == 0, up_over, up) + jnp.where(at == 7, down_over, down)
        s = s.reshape(rows, lanes)
    else:
        at = iota(w.shape, 0) & (nz - 1)
        up = jnp.where(at == 0, 0.0, pltpu.roll(w, 1, 0))
        down = jnp.where(at == nz - 1, 0.0, pltpu.roll(w, rows - 1, 0))
        s = w + up + down
    at = iota((rows, 128), 1)
    n = lanes // 128
    part = [s[:, 128 * b : 128 * b + 128] for b in range(n)]
    left = [pltpu.roll(p, 1, 1) for p in part]
    right = [pltpu.roll(p, 127, 1) for p in part]
    out = []
    for b in range(n):
        before = left[b - 1] if b else 0.0
        after = right[b + 1] if b < n - 1 else 0.0
        out.append(
            part[b] + jnp.where(at == 0, before, left[b]) + jnp.where(at == 127, after, right[b])
        )
    return jnp.concatenate(out, axis=1)


class Geometry:
    def __init__(self, shape, ns, nl):
        self.nz, self.nx, self.NY = shape
        self.ns, self.nl = ns, nl
        self.NZ = self.nz * ns
        self.ny = self.NY // ns
        self.WY = min(self.NY, -(-(self.ny + 2 * YH) // 128) * 128)
        self.PW = -(-self.ny // 128) * 128
        self.nxm, self.nxl = self.nx // 2, self.nx // 4
        self.NZm, self.NZl = self.NZ // 2, self.NZ // 4
        self.WYm, self.NYm, self.NYl = self.WY // 2, self.NY // 2, self.NY // 4
        self.CH = max(1, min(4, 64 // self.NZ))
        self.PF = self.nx + 2 * OUT
        self.PM = self.nxm + 2 * MH
        self.PL = self.nxl + 2 * LH
        assert self.nx % self.CH == 0 and OUT % self.CH == 0 and XH <= self.nx
        assert self.nxl < LH <= 2 * self.nxl and MH <= self.nxm
        assert (self.nxl * self.nz // 4) % 4 == 0 and self.WYm % 128 == 0 and self.NYl % 128 == 0
        self.lowrows = self.nxl * (self.nz // 4)
        self.rows_1st = self.nz * self.nx + -(-3 * self.lowrows // 8) * 8
        self.rows_2nd = 2 * self.nz * self.nx

    def start(self, s):
        return jnp.clip(s * self.ny - (self.WY - self.ny) // 2, 0, self.NY - self.WY)


def vmem_call(kernel, outs, scratch, smem, args):
    specs = [pl.BlockSpec(memory_space=pltpu.SMEM)] * smem
    specs += [pl.BlockSpec(memory_space=pltpu.VMEM)] * (len(args) - smem)
    shapes = list(outs) + list(scratch) + [a.shape for a in args[smem:]]
    held = sum(4 * math.prod(o) for o in shapes)
    return pl.pallas_call(
        kernel,
        out_shape=[jax.ShapeDtypeStruct(o, F32) for o in outs],
        in_specs=specs,
        out_specs=[pl.BlockSpec(memory_space=pltpu.VMEM)] * len(outs),
        scratch_shapes=[pltpu.VMEM(o, F32) for o in scratch],
        compiler_params=pltpu.CompilerParams(vmem_limit_bytes=min(held * 3 // 2 + (4 << 20), 60 << 20)),
        interpret=INTERPRET,
    )(*args)


def repeat(g, n, body):
    if g.ns <= 4:
        for i in range(n):
            body(i)
    else:
        lax.fori_loop(0, n, lambda i, carry: (body(i), carry)[1], 0)


def pack_kernel(g, idx, near, *outs):
    s = idx[0]
    lane_pick = jnp.where(
        iota((g.NY, g.NYl), 0) // 4 == iota((g.NY, g.NYl), 1), 1.0, 0.0
    ).astype(F32)
    row_pick = jnp.where(
        iota((g.nxl, g.nx), 1) // 4 == iota((g.nxl, g.nx), 0), 1.0 / 64.0, 0.0
    ).astype(F32)
    base = g.nz * g.nx
    first, second = outs[: g.ns], outs[g.ns :]
    turns = []
    for k in range(g.ns):
        first[k][base:, :] = jnp.zeros((g.rows_1st - base, g.WY), F32)
        partner = lax.rem(s - k + g.ns, g.ns)
        turns.append(lax.rem(g.NY - g.start(partner), g.NY))
    for a, (group, at_a) in enumerate(((first, 0), (second, 0), (second, 1))):
        arr = near.at[a]
        for k in range(g.ns):

            def row(z, at_a=at_a, k=k, arr=arr, group=group):
                at = (at_a * g.nz + z) * g.nx
                if not isinstance(at, int):
                    at = pl.multiple_of(at, 8)
                v = pltpu.roll(arr[z], turns[k], 1)[:, : g.WY]
                group[k][pl.ds(at, g.nx), :] = v

            repeat(g, g.nz, row)
        for zl in range(g.nz // 4):
            col = arr[4 * zl] + arr[4 * zl + 1] + arr[4 * zl + 2] + arr[4 * zl + 3]
            low = dot(row_pick, dot(col, lane_pick))
            at = base + a * g.lowrows + zl * g.nxl
            for k in range(g.ns):
                first[k][at : at + g.nxl, : g.NYl] = low


def fine_to_mid(src, row, planes, nz, scale):
    n = planes * nz // 2
    lanes = src.shape[0] * 128
    v = blocks(src, pl.ds(row, n, stride=2)) + blocks(src, pl.ds(row + 1, n, stride=2))
    v = v.reshape(planes // 2, 2, nz // 2, lanes)
    v = (v[:, 0] + v[:, 1]).reshape(planes // 2 * (nz // 2), lanes)
    half = (lanes, lanes // 2)
    pick = jnp.where(iota(half, 0) // 2 == iota(half, 1), scale / 8.0, 0.0).astype(F32)
    return dot(v, pick)


def assemble_kernel(g, count, idx, *refs):
    s = idx[0]
    recv, refs = refs[: g.ns], refs[g.ns :]
    f_out, m_out, to_left, to_right = refs[:4]
    l_out, fs = refs[4] if count == 1 else None, refs[-1]
    base = count * g.nz * g.nx
    for j in range(g.ns):
        src = lax.rem(s + j, g.ns)
        for a in range(count):

            def row(z, a=a, j=j, src=src):
                at = (a * g.nz + z) * g.nx
                if not isinstance(at, int):
                    at = pl.multiple_of(at, 8)
                rows = pl.ds(src * g.nz + z, g.nx, stride=g.NZ)
                put_blocks(fs.at[a], rows, recv[j][pl.ds(at, g.nx), :])

            repeat(g, g.nz, row)
        for i in range(3 if count == 1 else 0):
            for zl in range(g.nz // 4):
                at = base + i * g.lowrows + zl * g.nxl
                for x in range(g.nxl):
                    l_out[i, pl.ds(x * g.NZl + src * (g.nz // 4) + zl, 1), :] = recv[j][
                        at + x : at + x + 1, : g.NYl
                    ]
    nxz = g.nx * g.NZ
    at, n = 0, XH * g.NZ
    for a in range(count):
        f_out[a] = blocks(fs.at[a], slice(0, nxz))
        m_out[a] = fine_to_mid(fs.at[a], 0, g.nx, g.NZ, 1.0)
        for b in range(g.WY // 128):
            to_left[at : at + n, :] = fs[a, b, 0:n, :]
            to_right[at : at + n, :] = fs[a, b, nxz - n :, :]
            at += n
    n, total = MH * g.NZm, g.nxm * g.NZm
    for a in range(count):
        for y in range(0, g.WYm, 128):
            to_left[at : at + n, :] = m_out[a, 0:n, y : y + 128]
            to_right[at : at + n, :] = m_out[a, total - n :, y : y + 128]
            at += n
    n = g.nxl * g.NZl
    for i in range(3 if count == 1 else 0):
        for y in range(0, g.NYl, 128):
            to_left[at : at + n, :] = l_out[i, :, y : y + 128]
            to_right[at : at + n, :] = l_out[i, :, y : y + 128]
            at += n


def edge_rows(g, count):
    rows = count * XH * g.NZ * (g.WY // 128) + count * MH * g.NZm * (g.WYm // 128)
    return rows + (3 * g.nxl * g.NZl * (g.NYl // 128) if count == 1 else 0)


def coefficients(b, c, q):
    diag = c * c + q
    inv = 1.0 / diag
    scaled = (27.0 / 26.0 * (c * c) + q) * inv
    return diag, inv, scaled, c * inv / 26.0


def coarse_smooth(g, idx, tab, mid, low):
    for level, (gi, c, D, K, y, d, t) in ((1, mid), (2, low)):
        y[...] = gi[...] * tab[level, 0]
        d[...] = y[...]

    def turn(j, carry):
        for nz, (gi, c, D, K, y, d, t) in ((g.NZm, mid), (g.NZl, low)):
            rows = c.shape[0]
            t[nz : nz + rows, :] = zy_sum(c[...] * y[...], nz)
        for level, nz, (gi, c, D, K, y, d, t) in ((1, g.NZm, mid), (2, g.NZl, low)):
            rows = c.shape[0]
            box = t[0:rows, :] + t[nz : nz + rows, :] + t[2 * nz : 2 * nz + rows, :]
            e = gi[...] - D[...] * y[...] + K[...] * box
            nd = tab[level, j] * d[...] + tab[level, MAXDEG + j] * e
            d[...] = nd
            y[...] = y[...] + nd
        return carry

    lax.fori_loop(1, jnp.maximum(idx[3], idx[4]), turn, 0)


def fine_sweeps(g, idx, tab, gi, c, D, K, y, d):
    nz = g.NZ

    def rows(p):
        return slice((OUT + p) * nz, (OUT + p + 1) * nz)

    for p in range(-XH, g.nx + XH):
        r = rows(p)
        y[r, :] = gi[r, :] * tab[0, 0]
        d[r, :] = y[r, :]
    for j in range(1, MAXDEG):
        reach = MAXDEG - j

        @pl.when(j < idx[2])
        def _(j=j, reach=reach):
            alpha, beta = tab[0, j], tab[0, MAXDEG + j]
            first, last = -reach - 1, g.nx + reach
            held, sums = {}, {}
            for p in range(first, last + 1):
                held[p] = y[rows(p), :]
                sums[p] = zy_sum(c[rows(p), :] * held[p], nz)
                q = p - 1
                if q <= first:
                    continue
                r = rows(q)
                box = sums[q - 1] + sums[q] + sums[p]
                e = gi[r, :] - D[r, :] * held[q] + K[r, :] * box
                nd = alpha * d[r, :] + beta * e
                d[r, :] = nd
                y[r, :] = held[q] + nd


def fine_smooth(g, idx, tab, gi, c, D, K, y, d, t):
    if g.NZ <= 16:
        fine_sweeps(g, idx, tab, gi, c, D, K, y, d)
        return
    n = g.CH * g.NZ
    side, own = OUT // g.CH, g.nx // g.CH
    y[...] = gi[...] * tab[0, 0]
    d[...] = y[...]

    def turn(j, carry):
        radius = idx[2] - j
        ht = (radius + 1 + g.CH - 1) // g.CH
        h = (radius + g.CH - 1) // g.CH
        fine_boxes(g, side - ht, side + own + ht, c, y, t)

        def chunk(k, inner_carry):
            r = pl.ds(pl.multiple_of(k * n, n), n)
            old = y[r, :]
            e = gi[r, :] - D[r, :] * old + K[r, :] * box_at(g, t, k)
            nd = tab[0, j] * d[r, :] + tab[0, MAXDEG + j] * e
            d[r, :] = nd
            y[r, :] = old + nd
            return inner_carry

        lax.fori_loop(side - h, side + own + h, chunk, 0)
        return carry

    lax.fori_loop(1, idx[2], turn, 0)


def clear_box_edges(g, t, tm, tl):
    for ref, nz in ((t, g.NZ), (tm, g.NZm), (tl, g.NZl)):
        zeros = jnp.zeros((nz, ref.shape[1]), F32)
        ref[0:nz, :] = zeros
        ref[ref.shape[0] - nz :, :] = zeros


def fine_boxes(g, first, last, c, x, t):
    n = g.CH * g.NZ

    def turn(k, carry):
        r = pl.ds(pl.multiple_of(k * n, n), n)
        t[pl.ds(pl.multiple_of(g.NZ + k * n, g.NZ), n), :] = zy_sum(c[r, :] * x[r, :], g.NZ)
        return carry

    lax.fori_loop(first, last, turn, 0)


def box_at(g, t, k):
    n = g.CH * g.NZ
    parts = [t[pl.ds(pl.multiple_of(k * n + o * g.NZ, g.NZ), n), :] for o in range(3)]
    return parts[0] + parts[1] + parts[2]


def coarse_correction(g, s, ym, yl, zd):
    planes = g.nxm + 2
    rows = planes * g.NZm
    shape = (rows, g.PL * g.NZl)
    row, col = iota(shape, 0), iota(shape, 1)
    plane = row // g.NZm + (2 * LH - 1)
    want = (plane // 2) * g.NZl + (row % g.NZm) // 2
    up_rows = jnp.where(col == want, 1.0, 0.0).astype(F32)
    shape = (g.NYl, g.WYm)
    off = g.start(s) // 4
    up_lanes = jnp.where(
        iota(shape, 0) == off + iota(shape, 1) // 2, 1.0, 0.0
    ).astype(F32)
    low = dot(dot(up_rows, yl[...]), up_lanes)
    at = (MH - 1) * g.NZm
    both = ym[at : at + rows, :] + low
    shape = (g.WYm, g.WY)
    wide = jnp.where(iota(shape, 0) == iota(shape, 1) // 2, 1.0, 0.0).astype(F32)
    v = dot(both, wide)
    put_blocks(zd, pl.ds(0, rows, stride=2), v)
    put_blocks(zd, pl.ds(1, rows, stride=2), v)


def doubled(g, zd, plane, planes):
    at = (plane + 2) // 2 * g.NZ
    if planes == 1:
        return blocks(zd, slice(at, at + g.NZ))
    v = blocks(zd, slice(at, at + planes // 2 * g.NZ)).reshape(planes // 2, 1, g.NZ, g.WY)
    v = jnp.broadcast_to(v, (planes // 2, 2, g.NZ, g.WY))
    return v.reshape(planes * g.NZ, g.WY)


def pieces(g):
    return [(-1, 1)] + [(p, g.CH) for p in range(0, g.nx, g.CH)] + [(g.nx, 1)]


def cycle(g, idx, tab, fine, mid, low, x_old, x, bi, diag, zd, keep, xb=None):
    _, c, D, K, y, _, t = fine
    fine_smooth(g, idx, tab, *fine)
    coarse_smooth(g, idx, tab, mid, low)
    coarse_correction(g, idx[0], mid[4], low[4], zd)
    for p, planes in pieces(g):
        n = planes * g.NZ
        rr = slice((OUT + p) * g.NZ, (OUT + p) * g.NZ + n)
        r = slice((1 + p) * g.NZ, (1 + p) * g.NZ + n)
        v = 0.5 * (y[rr, :] + doubled(g, zd, p, planes))
        if x_old is not None:
            v = x_old[r, :] + v
        x[r, :] = v
        if xb is not None and planes == g.CH and 0 <= p < g.nx:
            put_blocks(xb, slice(p * g.NZ, p * g.NZ + n), v)
        t[r, :] = zy_sum(c[rr, :] * v, g.NZ)
    step = g.CH * g.NZ
    for p in range(0, g.nx, g.CH):
        at = p * g.NZ
        box = (
            t[at : at + step, :]
            + t[at + g.NZ : at + g.NZ + step, :]
            + t[at + 2 * g.NZ : at + 2 * g.NZ + step, :]
        )
        r = slice(at, at + step)
        rr = slice(OUT * g.NZ + at, OUT * g.NZ + at + step)
        v = bi[r, :] - D[rr, :] * x[at + g.NZ : at + g.NZ + step, :] + K[rr, :] * box
        keep(r, v, v * diag[r, :])


def send_defect(g, s, gi, rm, rl, res, to_l, to_r, to_l2, to_r2):
    rm[...] = fine_to_mid(res, 0, g.nx, g.NZ, 4.0)
    shape = (g.nxl * g.NZl, g.nxm * g.NZm)
    row, col = iota(shape, 0), iota(shape, 1)
    same_x = col // (2 * g.NZm) == row // g.NZl
    same_z = (col % g.NZm) // 2 == row % g.NZl
    rows = jnp.where(same_x & same_z, 0.5, 0.0).astype(F32)
    shape = (g.WYm, g.NYl)
    off = g.start(s) // 4
    lanes = jnp.where(iota(shape, 0) // 2 + off == iota(shape, 1), 1.0, 0.0).astype(F32)
    rl[...] = dot(dot(rows, rm[...]), lanes)
    at = 0
    for ref, n in ((gi, XH * g.NZ), (rm, MH * g.NZm), (rl, g.nxl * g.NZl)):
        total = ref.shape[0]
        for y in range(0, ref.shape[1], 128):
            to_l[at : at + n, :] = ref[0:n, y : y + 128]
            to_r[at : at + n, :] = ref[total - n :, y : y + 128]
            at += n
    far = (LH - g.nxl) * g.NZl
    total = rl.shape[0]
    for b in range(g.NYl // 128):
        lanes = slice(128 * b, 128 * b + 128)
        to_l2[b * far : b * far + far, :] = rl[0:far, lanes]
        to_r2[b * far : b * far + far, :] = rl[total - far :, lanes]


def first_kernel(g, idx, tab, *refs):
    f, m, l, f2nd, m2nd, from_l, from_r, from_l2nd, from_r2nd, from_l2, from_r2 = refs[:11]
    refs = refs[11:]
    (c, D, K, bi, diag, cm, Dm, Km, im, cl, Dl, Kl, il) = refs[:13]
    x, gi_own, rm, rl, to_l, to_r, to_l2, to_r2 = refs[13:21]
    (gi, y, d, t, gm, ym, dm, tm, gl, yl, dl, tl, zd, res) = refs[21:]
    s, li = idx[0], idx[1]
    clear_box_edges(g, t, tm, tl)
    fill = (0.0, 0.0, 1.0)

    def kept(ok, v, a):
        return jnp.where(ok, v, fill[a])

    n = XH * g.NZ
    lo, hi = OUT * g.NZ, (OUT + g.nx) * g.NZ
    at = {0: 0, 1: 0}
    region = (gi, c, y)
    for a in range(3):
        left, right = (from_l2nd, from_r2nd) if a else (from_l, from_r)
        q = min(a, 1)
        region[a][0 : lo - n, :] = jnp.full((lo - n, g.WY), fill[a], F32)
        region[a][hi + n :, :] = jnp.full((lo - n, g.WY), fill[a], F32)
        region[a][lo:hi, :] = f2nd[a - 1] if a else f[0]
        for yy in range(0, g.WY, 128):
            rows = slice(at[q], at[q] + n)
            region[a][lo - n : lo, yy : yy + 128] = kept(li > 0, left[rows, :], a)
            region[a][hi : hi + n, yy : yy + 128] = kept(
                li < g.nl - 1, right[rows, :], a
            )
            at[q] += n
    step = g.CH * g.NZ

    def build(k, carry):
        r = pl.ds(pl.multiple_of(k * step, step), step)
        b0 = gi[r, :]
        dg, inv, sc, kk = coefficients(b0, c[r, :], y[r, :])
        gi[r, :] = b0 * inv
        D[r, :] = sc
        K[r, :] = kk
        y[r, :] = dg
        return carry

    lax.fori_loop(0, g.PF // g.CH, build, 0)
    bi[...] = gi[lo:hi, :]
    diag[...] = y[lo:hi, :]

    n = MH * g.NZm
    parts = []
    for a in range(3):
        halves = []
        left, right = (from_l2nd, from_r2nd) if a else (from_l, from_r)
        q = min(a, 1)
        for _ in range(0, g.WYm, 128):
            rows = slice(at[q], at[q] + n)
            halves.append(
                (kept(li > 0, left[rows, :], a), kept(li < g.nl - 1, right[rows, :], a))
            )
            at[q] += n
        left = jnp.concatenate([v[0] for v in halves], axis=1)
        right = jnp.concatenate([v[1] for v in halves], axis=1)
        own_mid = m2nd[a - 1] if a else m[0]
        parts.append(jnp.concatenate([left, own_mid, right], axis=0))
    _, inv, sc, kk = coefficients(*parts)
    cm[...] = parts[1]
    Dm[...] = sc
    Km[...] = kk
    im[...] = inv
    gm[...] = 4.0 * parts[0] * inv

    n = g.nxl * g.NZl
    far = (LH - g.nxl) * g.NZl
    store = (gl, cl, il)
    at, at2 = at[0], 0
    for a in range(3):
        for yy in range(0, g.NYl, 128):
            lanes = slice(yy, yy + 128)
            ref = store[a]
            ref[0:far, lanes] = kept(li > 1, from_l2[at2 : at2 + far, :], a)
            ref[far : far + n, lanes] = kept(li > 0, from_l[at : at + n, :], a)
            ref[far + n : far + 2 * n, lanes] = l[a, :, lanes]
            ref[far + 2 * n : far + 3 * n, lanes] = kept(
                li < g.nl - 1, from_r[at : at + n, :], a
            )
            ref[far + 3 * n :, lanes] = kept(li < g.nl - 2, from_r2[at2 : at2 + far, :], a)
            at += n
            at2 += far
    _, inv, sc, kk = coefficients(gl[...], cl[...], il[...])
    Dl[...] = sc
    Kl[...] = kk
    il[...] = inv
    gl[...] = 16.0 * gl[...] * inv

    def keep(r, scaled, plain):
        gi_own[r, :] = scaled
        put_blocks(res, r, plain)

    fine = (gi, c, D, K, y, d, t)
    mid = (gm, cm, Dm, Km, ym, dm, tm)
    low = (gl, cl, Dl, Kl, yl, dl, tl)
    cycle(g, idx, tab, fine, mid, low, None, x, bi, diag, zd, keep)
    send_defect(g, s, gi_own, rm, rl, res, to_l, to_r, to_l2, to_r2)


def gather_defect(g, gi_own, rm, rl, from_l, from_r, from_l2, from_r2, gi, gm, im, gl, il):
    lo, hi = OUT * g.NZ, (OUT + g.nx) * g.NZ
    n = XH * g.NZ
    zeros = jnp.zeros((lo - n, g.WY), F32)
    gi[0 : lo - n, :] = zeros
    gi[hi + n :, :] = zeros
    gi[lo:hi, :] = gi_own[...]
    at = 0
    for y in range(0, g.WY, 128):
        gi[lo - n : lo, y : y + 128] = from_l[at : at + n, :]
        gi[hi : hi + n, y : y + 128] = from_r[at : at + n, :]
        at += n
    n, own = MH * g.NZm, rm.shape[0]
    for y in range(0, g.WYm, 128):
        lanes = slice(y, y + 128)
        gm[0:n, lanes] = from_l[at : at + n, :] * im[0:n, lanes]
        gm[n + own :, lanes] = from_r[at : at + n, :] * im[n + own :, lanes]
        at += n
    gm[n : n + own, :] = rm[...] * im[n : n + own, :]
    n = g.nxl * g.NZl
    far = (LH - g.nxl) * g.NZl
    for b in range(g.NYl // 128):
        lanes = slice(128 * b, 128 * b + 128)
        rows = slice(b * far, b * far + far)
        gl[0:far, lanes] = from_l2[rows, :]
        gl[far : far + n, lanes] = from_l[at : at + n, :]
        gl[far + n : far + 2 * n, lanes] = rl[:, lanes]
        gl[far + 2 * n : far + 3 * n, lanes] = from_r[at : at + n, :]
        gl[far + 3 * n :, lanes] = from_r2[rows, :]
        at += n
    gl[...] = gl[...] * il[...]


def cycle_kernel(g, n_outs, idx, tab, *refs):
    gi_own, rm, rl, x_old = refs[:4]
    received = refs[4:8]
    (c, D, K, bi, diag, cm, Dm, Km, im, cl, Dl, Kl, il) = refs[8:21]
    outs = refs[21 : 21 + n_outs]
    scr = refs[21 + n_outs :]
    (gi, y, d, t, gm, ym, dm, tm, gl, yl, dl, tl, zd, res) = scr[:14]
    clear_box_edges(g, t, tm, tl)
    gather_defect(g, gi_own, rm, rl, *received, gi, gm, im, gl, il)
    fine = (gi, c, D, K, y, d, t)
    mid = (gm, cm, Dm, Km, ym, dm, tm)
    low = (gl, cl, Dl, Kl, yl, dl, tl)
    s = idx[0]
    if len(scr) == 14:
        x, gi_new, rm_new, rl_new = outs[:4]

        def keep(r, scaled, plain):
            gi_new[r, :] = scaled
            put_blocks(res, r, plain)

        cycle(g, idx, tab, fine, mid, low, x_old, x, bi, diag, zd, keep)
        send_defect(g, s, gi_new, rm_new, rl_new, res, *outs[4:])
        return
    x, xb = scr[14:]

    def keep_plain(r, scaled, plain):
        put_blocks(res, r, plain)

    cycle(g, idx, tab, fine, mid, low, x_old, x, bi, diag, zd, keep_plain, xb)
    shift = lax.rem(g.WY - (s * g.ny - g.start(s)), g.WY)
    for k in range(g.ns):
        partner = lax.rem(s - k + g.ns, g.ns)
        for o, ref in enumerate((xb, res)):

            def row(z, o=o, ref=ref, k=k, partner=partner):
                v = blocks(ref, pl.ds(partner * g.nz + z, g.nx, stride=g.NZ))
                at = (o * g.nz + z) * g.nx
                if not isinstance(at, int):
                    at = pl.multiple_of(at, 8)
                outs[k][pl.ds(at, g.nx), :] = pltpu.roll(v, shift, 1)[:, : g.PW]

            repeat(g, g.nz, row)


def unpack_kernel(g, idx, *refs):
    s = idx[0]
    recv, outs = refs[: g.ns], refs[g.ns :]
    for o in range(2):
        for z in range(g.nz):
            at = (o * g.nz + z) * g.nx
            total = None
            if g.ny % 128 == 0:
                wide = jnp.concatenate(
                    [recv[j][at : at + g.nx, : g.ny] for j in range(g.ns)], axis=1
                )
                total = pltpu.roll(wide, s * g.ny, 1)
            else:
                mine = iota((g.nx, g.NY), 1) < g.ny
                for j in range(g.ns):
                    src = lax.rem(s + j, g.ns)
                    v = recv[j][at : at + g.nx, :]
                    pad = jnp.zeros((g.nx, g.NY - g.PW), F32)
                    v = jnp.where(mine, jnp.concatenate([v, pad], axis=1), 0.0)
                    v = pltpu.roll(v, src * g.ny, 1)
                    total = v if total is None else total + v
            outs[o][z] = total


def ring(value, axis, by):
    peers = lax.axis_size(axis)
    if by % peers == 0:
        return value
    return lax.ppermute(value, axis, [(i, (i - by) % peers) for i in range(peers)])


def sweep_tables(degrees, lower, upper):
    centre = (upper + lower) * 0.5
    radius = (upper - lower) * 0.5
    ratio = centre / radius
    rho = 1.0 / ratio
    alphas, betas = [], []
    for j in range(1, MAXDEG):
        new = 1.0 / (2.0 * ratio - rho)
        active = j < degrees
        alphas.append(jnp.where(active, new * rho, 0.0))
        betas.append(jnp.where(active, 2.0 * new / radius, 0.0))
        rho = new
    zero = jnp.zeros_like(rho)
    return jnp.stack([1.0 / centre] + alphas + [zero] + betas, axis=1)


def shards(right_side, scale_field, mass_field, degrees, lower_bound, upper_bound):
    g = Geometry(right_side.shape, lax.axis_size("slab"), lax.axis_size("level"))
    place = jnp.stack([lax.axis_index("slab"), lax.axis_index("level")])
    place = place.astype(jnp.int32)
    idx = jnp.concatenate([place, degrees])
    tab = sweep_tables(degrees, lower_bound, upper_bound)

    def call(kernel, outs, scratch, smem, *args):
        return vmem_call(lambda *refs: kernel(g, *refs), outs, scratch, smem, args)

    shape = right_side.shape
    packs = call(
        pack_kernel, [(g.rows_1st, g.WY)] * g.ns + [(g.rows_2nd, g.WY)] * g.ns, [], 1,
        place, jnp.stack([right_side, scale_field, mass_field]),
    )
    packs_1st, packs_2nd = [], []
    for k in range(g.ns):
        packs_1st.append(ring(packs[k], "slab", k))
    for k in range(g.ns):
        packs_2nd.append(ring(packs[g.ns + k], "slab", k))

    fine = (g.PF * g.NZ, g.WY)
    own = (g.nx * g.NZ, g.WY)
    mid = (g.PM * g.NZm, g.WYm)
    low = (g.PL * g.NZl, g.NYl)
    own_blocks = (g.WY // 128, own[0], 128)
    scratch = [
        fine, fine, fine, (fine[0] + 2 * g.NZ, g.WY),
        mid, mid, mid, (mid[0] + 2 * g.NZm, g.WYm),
        low, low, low, (low[0] + 2 * g.NZl, g.NYl),
        (g.WY // 128, (g.nxm + 2) * g.NZ, 128), own_blocks,
    ]

    def assemble(count, packs):
        outs = [
            (count, *own), (count, g.nxm * g.NZm, g.WYm),
            (edge_rows(g, count), 128), (edge_rows(g, count), 128),
        ] + [(3, g.nxl * g.NZl, g.NYl)] * (count == 1)
        return vmem_call(
            lambda *refs: assemble_kernel(g, count, *refs),
            outs, [(count, *own_blocks)], 1, (place, *packs),
        )

    f, m, to_left, to_right, l = assemble(1, packs_1st)
    far = (LH - g.nxl) * g.NZl
    lanes = g.NYl // 128

    def far_rows(part):
        parts = part.reshape(3, part.shape[1], lanes, 128)
        return parts.transpose(0, 2, 1, 3).reshape(3 * lanes * far, 128)

    from_l = ring(to_right, "level", -1)
    from_r = ring(to_left, "level", 1)
    from_l2 = ring(far_rows(l[:, l.shape[1] - far :]), "level", -2)
    from_r2 = ring(far_rows(l[:, :far]), "level", 2)

    f2nd, m2nd, to_left, to_right = assemble(2, packs_2nd)
    from_l2nd = ring(to_right, "level", -1)
    from_r2nd = ring(to_left, "level", 1)

    x_shape = ((g.nx + 2) * g.NZ, g.WY)
    rm_shape, rl_shape = (g.nxm * g.NZm, g.WYm), (g.nxl * g.NZl, g.NYl)
    sent = (
        XH * g.NZ * (g.WY // 128) + MH * g.NZm * (g.WYm // 128) + rl_shape[0] * lanes,
        128,
    )
    sent2 = (lanes * far, 128)
    state = [x_shape, own, rm_shape, rl_shape, sent, sent, sent2, sent2]
    outs = call(
        first_kernel, [fine] * 3 + [own] * 2 + [mid] * 4 + [low] * 4 + state, scratch, 2,
        idx, tab, f, m, l, f2nd, m2nd,
        from_l, from_r, from_l2nd, from_r2nd, from_l2, from_r2,
    )
    coefs, outs = outs[:13], outs[13:]
    for cycle_no in range(1, CYCLES):
        x, gi, rm, rl, to_l, to_r, to_l2, to_r2 = outs
        received = (
            ring(to_r, "level", -1),
            ring(to_l, "level", 1),
            ring(to_r2, "level", -2),
            ring(to_l2, "level", 2),
        )
        if cycle_no < CYCLES - 1:
            shapes, more = state, []
        else:
            shapes, more = [(2 * g.nz * g.nx, g.PW)] * g.ns, [x_shape, own_blocks]
        outs = vmem_call(
            lambda *refs, n=len(shapes): cycle_kernel(g, n, *refs),
            shapes, scratch + more, 2,
            (idx, tab, gi, rm, rl, x, *received, *coefs),
        )
    packs = [ring(v, "slab", k) for k, v in enumerate(outs)]
    return tuple(call(unpack_kernel, [shape, shape], [], 1, place, *packs))


def solution(mesh):
    spread = P("slab", "level", None)
    return jax.shard_map(
        shards,
        mesh=mesh,
        in_specs=(spread, spread, spread, P(), P(), P()),
        out_specs=(spread, spread),
        check_vma=False,
    )
```

```python
import math

import jax
import jax.numpy as jnp
from jax import lax
from jax.experimental import pallas as pl
from jax.experimental.pallas import tpu as pltpu
from jax.sharding import PartitionSpec as P


CYCLES = 3
MAXDEG = 6
INTERPRET = False

F32 = jnp.float32
OUT = 8
XH = 6
MH = 6
LH = 6
YH = 64


def blocks(ref, rows):
    return jnp.concatenate([ref[b, rows, :] for b in range(ref.shape[0])], axis=1)


def put_blocks(ref, rows, value):
    for b in range(ref.shape[0]):
        ref[b, rows, :] = value[:, 128 * b : 128 * b + 128]


def thirds(v):
    high = v.astype(jnp.bfloat16)
    rest = v - high.astype(F32)
    mid = rest.astype(jnp.bfloat16)
    return high, mid, (rest - mid.astype(F32)).astype(jnp.bfloat16)


def spread(v, pick):
    parts = [jnp.dot(p, pick, preferred_element_type=F32) for p in thirds(v)]
    return parts[0] + (parts[1] + parts[2])


def gathered(pick, v):
    parts = [jnp.dot(pick, p, preferred_element_type=F32) for p in thirds(v)]
    return parts[0] + (parts[1] + parts[2])


def chosen(test, value=1.0):
    return jnp.where(test, value, 0.0).astype(F32).astype(jnp.bfloat16)


def iota(shape, dim):
    return lax.broadcasted_iota(jnp.int32, shape, dim)


def zy_sum(w, nz):
    rows, lanes = w.shape
    if nz % 8 == 0:
        v = w.reshape(rows // nz, nz // 8, 8, lanes)
        at = iota(v.shape, 2)
        edge = jnp.zeros_like(v[:, :1])
        up = pltpu.roll(w.reshape(rows // 8, 8, lanes), 1, 1).reshape(v.shape)
        down = pltpu.roll(w.reshape(rows // 8, 8, lanes), 7, 1).reshape(v.shape)
        up_over = down_over = edge
        if nz > 8:
            up_over = jnp.concatenate([edge, up[:, :-1]], axis=1)
            down_over = jnp.concatenate([down[:, 1:], edge], axis=1)
        s = v + jnp.where(at == 0, up_over, up) + jnp.where(at == 7, down_over, down)
        s = s.reshape(rows, lanes)
    else:
        at = iota(w.shape, 0) & (nz - 1)
        up = jnp.where(at == 0, 0.0, pltpu.roll(w, 1, 0))
        down = jnp.where(at == nz - 1, 0.0, pltpu.roll(w, rows - 1, 0))
        s = w + up + down
    at = iota((rows, 128), 1)
    n = lanes // 128
    part = [s[:, 128 * b : 128 * b + 128] for b in range(n)]
    left = [pltpu.roll(p, 1, 1) for p in part]
    right = [pltpu.roll(p, 127, 1) for p in part]
    out = []
    for b in range(n):
        before = left[b - 1] if b else 0.0
        after = right[b + 1] if b < n - 1 else 0.0
        out.append(
            part[b] + jnp.where(at == 0, before, left[b]) + jnp.where(at == 127, after, right[b])
        )
    return jnp.concatenate(out, axis=1)


class Geometry:
    def __init__(self, shape, ns, nl):
        self.nz, self.nx, self.NY = shape
        self.ns, self.nl = ns, nl
        self.NZ = self.nz * ns
        self.ny = self.NY // ns
        self.WY = min(self.NY, -(-(self.ny + 2 * YH) // 128) * 128)
        self.PW = -(-self.ny // 128) * 128
        self.nxm, self.nxl = self.nx // 2, self.nx // 4
        self.NZm, self.NZl = self.NZ // 2, self.NZ // 4
        self.WYm, self.NYm, self.NYl = self.WY // 2, self.NY // 2, self.NY // 4
        self.CH = max(1, min(4, 64 // self.NZ))
        self.unrolled = self.NZ <= 16
        self.PF = self.nx + 2 * OUT
        self.PM = self.nxm + 2 * MH
        self.PL = self.nxl + 2 * LH
        assert self.nx % self.CH == 0 and OUT % self.CH == 0 and XH <= self.nx
        assert self.nxl < LH <= 2 * self.nxl and MH <= self.nxm
        assert (self.nxl * self.nz // 4) % 4 == 0 and self.WYm % 128 == 0 and self.NYl % 128 == 0
        self.lowrows = self.nxl * (self.nz // 4)
        self.rows_1st = self.nz * self.nx + -(-3 * self.lowrows // 8) * 8
        self.rows_2nd = 2 * self.nz * self.nx

    def start(self, s):
        return jnp.clip(s * self.ny - (self.WY - self.ny) // 2, 0, self.NY - self.WY)


def vmem_call(kernel, outs, scratch, smem, args):
    specs = [pl.BlockSpec(memory_space=pltpu.SMEM)] * smem
    specs += [pl.BlockSpec(memory_space=pltpu.VMEM)] * (len(args) - smem)
    shapes = list(outs) + list(scratch) + [a.shape for a in args[smem:]]
    held = sum(4 * math.prod(o) for o in shapes)
    return pl.pallas_call(
        kernel,
        out_shape=[jax.ShapeDtypeStruct(o, F32) for o in outs],
        in_specs=specs,
        out_specs=[pl.BlockSpec(memory_space=pltpu.VMEM)] * len(outs),
        scratch_shapes=[pltpu.VMEM(o, F32) for o in scratch],
        compiler_params=pltpu.CompilerParams(vmem_limit_bytes=min(held * 3 // 2 + (4 << 20), 60 << 20)),
        interpret=INTERPRET,
    )(*args)


def repeat(g, n, body):
    if g.ns <= 4:
        for i in range(n):
            body(i)
    else:
        lax.fori_loop(0, n, lambda i, carry: (body(i), carry)[1], 0)


def pack_kernel(g, idx, near, *outs):
    s = idx[0]
    lane_pick = chosen(iota((g.NY, g.NYl), 0) // 4 == iota((g.NY, g.NYl), 1))
    row_pick = chosen(iota((g.nxl, g.nx), 1) // 4 == iota((g.nxl, g.nx), 0), 1.0 / 64.0)
    base = g.nz * g.nx
    first, second = outs[: g.ns], outs[g.ns :]
    turns = []
    for k in range(g.ns):
        first[k][base:, :] = jnp.zeros((g.rows_1st - base, g.WY), F32)
        partner = lax.rem(s - k + g.ns, g.ns)
        turns.append(lax.rem(g.NY - g.start(partner), g.NY))
    for a, (group, at_a) in enumerate(((first, 0), (second, 0), (second, 1))):
        arr = near.at[a]
        for k in range(g.ns):

            def row(z, at_a=at_a, k=k, arr=arr, group=group):
                at = (at_a * g.nz + z) * g.nx
                if not isinstance(at, int):
                    at = pl.multiple_of(at, 8)
                v = pltpu.roll(arr[z], turns[k], 1)[:, : g.WY]
                group[k][pl.ds(at, g.nx), :] = v

            repeat(g, g.nz, row)
        for zl in range(g.nz // 4):
            col = arr[4 * zl] + arr[4 * zl + 1] + arr[4 * zl + 2] + arr[4 * zl + 3]
            low = gathered(row_pick, spread(col, lane_pick))
            at = base + a * g.lowrows + zl * g.nxl
            for k in range(g.ns):
                first[k][at : at + g.nxl, : g.NYl] = low


def fine_to_mid(src, row, planes, nz, scale):
    n = planes * nz // 2
    lanes = src.shape[0] * 128
    v = blocks(src, pl.ds(row, n, stride=2)) + blocks(src, pl.ds(row + 1, n, stride=2))
    v = v.reshape(planes // 2, 2, nz // 2, lanes)
    v = (v[:, 0] + v[:, 1]).reshape(planes // 2 * (nz // 2), lanes)
    half = (lanes, lanes // 2)
    return spread(v, chosen(iota(half, 0) // 2 == iota(half, 1), scale / 8.0))


def assemble_kernel(g, count, idx, *refs):
    s = idx[0]
    recv, refs = refs[: g.ns], refs[g.ns :]
    f_out, m_out, to_left, to_right = refs[:4]
    l_out, fs = refs[4] if count == 1 else None, refs[-1]
    base = count * g.nz * g.nx
    for j in range(g.ns):
        src = lax.rem(s + j, g.ns)
        for a in range(count):

            def row(z, a=a, j=j, src=src):
                at = (a * g.nz + z) * g.nx
                if not isinstance(at, int):
                    at = pl.multiple_of(at, 8)
                rows = pl.ds(src * g.nz + z, g.nx, stride=g.NZ)
                put_blocks(fs.at[a], rows, recv[j][pl.ds(at, g.nx), :])

            repeat(g, g.nz, row)
        for i in range(3 if count == 1 else 0):
            for zl in range(g.nz // 4):
                at = base + i * g.lowrows + zl * g.nxl
                for x in range(g.nxl):
                    l_out[i, pl.ds(x * g.NZl + src * (g.nz // 4) + zl, 1), :] = recv[j][
                        at + x : at + x + 1, : g.NYl
                    ]
    nxz = g.nx * g.NZ
    at, n = 0, XH * g.NZ
    for a in range(count):
        f_out[a] = blocks(fs.at[a], slice(0, nxz))
        m_out[a] = fine_to_mid(fs.at[a], 0, g.nx, g.NZ, 1.0)
        for b in range(g.WY // 128):
            to_left[at : at + n, :] = fs[a, b, 0:n, :]
            to_right[at : at + n, :] = fs[a, b, nxz - n :, :]
            at += n
    n, total = MH * g.NZm, g.nxm * g.NZm
    for a in range(count):
        for y in range(0, g.WYm, 128):
            to_left[at : at + n, :] = m_out[a, 0:n, y : y + 128]
            to_right[at : at + n, :] = m_out[a, total - n :, y : y + 128]
            at += n
    n = g.nxl * g.NZl
    for i in range(3 if count == 1 else 0):
        for y in range(0, g.NYl, 128):
            to_left[at : at + n, :] = l_out[i, :, y : y + 128]
            to_right[at : at + n, :] = l_out[i, :, y : y + 128]
            at += n


def edge_rows(g, count):
    rows = count * XH * g.NZ * (g.WY // 128) + count * MH * g.NZm * (g.WYm // 128)
    return rows + (3 * g.nxl * g.NZl * (g.NYl // 128) if count == 1 else 0)


def coefficients(b, c, q):
    diag = c * c + q
    inv = 1.0 / diag
    scaled = (27.0 / 26.0 * (c * c) + q) * inv
    return diag, inv, scaled, c * inv / 26.0


def coarse_smooth(g, idx, tab, mid, low):
    for level, (gi, c, D, K, y, d, t) in ((1, mid), (2, low)):
        y[...] = gi[...] * tab[level, 0]
        d[...] = y[...]

    def turn(j, carry):
        for nz, (gi, c, D, K, y, d, t) in ((g.NZm, mid), (g.NZl, low)):
            rows = c.shape[0]
            t[nz : nz + rows, :] = zy_sum(c[...] * y[...], nz)
        for level, nz, (gi, c, D, K, y, d, t) in ((1, g.NZm, mid), (2, g.NZl, low)):
            rows = c.shape[0]
            box = t[0:rows, :] + t[nz : nz + rows, :] + t[2 * nz : 2 * nz + rows, :]
            e = gi[...] - D[...] * y[...] + K[...] * box
            nd = tab[level, j] * d[...] + tab[level, MAXDEG + j] * e
            d[...] = nd
            y[...] = y[...] + nd
        return carry

    lax.fori_loop(1, jnp.maximum(idx[3], idx[4]), turn, 0)


def small_sweep(tab, j, grids):
    for level, nz, (gi, c, D, K, y, d, t) in grids:
        rows = c.shape[0]
        t[nz : nz + rows, :] = zy_sum(c[...] * y[...], nz)
    for level, nz, (gi, c, D, K, y, d, t) in grids:
        rows = c.shape[0]
        box = t[0:rows, :] + t[nz : nz + rows, :] + t[2 * nz : 2 * nz + rows, :]
        e = gi[...] - D[...] * y[...] + K[...] * box
        nd = tab[level, j] * d[...] + tab[level, MAXDEG + j] * e
        d[...] = nd
        y[...] = y[...] + nd


def all_sweeps(g, idx, tab, gi_at, fine, mid, low):
    _, c, D, K, y, d, _ = fine
    nz = g.NZ
    grids = ((1, g.NZm, mid), (2, g.NZl, low))
    for level, _, (gi, _, _, _, ys, ds, _) in grids:
        ys[...] = gi[...] * tab[level, 0]
        ds[...] = ys[...]

    def rows(p):
        return slice((OUT + p) * nz, (OUT + p + 1) * nz)

    def fine_sweep(j):
        alpha, beta = tab[0, j], tab[0, MAXDEG + j]
        reach = MAXDEG - j
        first, last = -reach - 1, g.nx + reach
        held, sums = {}, {}
        for p in range(first, last + 1):
            held[p] = gi_at(p) * tab[0, 0] if j == 1 else y[rows(p), :]
            sums[p] = zy_sum(c[rows(p), :] * held[p], nz)
            q = p - 1
            if q <= first:
                continue
            r = rows(q)
            box = sums[q - 1] + sums[q] + sums[p]
            e = gi_at(q) - D[r, :] * held[q] + K[r, :] * box
            nd = alpha * (held[q] if j == 1 else d[r, :]) + beta * e
            if j < MAXDEG - 1:
                d[r, :] = nd
            y[r, :] = held[q] + nd

    fine_sweep(1)
    small_sweep(tab, 1, grids)
    for j in range(2, MAXDEG):

        @pl.when(j < idx[2])
        def _(j=j):
            fine_sweep(j)
            small_sweep(tab, j, grids)

        @pl.when((j >= idx[2]) & (j < jnp.maximum(idx[3], idx[4])))
        def _(j=j):
            small_sweep(tab, j, grids)


def fine_smooth(g, idx, tab, gi, c, D, K, y, d, t):
    n = g.CH * g.NZ
    side, own = OUT // g.CH, g.nx // g.CH
    y[...] = gi[...] * tab[0, 0]
    d[...] = y[...]

    def turn(j, carry):
        radius = idx[2] - j
        ht = (radius + 1 + g.CH - 1) // g.CH
        h = (radius + g.CH - 1) // g.CH
        fine_boxes(g, side - ht, side + own + ht, c, y, t)

        def chunk(k, inner_carry):
            r = pl.ds(pl.multiple_of(k * n, n), n)
            old = y[r, :]
            e = gi[r, :] - D[r, :] * old + K[r, :] * box_at(g, t, k)
            nd = tab[0, j] * d[r, :] + tab[0, MAXDEG + j] * e
            d[r, :] = nd
            y[r, :] = old + nd
            return inner_carry

        lax.fori_loop(side - h, side + own + h, chunk, 0)
        return carry

    lax.fori_loop(1, idx[2], turn, 0)


def clear_box_edges(g, t, tm, tl):
    for ref, nz in ((t, g.NZ), (tm, g.NZm), (tl, g.NZl)):
        zeros = jnp.zeros((nz, ref.shape[1]), F32)
        ref[0:nz, :] = zeros
        ref[ref.shape[0] - nz :, :] = zeros


def fine_boxes(g, first, last, c, x, t):
    n = g.CH * g.NZ

    def turn(k, carry):
        r = pl.ds(pl.multiple_of(k * n, n), n)
        t[pl.ds(pl.multiple_of(g.NZ + k * n, g.NZ), n), :] = zy_sum(c[r, :] * x[r, :], g.NZ)
        return carry

    lax.fori_loop(first, last, turn, 0)


def box_at(g, t, k):
    n = g.CH * g.NZ
    parts = [t[pl.ds(pl.multiple_of(k * n + o * g.NZ, g.NZ), n), :] for o in range(3)]
    return parts[0] + parts[1] + parts[2]


def coarse_correction(g, s, ym, yl, zd):
    planes = g.nxm + 2
    shape = (g.WYm, g.WY)
    mid_lanes = chosen(iota(shape, 0) == iota(shape, 1) // 2)
    shape = (g.NYl, g.WY)
    low_lanes = chosen(iota(shape, 0) == g.start(s) // 4 + iota(shape, 1) // 4)
    first = (MH - 1) * g.NZm
    mid = spread(ym[first : first + planes * g.NZm, :], mid_lanes)
    low = spread(yl[...], low_lanes)
    shape = (planes * g.NZm, g.PL * g.NZl)
    row, col = iota(shape, 0), iota(shape, 1)
    plane = row // g.NZm + (2 * LH - 1)
    want = (plane // 2) * g.NZl + (row % g.NZm) // 2
    v = mid + gathered(chosen(col == want), low)
    n = planes * g.NZm
    put_blocks(zd, pl.ds(0, n, stride=2), v)
    put_blocks(zd, pl.ds(1, n, stride=2), v)


def doubled(g, zd, plane, planes):
    at = (plane + 2) // 2 * g.NZ
    if planes == 1:
        return blocks(zd, slice(at, at + g.NZ))
    v = blocks(zd, slice(at, at + planes // 2 * g.NZ)).reshape(planes // 2, 1, g.NZ, g.WY)
    v = jnp.broadcast_to(v, (planes // 2, 2, g.NZ, g.WY))
    return v.reshape(planes * g.NZ, g.WY)


def pieces(g):
    return [(-1, 1)] + [(p, g.CH) for p in range(0, g.nx, g.CH)] + [(g.nx, 1)]


def cycle(g, idx, tab, gi_at, fine, mid, low, x_old, x, bi, diag, zd, keep, xb=None):
    _, c, D, K, y, _, t = fine
    if g.unrolled:
        all_sweeps(g, idx, tab, gi_at, fine, mid, low)
    else:
        fine_smooth(g, idx, tab, *fine)
        coarse_smooth(g, idx, tab, mid, low)
    coarse_correction(g, idx[0], mid[4], low[4], zd)
    for p, planes in pieces(g):
        n = planes * g.NZ
        rr = slice((OUT + p) * g.NZ, (OUT + p) * g.NZ + n)
        r = slice((1 + p) * g.NZ, (1 + p) * g.NZ + n)
        v = 0.5 * (y[rr, :] + doubled(g, zd, p, planes))
        if x_old is not None:
            v = x_old[r, :] + v
        x[r, :] = v
        if xb is not None and planes == g.CH and 0 <= p < g.nx:
            put_blocks(xb, slice(p * g.NZ, p * g.NZ + n), v)
        t[r, :] = zy_sum(c[rr, :] * v, g.NZ)
    step = g.CH * g.NZ
    for p in range(0, g.nx, g.CH):
        at = p * g.NZ
        box = (
            t[at : at + step, :]
            + t[at + g.NZ : at + g.NZ + step, :]
            + t[at + 2 * g.NZ : at + 2 * g.NZ + step, :]
        )
        r = slice(at, at + step)
        rr = slice(OUT * g.NZ + at, OUT * g.NZ + at + step)
        v = bi[r, :] - D[rr, :] * x[at + g.NZ : at + g.NZ + step, :] + K[rr, :] * box
        keep(r, v, v * diag[r, :])


def send_defect(g, s, gi, rm, rl, res, to_l, to_r, to_l2, to_r2):
    rm[...] = fine_to_mid(res, 0, g.nx, g.NZ, 4.0)
    shape = (g.nxl * g.NZl, g.nxm * g.NZm)
    row, col = iota(shape, 0), iota(shape, 1)
    same_x = col // (2 * g.NZm) == row // g.NZl
    same_z = (col % g.NZm) // 2 == row % g.NZl
    rows = chosen(same_x & same_z, 0.5)
    shape = (g.WYm, g.NYl)
    off = g.start(s) // 4
    lanes = chosen(iota(shape, 0) // 2 + off == iota(shape, 1))
    rl[...] = spread(gathered(rows, rm[...]), lanes)
    at = 0
    for ref, n in ((gi, XH * g.NZ), (rm, MH * g.NZm), (rl, g.nxl * g.NZl)):
        total = ref.shape[0]
        for y in range(0, ref.shape[1], 128):
            to_l[at : at + n, :] = ref[0:n, y : y + 128]
            to_r[at : at + n, :] = ref[total - n :, y : y + 128]
            at += n
    far = (LH - g.nxl) * g.NZl
    total = rl.shape[0]
    for b in range(g.NYl // 128):
        lanes = slice(128 * b, 128 * b + 128)
        to_l2[b * far : b * far + far, :] = rl[0:far, lanes]
        to_r2[b * far : b * far + far, :] = rl[total - far :, lanes]


def first_kernel(g, idx, tab, *refs):
    f, m, l, f2nd, m2nd, from_l, from_r, from_l2nd, from_r2nd, from_l2, from_r2 = refs[:11]
    refs = refs[11:]
    (c, D, K, bi, diag, cm, Dm, Km, im, cl, Dl, Kl, il) = refs[:13]
    x, gi_own, rm, rl, to_l, to_r, to_l2, to_r2 = refs[13:21]
    (gi, y, d, t, gm, ym, dm, tm, gl, yl, dl, tl, zd, res) = refs[21:]
    s, li = idx[0], idx[1]
    clear_box_edges(g, t, tm, tl)
    fill = (0.0, 0.0, 1.0)

    def kept(ok, v, a):
        return jnp.where(ok, v, fill[a])

    n = XH * g.NZ
    lo, hi = OUT * g.NZ, (OUT + g.nx) * g.NZ
    at = {0: 0, 1: 0}
    region = (gi, c, y)
    for a in range(3):
        left, right = (from_l2nd, from_r2nd) if a else (from_l, from_r)
        q = min(a, 1)
        region[a][0 : lo - n, :] = jnp.full((lo - n, g.WY), fill[a], F32)
        region[a][hi + n :, :] = jnp.full((lo - n, g.WY), fill[a], F32)
        region[a][lo:hi, :] = f2nd[a - 1] if a else f[0]
        for yy in range(0, g.WY, 128):
            rows = slice(at[q], at[q] + n)
            region[a][lo - n : lo, yy : yy + 128] = kept(li > 0, left[rows, :], a)
            region[a][hi : hi + n, yy : yy + 128] = kept(
                li < g.nl - 1, right[rows, :], a
            )
            at[q] += n
    step = g.CH * g.NZ

    def build(k, carry):
        r = pl.ds(pl.multiple_of(k * step, step), step)
        b0 = gi[r, :]
        dg, inv, sc, kk = coefficients(b0, c[r, :], y[r, :])
        gi[r, :] = b0 * inv
        D[r, :] = sc
        K[r, :] = kk
        y[r, :] = dg
        return carry

    lax.fori_loop(0, g.PF // g.CH, build, 0)
    bi[...] = gi[lo:hi, :]
    diag[...] = y[lo:hi, :]

    n = MH * g.NZm
    parts = []
    for a in range(3):
        halves = []
        left, right = (from_l2nd, from_r2nd) if a else (from_l, from_r)
        q = min(a, 1)
        for _ in range(0, g.WYm, 128):
            rows = slice(at[q], at[q] + n)
            halves.append(
                (kept(li > 0, left[rows, :], a), kept(li < g.nl - 1, right[rows, :], a))
            )
            at[q] += n
        left = jnp.concatenate([v[0] for v in halves], axis=1)
        right = jnp.concatenate([v[1] for v in halves], axis=1)
        own_mid = m2nd[a - 1] if a else m[0]
        parts.append(jnp.concatenate([left, own_mid, right], axis=0))
    _, inv, sc, kk = coefficients(*parts)
    cm[...] = parts[1]
    Dm[...] = sc
    Km[...] = kk
    im[...] = inv
    gm[...] = 4.0 * parts[0] * inv

    n = g.nxl * g.NZl
    far = (LH - g.nxl) * g.NZl
    store = (gl, cl, il)
    at, at2 = at[0], 0
    for a in range(3):
        for yy in range(0, g.NYl, 128):
            lanes = slice(yy, yy + 128)
            ref = store[a]
            ref[0:far, lanes] = kept(li > 1, from_l2[at2 : at2 + far, :], a)
            ref[far : far + n, lanes] = kept(li > 0, from_l[at : at + n, :], a)
            ref[far + n : far + 2 * n, lanes] = l[a, :, lanes]
            ref[far + 2 * n : far + 3 * n, lanes] = kept(
                li < g.nl - 1, from_r[at : at + n, :], a
            )
            ref[far + 3 * n :, lanes] = kept(li < g.nl - 2, from_r2[at2 : at2 + far, :], a)
            at += n
            at2 += far
    _, inv, sc, kk = coefficients(gl[...], cl[...], il[...])
    Dl[...] = sc
    Kl[...] = kk
    il[...] = inv
    gl[...] = 16.0 * gl[...] * inv

    def keep(r, scaled, plain):
        gi_own[r, :] = scaled
        put_blocks(res, r, plain)

    fine = (gi, c, D, K, y, d, t)
    mid = (gm, cm, Dm, Km, ym, dm, tm)
    low = (gl, cl, Dl, Kl, yl, dl, tl)

    def gi_at(p):
        return gi[(OUT + p) * g.NZ : (OUT + p + 1) * g.NZ, :]

    cycle(g, idx, tab, gi_at, fine, mid, low, None, x, bi, diag, zd, keep)
    send_defect(g, s, gi_own, rm, rl, res, to_l, to_r, to_l2, to_r2)


def gather_defect(g, gi_own, rm, rl, from_l, from_r, from_l2, from_r2, gi, gm, im, gl, il):
    lo, hi = OUT * g.NZ, (OUT + g.nx) * g.NZ
    n = XH * g.NZ
    at = 0 if not g.unrolled else g.WY // 128 * n
    if not g.unrolled:
        zeros = jnp.zeros((lo - n, g.WY), F32)
        gi[0 : lo - n, :] = zeros
        gi[hi + n :, :] = zeros
        gi[lo:hi, :] = gi_own[...]
        for y in range(0, g.WY, 128):
            gi[lo - n : lo, y : y + 128] = from_l[at : at + n, :]
            gi[hi : hi + n, y : y + 128] = from_r[at : at + n, :]
            at += n
    n, own = MH * g.NZm, rm.shape[0]
    for y in range(0, g.WYm, 128):
        lanes = slice(y, y + 128)
        gm[0:n, lanes] = from_l[at : at + n, :] * im[0:n, lanes]
        gm[n + own :, lanes] = from_r[at : at + n, :] * im[n + own :, lanes]
        at += n
    gm[n : n + own, :] = rm[...] * im[n : n + own, :]
    n = g.nxl * g.NZl
    far = (LH - g.nxl) * g.NZl
    for b in range(g.NYl // 128):
        lanes = slice(128 * b, 128 * b + 128)
        rows = slice(b * far, b * far + far)
        gl[0:far, lanes] = from_l2[rows, :]
        gl[far : far + n, lanes] = from_l[at : at + n, :]
        gl[far + n : far + 2 * n, lanes] = rl[:, lanes]
        gl[far + 2 * n : far + 3 * n, lanes] = from_r[at : at + n, :]
        gl[far + 3 * n :, lanes] = from_r2[rows, :]
        at += n
    gl[...] = gl[...] * il[...]


def cycle_kernel(g, n_outs, idx, tab, *refs):
    gi_own, rm, rl, x_old = refs[:4]
    received = refs[4:8]
    (c, D, K, bi, diag, cm, Dm, Km, im, cl, Dl, Kl, il) = refs[8:21]
    outs = refs[21 : 21 + n_outs]
    scr = refs[21 + n_outs :]
    (gi, y, d, t, gm, ym, dm, tm, gl, yl, dl, tl, zd, res) = scr[:14]
    clear_box_edges(g, t, tm, tl)
    gather_defect(g, gi_own, rm, rl, *received, gi, gm, im, gl, il)
    fine = (gi, c, D, K, y, d, t)
    mid = (gm, cm, Dm, Km, ym, dm, tm)
    low = (gl, cl, Dl, Kl, yl, dl, tl)
    s = idx[0]

    def gi_at(p):
        if 0 <= p < g.nx:
            return gi_own[p * g.NZ : (p + 1) * g.NZ, :]
        part = received[0] if p < 0 else received[1]
        at = (p + XH if p < 0 else p - g.nx) * g.NZ
        step = XH * g.NZ
        return jnp.concatenate(
            [part[at + b * step : at + b * step + g.NZ, :] for b in range(g.WY // 128)],
            axis=1,
        )

    if len(scr) == 14:
        x, gi_new, rm_new, rl_new = outs[:4]

        def keep(r, scaled, plain):
            gi_new[r, :] = scaled
            put_blocks(res, r, plain)

        cycle(g, idx, tab, gi_at, fine, mid, low, x_old, x, bi, diag, zd, keep)
        send_defect(g, s, gi_new, rm_new, rl_new, res, *outs[4:])
        return
    x, xb = scr[14:]

    def keep_plain(r, scaled, plain):
        put_blocks(res, r, plain)

    cycle(g, idx, tab, gi_at, fine, mid, low, x_old, x, bi, diag, zd, keep_plain, xb)
    shift = lax.rem(g.WY - (s * g.ny - g.start(s)), g.WY)
    for k in range(g.ns):
        partner = lax.rem(s - k + g.ns, g.ns)
        for o, ref in enumerate((xb, res)):

            def row(z, o=o, ref=ref, k=k, partner=partner):
                v = blocks(ref, pl.ds(partner * g.nz + z, g.nx, stride=g.NZ))
                at = (o * g.nz + z) * g.nx
                if not isinstance(at, int):
                    at = pl.multiple_of(at, 8)
                outs[k][pl.ds(at, g.nx), :] = pltpu.roll(v, shift, 1)[:, : g.PW]

            repeat(g, g.nz, row)


def unpack_kernel(g, idx, *refs):
    s = idx[0]
    recv, outs = refs[: g.ns], refs[g.ns :]
    for o in range(2):
        for z in range(g.nz):
            at = (o * g.nz + z) * g.nx
            total = None
            if g.ny % 128 == 0:
                wide = jnp.concatenate(
                    [recv[j][at : at + g.nx, : g.ny] for j in range(g.ns)], axis=1
                )
                total = pltpu.roll(wide, s * g.ny, 1)
            else:
                mine = iota((g.nx, g.NY), 1) < g.ny
                for j in range(g.ns):
                    src = lax.rem(s + j, g.ns)
                    v = recv[j][at : at + g.nx, :]
                    pad = jnp.zeros((g.nx, g.NY - g.PW), F32)
                    v = jnp.where(mine, jnp.concatenate([v, pad], axis=1), 0.0)
                    v = pltpu.roll(v, src * g.ny, 1)
                    total = v if total is None else total + v
            outs[o][z] = total


def ring(value, axis, by):
    peers = lax.axis_size(axis)
    if by % peers == 0:
        return value
    return lax.ppermute(value, axis, [(i, (i - by) % peers) for i in range(peers)])


def sweep_tables(degrees, lower, upper):
    centre = (upper + lower) * 0.5
    radius = (upper - lower) * 0.5
    ratio = centre / radius
    rho = 1.0 / ratio
    alphas, betas = [], []
    for j in range(1, MAXDEG):
        new = 1.0 / (2.0 * ratio - rho)
        active = j < degrees
        alphas.append(jnp.where(active, new * rho, 0.0))
        betas.append(jnp.where(active, 2.0 * new / radius, 0.0))
        rho = new
    zero = jnp.zeros_like(rho)
    return jnp.stack([1.0 / centre] + alphas + [zero] + betas, axis=1)


def shards(right_side, scale_field, mass_field, degrees, lower_bound, upper_bound):
    g = Geometry(right_side.shape, lax.axis_size("slab"), lax.axis_size("level"))
    place = jnp.stack([lax.axis_index("slab"), lax.axis_index("level")])
    place = place.astype(jnp.int32)
    idx = jnp.concatenate([place, degrees])
    tab = sweep_tables(degrees, lower_bound, upper_bound)

    def call(kernel, outs, scratch, smem, *args):
        return vmem_call(lambda *refs: kernel(g, *refs), outs, scratch, smem, args)

    shape = right_side.shape
    packs = call(
        pack_kernel, [(g.rows_1st, g.WY)] * g.ns + [(g.rows_2nd, g.WY)] * g.ns, [], 1,
        place, jnp.stack([right_side, scale_field, mass_field]),
    )
    packs_1st, packs_2nd = [], []
    for k in range(g.ns):
        packs_1st.append(ring(packs[k], "slab", k))
    for k in range(g.ns):
        packs_2nd.append(ring(packs[g.ns + k], "slab", k))

    fine = (g.PF * g.NZ, g.WY)
    own = (g.nx * g.NZ, g.WY)
    mid = (g.PM * g.NZm, g.WYm)
    low = (g.PL * g.NZl, g.NYl)
    own_blocks = (g.WY // 128, own[0], 128)
    scratch = [
        fine, fine, fine, (fine[0] + 2 * g.NZ, g.WY),
        mid, mid, mid, (mid[0] + 2 * g.NZm, g.WYm),
        low, low, low, (low[0] + 2 * g.NZl, g.NYl),
        (g.WY // 128, (g.nxm + 2) * g.NZ, 128), own_blocks,
    ]

    def assemble(count, packs):
        outs = [
            (count, *own), (count, g.nxm * g.NZm, g.WYm),
            (edge_rows(g, count), 128), (edge_rows(g, count), 128),
        ] + [(3, g.nxl * g.NZl, g.NYl)] * (count == 1)
        return vmem_call(
            lambda *refs: assemble_kernel(g, count, *refs),
            outs, [(count, *own_blocks)], 1, (place, *packs),
        )

    f, m, to_left, to_right, l = assemble(1, packs_1st)
    far = (LH - g.nxl) * g.NZl
    lanes = g.NYl // 128

    def far_rows(part):
        parts = part.reshape(3, part.shape[1], lanes, 128)
        return parts.transpose(0, 2, 1, 3).reshape(3 * lanes * far, 128)

    from_l = ring(to_right, "level", -1)
    from_r = ring(to_left, "level", 1)
    from_l2 = ring(far_rows(l[:, l.shape[1] - far :]), "level", -2)
    from_r2 = ring(far_rows(l[:, :far]), "level", 2)

    f2nd, m2nd, to_left, to_right = assemble(2, packs_2nd)
    from_l2nd = ring(to_right, "level", -1)
    from_r2nd = ring(to_left, "level", 1)

    x_shape = ((g.nx + 2) * g.NZ, g.WY)
    rm_shape, rl_shape = (g.nxm * g.NZm, g.WYm), (g.nxl * g.NZl, g.NYl)
    sent = (
        XH * g.NZ * (g.WY // 128) + MH * g.NZm * (g.WYm // 128) + rl_shape[0] * lanes,
        128,
    )
    sent2 = (lanes * far, 128)
    state = [x_shape, own, rm_shape, rl_shape, sent, sent, sent2, sent2]
    outs = call(
        first_kernel, [fine] * 3 + [own] * 2 + [mid] * 4 + [low] * 4 + state, scratch, 2,
        idx, tab, f, m, l, f2nd, m2nd,
        from_l, from_r, from_l2nd, from_r2nd, from_l2, from_r2,
    )
    coefs, outs = outs[:13], outs[13:]
    for cycle_no in range(1, CYCLES):
        x, gi, rm, rl, to_l, to_r, to_l2, to_r2 = outs
        received = (
            ring(to_r, "level", -1),
            ring(to_l, "level", 1),
            ring(to_r2, "level", -2),
            ring(to_l2, "level", 2),
        )
        if cycle_no < CYCLES - 1:
            shapes, more = state, []
        else:
            shapes, more = [(2 * g.nz * g.nx, g.PW)] * g.ns, [x_shape, own_blocks]
        outs = vmem_call(
            lambda *refs, n=len(shapes): cycle_kernel(g, n, *refs),
            shapes, scratch + more, 2,
            (idx, tab, gi, rm, rl, x, *received, *coefs),
        )
    packs = [ring(v, "slab", k) for k, v in enumerate(outs)]
    return tuple(call(unpack_kernel, [shape, shape], [], 1, place, *packs))


def solution(mesh):
    spread = P("slab", "level", None)
    return jax.shard_map(
        shards,
        mesh=mesh,
        in_specs=(spread, spread, spread, P(), P(), P()),
        out_specs=(spread, spread),
        check_vma=False,
    )
```

```python
import math

import jax
import jax.numpy as jnp
from jax import lax
from jax.experimental import pallas as pl
from jax.experimental.pallas import tpu as pltpu
from jax.sharding import PartitionSpec as P


CYCLES = 3
MAXDEG = 6
INTERPRET = False

F32 = jnp.float32
OUT = 8
XH = 6
MH = 6
LH = 6
YH = 64


def blocks(ref, rows):
    return jnp.concatenate([ref[b, rows, :] for b in range(ref.shape[0])], axis=1)


def put_blocks(ref, rows, value):
    for b in range(ref.shape[0]):
        ref[b, rows, :] = value[:, 128 * b : 128 * b + 128]


def thirds(v):
    high = v.astype(jnp.bfloat16)
    rest = v - high.astype(F32)
    mid = rest.astype(jnp.bfloat16)
    return high, mid, (rest - mid.astype(F32)).astype(jnp.bfloat16)


def spread(v, pick):
    parts = [jnp.dot(p, pick, preferred_element_type=F32) for p in thirds(v)]
    return parts[0] + (parts[1] + parts[2])


def gathered(pick, v):
    parts = [jnp.dot(pick, p, preferred_element_type=F32) for p in thirds(v)]
    return parts[0] + (parts[1] + parts[2])


def chosen(test, value=1.0):
    return jnp.where(test, value, 0.0).astype(F32).astype(jnp.bfloat16)


def iota(shape, dim):
    return lax.broadcasted_iota(jnp.int32, shape, dim)


def zy_sum(w, nz):
    rows, lanes = w.shape
    if nz % 8 == 0:
        v = w.reshape(rows // nz, nz // 8, 8, lanes)
        at = iota(v.shape, 2)
        edge = jnp.zeros_like(v[:, :1])
        up = pltpu.roll(w.reshape(rows // 8, 8, lanes), 1, 1).reshape(v.shape)
        down = pltpu.roll(w.reshape(rows // 8, 8, lanes), 7, 1).reshape(v.shape)
        up_over = down_over = edge
        if nz > 8:
            up_over = jnp.concatenate([edge, up[:, :-1]], axis=1)
            down_over = jnp.concatenate([down[:, 1:], edge], axis=1)
        s = v + jnp.where(at == 0, up_over, up) + jnp.where(at == 7, down_over, down)
        s = s.reshape(rows, lanes)
    else:
        at = iota(w.shape, 0) & (nz - 1)
        up = jnp.where(at == 0, 0.0, pltpu.roll(w, 1, 0))
        down = jnp.where(at == nz - 1, 0.0, pltpu.roll(w, rows - 1, 0))
        s = w + up + down
    at = iota((rows, 128), 1)
    n = lanes // 128
    part = [s[:, 128 * b : 128 * b + 128] for b in range(n)]
    left = [pltpu.roll(p, 1, 1) for p in part]
    right = [pltpu.roll(p, 127, 1) for p in part]
    out = []
    for b in range(n):
        before = left[b - 1] if b else 0.0
        after = right[b + 1] if b < n - 1 else 0.0
        out.append(
            part[b] + jnp.where(at == 0, before, left[b]) + jnp.where(at == 127, after, right[b])
        )
    return jnp.concatenate(out, axis=1)


class Geometry:
    def __init__(self, shape, ns, nl):
        self.nz, self.nx, self.NY = shape
        self.ns, self.nl = ns, nl
        self.NZ = self.nz * ns
        self.ny = self.NY // ns
        self.WY = min(self.NY, -(-(self.ny + 2 * YH) // 128) * 128)
        self.PW = -(-self.ny // 128) * 128
        self.nxm, self.nxl = self.nx // 2, self.nx // 4
        self.NZm, self.NZl = self.NZ // 2, self.NZ // 4
        self.WYm, self.NYm, self.NYl = self.WY // 2, self.NY // 2, self.NY // 4
        self.CH = max(1, min(4, 64 // self.NZ))
        self.unrolled = self.NZ <= 16
        self.PF = self.nx + 2 * OUT
        self.PM = self.nxm + 2 * MH
        self.PL = self.nxl + 2 * LH
        assert self.nx % self.CH == 0 and OUT % self.CH == 0 and XH <= self.nx
        assert self.nxl < LH <= 2 * self.nxl and MH <= self.nxm
        assert (self.nxl * self.nz // 4) % 4 == 0 and self.WYm % 128 == 0 and self.NYl % 128 == 0
        self.lowrows = self.nxl * (self.nz // 4)
        self.rows_1st = self.nz * self.nx + -(-3 * self.lowrows // 8) * 8
        self.rows_2nd = 2 * self.nz * self.nx

    def start(self, s):
        return jnp.clip(s * self.ny - (self.WY - self.ny) // 2, 0, self.NY - self.WY)


def vmem_call(kernel, outs, scratch, smem, args):
    specs = [pl.BlockSpec(memory_space=pltpu.SMEM)] * smem
    specs += [pl.BlockSpec(memory_space=pltpu.VMEM)] * (len(args) - smem)
    shapes = list(outs) + list(scratch) + [a.shape for a in args[smem:]]
    held = sum(4 * math.prod(o) for o in shapes)
    return pl.pallas_call(
        kernel,
        out_shape=[jax.ShapeDtypeStruct(o, F32) for o in outs],
        in_specs=specs,
        out_specs=[pl.BlockSpec(memory_space=pltpu.VMEM)] * len(outs),
        scratch_shapes=[pltpu.VMEM(o, F32) for o in scratch],
        compiler_params=pltpu.CompilerParams(vmem_limit_bytes=min(held * 3 // 2 + (4 << 20), 60 << 20)),
        interpret=INTERPRET,
    )(*args)


def repeat(g, n, body):
    if g.ns <= 4:
        for i in range(n):
            body(i)
    else:
        lax.fori_loop(0, n, lambda i, carry: (body(i), carry)[1], 0)


def pack_kernel(g, idx, near, *outs):
    s = idx[0]
    lane_pick = chosen(iota((g.NY, g.NYl), 0) // 4 == iota((g.NY, g.NYl), 1))
    row_pick = chosen(iota((g.nxl, g.nx), 1) // 4 == iota((g.nxl, g.nx), 0), 1.0 / 64.0)
    base = g.nz * g.nx
    first, second = outs[: g.ns], outs[g.ns :]
    turns = []
    for k in range(g.ns):
        first[k][base:, :] = jnp.zeros((g.rows_1st - base, g.WY), F32)
        partner = lax.rem(s - k + g.ns, g.ns)
        turns.append(lax.rem(g.NY - g.start(partner), g.NY))
    for a, (group, at_a) in enumerate(((first, 0), (second, 0), (second, 1))):
        arr = near.at[a]
        for k in range(g.ns):

            def row(z, at_a=at_a, k=k, arr=arr, group=group):
                at = (at_a * g.nz + z) * g.nx
                if not isinstance(at, int):
                    at = pl.multiple_of(at, 8)
                v = pltpu.roll(arr[z], turns[k], 1)[:, : g.WY]
                group[k][pl.ds(at, g.nx), :] = v

            repeat(g, g.nz, row)
        for zl in range(g.nz // 4):
            col = arr[4 * zl] + arr[4 * zl + 1] + arr[4 * zl + 2] + arr[4 * zl + 3]
            low = gathered(row_pick, spread(col, lane_pick))
            at = base + a * g.lowrows + zl * g.nxl
            for k in range(g.ns):
                first[k][at : at + g.nxl, : g.NYl] = low


def pair_sums(src, planes, nz):
    n = planes * nz // 2
    lanes = src.shape[0] * 128
    v = blocks(src, pl.ds(0, n, stride=2)) + blocks(src, pl.ds(1, n, stride=2))
    v = v.reshape(planes // 2, 2, nz // 2, lanes)
    return (v[:, 0] + v[:, 1]).reshape(planes // 2 * (nz // 2), lanes)


def to_mid(v, scale):
    half = (v.shape[1], v.shape[1] // 2)
    return spread(v, chosen(iota(half, 0) // 2 == iota(half, 1), scale / 8.0))


def assemble_kernel(g, count, idx, *refs):
    s = idx[0]
    recv, refs = refs[: g.ns], refs[g.ns :]
    f_out, m_out, to_left, to_right = refs[:4]
    l_out, fs = refs[4] if count == 1 else None, refs[-1]
    base = count * g.nz * g.nx
    for j in range(g.ns):
        src = lax.rem(s + j, g.ns)
        for a in range(count):

            def row(z, a=a, j=j, src=src):
                at = (a * g.nz + z) * g.nx
                if not isinstance(at, int):
                    at = pl.multiple_of(at, 8)
                rows = pl.ds(src * g.nz + z, g.nx, stride=g.NZ)
                put_blocks(fs.at[a], rows, recv[j][pl.ds(at, g.nx), :])

            repeat(g, g.nz, row)
        for i in range(3 if count == 1 else 0):
            for zl in range(g.nz // 4):
                at = base + i * g.lowrows + zl * g.nxl
                for x in range(g.nxl):
                    l_out[i, pl.ds(x * g.NZl + src * (g.nz // 4) + zl, 1), :] = recv[j][
                        at + x : at + x + 1, : g.NYl
                    ]
    nxz = g.nx * g.NZ
    at, n = 0, XH * g.NZ
    for a in range(count):
        f_out[a] = blocks(fs.at[a], slice(0, nxz))
        m_out[a] = to_mid(pair_sums(fs.at[a], g.nx, g.NZ), 1.0)
        for b in range(g.WY // 128):
            to_left[at : at + n, :] = fs[a, b, 0:n, :]
            to_right[at : at + n, :] = fs[a, b, nxz - n :, :]
            at += n
    n, total = MH * g.NZm, g.nxm * g.NZm
    for a in range(count):
        for y in range(0, g.WYm, 128):
            to_left[at : at + n, :] = m_out[a, 0:n, y : y + 128]
            to_right[at : at + n, :] = m_out[a, total - n :, y : y + 128]
            at += n
    n = g.nxl * g.NZl
    for i in range(3 if count == 1 else 0):
        for y in range(0, g.NYl, 128):
            to_left[at : at + n, :] = l_out[i, :, y : y + 128]
            to_right[at : at + n, :] = l_out[i, :, y : y + 128]
            at += n


def edge_rows(g, count):
    rows = count * XH * g.NZ * (g.WY // 128) + count * MH * g.NZm * (g.WYm // 128)
    return rows + (3 * g.nxl * g.NZl * (g.NYl // 128) if count == 1 else 0)


def coefficients(b, c, q):
    diag = c * c + q
    inv = 1.0 / diag
    scaled = (27.0 / 26.0 * (c * c) + q) * inv
    return diag, inv, scaled, c * inv / 26.0


def coarse_smooth(g, idx, tab, mid, low):
    for level, (gi, c, D, K, y, d, t) in ((1, mid), (2, low)):
        y[...] = gi[...] * tab[level, 0]
        d[...] = y[...]

    def turn(j, carry):
        for nz, (gi, c, D, K, y, d, t) in ((g.NZm, mid), (g.NZl, low)):
            rows = c.shape[0]
            t[nz : nz + rows, :] = zy_sum(c[...] * y[...], nz)
        for level, nz, (gi, c, D, K, y, d, t) in ((1, g.NZm, mid), (2, g.NZl, low)):
            rows = c.shape[0]
            box = t[0:rows, :] + t[nz : nz + rows, :] + t[2 * nz : 2 * nz + rows, :]
            e = gi[...] - D[...] * y[...] + K[...] * box
            nd = tab[level, j] * d[...] + tab[level, MAXDEG + j] * e
            d[...] = nd
            y[...] = y[...] + nd
        return carry

    lax.fori_loop(1, jnp.maximum(idx[3], idx[4]), turn, 0)


def small_sweep(tab, j, grids):
    for level, nz, (gi, c, D, K, y, d, t) in grids:
        rows = c.shape[0]
        t[nz : nz + rows, :] = zy_sum(c[...] * y[...], nz)
    for level, nz, (gi, c, D, K, y, d, t) in grids:
        rows = c.shape[0]
        box = t[0:rows, :] + t[nz : nz + rows, :] + t[2 * nz : 2 * nz + rows, :]
        e = gi[...] - D[...] * y[...] + K[...] * box
        nd = tab[level, j] * d[...] + tab[level, MAXDEG + j] * e
        d[...] = nd
        y[...] = y[...] + nd


def all_sweeps(g, idx, tab, gi_at, fine, mid, low, zd):
    _, c, D, K, y, d, _ = fine
    nz = g.NZ
    grids = ((1, g.NZm, mid), (2, g.NZl, low))
    for level, _, (gi, _, _, _, ys, ds, _) in grids:
        ys[...] = gi[...] * tab[level, 0]
        ds[...] = ys[...]

    def rows(p):
        return slice((OUT + p) * nz, (OUT + p + 1) * nz)

    def fine_sweep(j):
        alpha, beta = tab[0, j], tab[0, MAXDEG + j]
        reach = MAXDEG - j
        first, last = -reach - 1, g.nx + reach
        held, sums = {}, {}
        for p in range(first, last + 1):
            held[p] = gi_at(p) * tab[0, 0] if j == 1 else y[rows(p), :]
            sums[p] = zy_sum(c[rows(p), :] * held[p], nz)
            q = p - 1
            if q <= first:
                continue
            r = rows(q)
            box = sums[q - 1] + sums[q] + sums[p]
            e = gi_at(q) - D[r, :] * held[q] + K[r, :] * box
            nd = alpha * (held[q] if j == 1 else d[r, :]) + beta * e
            if j < MAXDEG - 1:
                d[r, :] = nd
            y[r, :] = held[q] + nd

    ahead = {j: () for j in range(1, MAXDEG)}
    ahead[1], ahead[2], ahead[3] = (1, 2), (3, 4), (5,)

    def beside(j):
        for k in ahead[j]:
            small_sweep(tab, k, grids)
        if j == 4:
            coarse_correction(g, idx[0], mid[4], low[4], zd)

    fine_sweep(1)
    beside(1)
    for j in range(2, MAXDEG):

        @pl.when(j < idx[2])
        def _(j=j):
            fine_sweep(j)
            beside(j)

        if j < 5:

            @pl.when(j >= idx[2])
            def _(j=j):
                beside(j)


def fine_smooth(g, idx, tab, gi, c, D, K, y, d, t):
    n = g.CH * g.NZ
    side, own = OUT // g.CH, g.nx // g.CH
    y[...] = gi[...] * tab[0, 0]
    d[...] = y[...]

    def turn(j, carry):
        radius = idx[2] - j
        ht = (radius + 1 + g.CH - 1) // g.CH
        h = (radius + g.CH - 1) // g.CH
        fine_boxes(g, side - ht, side + own + ht, c, y, t)

        def chunk(k, inner_carry):
            r = pl.ds(pl.multiple_of(k * n, n), n)
            old = y[r, :]
            e = gi[r, :] - D[r, :] * old + K[r, :] * box_at(g, t, k)
            nd = tab[0, j] * d[r, :] + tab[0, MAXDEG + j] * e
            d[r, :] = nd
            y[r, :] = old + nd
            return inner_carry

        lax.fori_loop(side - h, side + own + h, chunk, 0)
        return carry

    lax.fori_loop(1, idx[2], turn, 0)


def clear_box_edges(g, t, tm, tl):
    for ref, nz in ((t, g.NZ), (tm, g.NZm), (tl, g.NZl)):
        zeros = jnp.zeros((nz, ref.shape[1]), F32)
        ref[0:nz, :] = zeros
        ref[ref.shape[0] - nz :, :] = zeros


def fine_boxes(g, first, last, c, x, t):
    n = g.CH * g.NZ

    def turn(k, carry):
        r = pl.ds(pl.multiple_of(k * n, n), n)
        t[pl.ds(pl.multiple_of(g.NZ + k * n, g.NZ), n), :] = zy_sum(c[r, :] * x[r, :], g.NZ)
        return carry

    lax.fori_loop(first, last, turn, 0)


def box_at(g, t, k):
    n = g.CH * g.NZ
    parts = [t[pl.ds(pl.multiple_of(k * n + o * g.NZ, g.NZ), n), :] for o in range(3)]
    return parts[0] + parts[1] + parts[2]


def coarse_correction(g, s, ym, yl, zd):
    planes = g.nxm + 2
    shape = (g.WYm, g.WY)
    mid_lanes = chosen(iota(shape, 0) == iota(shape, 1) // 2)
    shape = (g.NYl, g.WY)
    low_lanes = chosen(iota(shape, 0) == g.start(s) // 4 + iota(shape, 1) // 4)
    first = (MH - 1) * g.NZm
    mid = spread(ym[first : first + planes * g.NZm, :], mid_lanes)
    low = spread(yl[...], low_lanes)
    shape = (planes * g.NZm, g.PL * g.NZl)
    row, col = iota(shape, 0), iota(shape, 1)
    plane = row // g.NZm + (2 * LH - 1)
    want = (plane // 2) * g.NZl + (row % g.NZm) // 2
    v = mid + gathered(chosen(col == want), low)
    n = planes * g.NZm
    put_blocks(zd, pl.ds(0, n, stride=2), v)
    put_blocks(zd, pl.ds(1, n, stride=2), v)


def doubled(g, zd, plane, planes):
    at = (plane + 2) // 2 * g.NZ
    if planes == 1:
        return blocks(zd, slice(at, at + g.NZ))
    v = blocks(zd, slice(at, at + planes // 2 * g.NZ)).reshape(planes // 2, 1, g.NZ, g.WY)
    v = jnp.broadcast_to(v, (planes // 2, 2, g.NZ, g.WY))
    return v.reshape(planes * g.NZ, g.WY)


def pieces(g):
    return [(-1, 1)] + [(p, g.CH) for p in range(0, g.nx, g.CH)] + [(g.nx, 1)]


def cycle(g, idx, tab, gi_at, fine, mid, low, x_old, x, bi, diag, zd, keep, xb=None):
    _, c, D, K, y, _, t = fine
    if g.unrolled:
        all_sweeps(g, idx, tab, gi_at, fine, mid, low, zd)
    else:
        fine_smooth(g, idx, tab, *fine)
        coarse_smooth(g, idx, tab, mid, low)
        coarse_correction(g, idx[0], mid[4], low[4], zd)
    for p, planes in pieces(g):
        n = planes * g.NZ
        rr = slice((OUT + p) * g.NZ, (OUT + p) * g.NZ + n)
        r = slice((1 + p) * g.NZ, (1 + p) * g.NZ + n)
        v = 0.5 * (y[rr, :] + doubled(g, zd, p, planes))
        if x_old is not None:
            v = x_old[r, :] + v
        x[r, :] = v
        if xb is not None and planes == g.CH and 0 <= p < g.nx:
            put_blocks(xb, slice(p * g.NZ, p * g.NZ + n), v)
        t[r, :] = zy_sum(c[rr, :] * v, g.NZ)
    step = g.CH * g.NZ
    for p in range(0, g.nx, g.CH):
        at = p * g.NZ
        box = (
            t[at : at + step, :]
            + t[at + g.NZ : at + g.NZ + step, :]
            + t[at + 2 * g.NZ : at + 2 * g.NZ + step, :]
        )
        r = slice(at, at + step)
        rr = slice(OUT * g.NZ + at, OUT * g.NZ + at + step)
        v = bi[r, :] - D[rr, :] * x[at + g.NZ : at + g.NZ + step, :] + K[rr, :] * box
        keep(r, v, v * diag[r, :])


def send_defect(g, s, gi, rm, rl, res, to_l, to_r, to_l2, to_r2):
    sums = pair_sums(res, g.nx, g.NZ)
    rm[...] = to_mid(sums, 4.0)
    shape = (g.nxl * g.NZl, g.nxm * g.NZm)
    row, col = iota(shape, 0), iota(shape, 1)
    same_x = col // (2 * g.NZm) == row // g.NZl
    same_z = (col % g.NZm) // 2 == row % g.NZl
    rows = chosen(same_x & same_z, 0.25)
    shape = (g.WY, g.NYl)
    lanes = chosen(iota(shape, 0) // 4 + g.start(s) // 4 == iota(shape, 1))
    rl[...] = spread(gathered(rows, sums), lanes)
    at = 0
    for ref, n in ((gi, XH * g.NZ), (rm, MH * g.NZm), (rl, g.nxl * g.NZl)):
        total = ref.shape[0]
        for y in range(0, ref.shape[1], 128):
            to_l[at : at + n, :] = ref[0:n, y : y + 128]
            to_r[at : at + n, :] = ref[total - n :, y : y + 128]
            at += n
    far = (LH - g.nxl) * g.NZl
    total = rl.shape[0]
    for b in range(g.NYl // 128):
        lanes = slice(128 * b, 128 * b + 128)
        to_l2[b * far : b * far + far, :] = rl[0:far, lanes]
        to_r2[b * far : b * far + far, :] = rl[total - far :, lanes]


def first_kernel(g, idx, tab, *refs):
    f, m, l, f2nd, m2nd, from_l, from_r, from_l2nd, from_r2nd, from_l2, from_r2 = refs[:11]
    refs = refs[11:]
    (c, D, K, bi, diag, cm, Dm, Km, im, cl, Dl, Kl, il) = refs[:13]
    x, gi_own, rm, rl, to_l, to_r, to_l2, to_r2 = refs[13:21]
    (gi, y, d, t, gm, ym, dm, tm, gl, yl, dl, tl, zd, res) = refs[21:]
    s, li = idx[0], idx[1]
    clear_box_edges(g, t, tm, tl)
    fill = (0.0, 0.0, 1.0)

    def kept(ok, v, a):
        return jnp.where(ok, v, fill[a])

    n = XH * g.NZ
    lo, hi = OUT * g.NZ, (OUT + g.nx) * g.NZ
    at = {0: 0, 1: 0}
    region = (gi, c, y)
    for a in range(3):
        left, right = (from_l2nd, from_r2nd) if a else (from_l, from_r)
        q = min(a, 1)
        region[a][0 : lo - n, :] = jnp.full((lo - n, g.WY), fill[a], F32)
        region[a][hi + n :, :] = jnp.full((lo - n, g.WY), fill[a], F32)
        region[a][lo:hi, :] = f2nd[a - 1] if a else f[0]
        for yy in range(0, g.WY, 128):
            rows = slice(at[q], at[q] + n)
            region[a][lo - n : lo, yy : yy + 128] = kept(li > 0, left[rows, :], a)
            region[a][hi : hi + n, yy : yy + 128] = kept(
                li < g.nl - 1, right[rows, :], a
            )
            at[q] += n
    step = g.CH * g.NZ

    def build(k, carry):
        r = pl.ds(pl.multiple_of(k * step, step), step)
        b0 = gi[r, :]
        dg, inv, sc, kk = coefficients(b0, c[r, :], y[r, :])
        gi[r, :] = b0 * inv
        D[r, :] = sc
        K[r, :] = kk
        y[r, :] = dg
        return carry

    lax.fori_loop(0, g.PF // g.CH, build, 0)
    bi[...] = gi[lo:hi, :]
    diag[...] = y[lo:hi, :]

    n = MH * g.NZm
    parts = []
    for a in range(3):
        halves = []
        left, right = (from_l2nd, from_r2nd) if a else (from_l, from_r)
        q = min(a, 1)
        for _ in range(0, g.WYm, 128):
            rows = slice(at[q], at[q] + n)
            halves.append(
                (kept(li > 0, left[rows, :], a), kept(li < g.nl - 1, right[rows, :], a))
            )
            at[q] += n
        left = jnp.concatenate([v[0] for v in halves], axis=1)
        right = jnp.concatenate([v[1] for v in halves], axis=1)
        own_mid = m2nd[a - 1] if a else m[0]
        parts.append(jnp.concatenate([left, own_mid, right], axis=0))
    _, inv, sc, kk = coefficients(*parts)
    cm[...] = parts[1]
    Dm[...] = sc
    Km[...] = kk
    im[...] = inv
    gm[...] = 4.0 * parts[0] * inv

    n = g.nxl * g.NZl
    far = (LH - g.nxl) * g.NZl
    store = (gl, cl, il)
    at, at2 = at[0], 0
    for a in range(3):
        for yy in range(0, g.NYl, 128):
            lanes = slice(yy, yy + 128)
            ref = store[a]
            ref[0:far, lanes] = kept(li > 1, from_l2[at2 : at2 + far, :], a)
            ref[far : far + n, lanes] = kept(li > 0, from_l[at : at + n, :], a)
            ref[far + n : far + 2 * n, lanes] = l[a, :, lanes]
            ref[far + 2 * n : far + 3 * n, lanes] = kept(
                li < g.nl - 1, from_r[at : at + n, :], a
            )
            ref[far + 3 * n :, lanes] = kept(li < g.nl - 2, from_r2[at2 : at2 + far, :], a)
            at += n
            at2 += far
    _, inv, sc, kk = coefficients(gl[...], cl[...], il[...])
    Dl[...] = sc
    Kl[...] = kk
    il[...] = inv
    gl[...] = 16.0 * gl[...] * inv

    def keep(r, scaled, plain):
        gi_own[r, :] = scaled
        put_blocks(res, r, plain)

    fine = (gi, c, D, K, y, d, t)
    mid = (gm, cm, Dm, Km, ym, dm, tm)
    low = (gl, cl, Dl, Kl, yl, dl, tl)

    def gi_at(p):
        return gi[(OUT + p) * g.NZ : (OUT + p + 1) * g.NZ, :]

    cycle(g, idx, tab, gi_at, fine, mid, low, None, x, bi, diag, zd, keep)
    send_defect(g, s, gi_own, rm, rl, res, to_l, to_r, to_l2, to_r2)


def gather_defect(g, gi_own, rm, rl, from_l, from_r, from_l2, from_r2, gi, gm, im, gl, il):
    lo, hi = OUT * g.NZ, (OUT + g.nx) * g.NZ
    n = XH * g.NZ
    at = 0 if not g.unrolled else g.WY // 128 * n
    if not g.unrolled:
        zeros = jnp.zeros((lo - n, g.WY), F32)
        gi[0 : lo - n, :] = zeros
        gi[hi + n :, :] = zeros
        gi[lo:hi, :] = gi_own[...]
        for y in range(0, g.WY, 128):
            gi[lo - n : lo, y : y + 128] = from_l[at : at + n, :]
            gi[hi : hi + n, y : y + 128] = from_r[at : at + n, :]
            at += n
    n, own = MH * g.NZm, rm.shape[0]
    for y in range(0, g.WYm, 128):
        lanes = slice(y, y + 128)
        gm[0:n, lanes] = from_l[at : at + n, :] * im[0:n, lanes]
        gm[n + own :, lanes] = from_r[at : at + n, :] * im[n + own :, lanes]
        at += n
    gm[n : n + own, :] = rm[...] * im[n : n + own, :]
    n = g.nxl * g.NZl
    far = (LH - g.nxl) * g.NZl
    for b in range(g.NYl // 128):
        lanes = slice(128 * b, 128 * b + 128)
        rows = slice(b * far, b * far + far)
        gl[0:far, lanes] = from_l2[rows, :]
        gl[far : far + n, lanes] = from_l[at : at + n, :]
        gl[far + n : far + 2 * n, lanes] = rl[:, lanes]
        gl[far + 2 * n : far + 3 * n, lanes] = from_r[at : at + n, :]
        gl[far + 3 * n :, lanes] = from_r2[rows, :]
        at += n
    gl[...] = gl[...] * il[...]


def cycle_kernel(g, n_outs, idx, tab, *refs):
    gi_own, rm, rl, x_old = refs[:4]
    received = refs[4:8]
    (c, D, K, bi, diag, cm, Dm, Km, im, cl, Dl, Kl, il) = refs[8:21]
    outs = refs[21 : 21 + n_outs]
    scr = refs[21 + n_outs :]
    (gi, y, d, t, gm, ym, dm, tm, gl, yl, dl, tl, zd, res) = scr[:14]
    clear_box_edges(g, t, tm, tl)
    gather_defect(g, gi_own, rm, rl, *received, gi, gm, im, gl, il)
    fine = (gi, c, D, K, y, d, t)
    mid = (gm, cm, Dm, Km, ym, dm, tm)
    low = (gl, cl, Dl, Kl, yl, dl, tl)
    s = idx[0]

    def gi_at(p):
        if 0 <= p < g.nx:
            return gi_own[p * g.NZ : (p + 1) * g.NZ, :]
        part = received[0] if p < 0 else received[1]
        at = (p + XH if p < 0 else p - g.nx) * g.NZ
        step = XH * g.NZ
        return jnp.concatenate(
            [part[at + b * step : at + b * step + g.NZ, :] for b in range(g.WY // 128)],
            axis=1,
        )

    if len(scr) == 14:
        x, gi_new, rm_new, rl_new = outs[:4]

        def keep(r, scaled, plain):
            gi_new[r, :] = scaled
            put_blocks(res, r, plain)

        cycle(g, idx, tab, gi_at, fine, mid, low, x_old, x, bi, diag, zd, keep)
        send_defect(g, s, gi_new, rm_new, rl_new, res, *outs[4:])
        return
    x, xb = scr[14:]

    def keep_plain(r, scaled, plain):
        put_blocks(res, r, plain)

    cycle(g, idx, tab, gi_at, fine, mid, low, x_old, x, bi, diag, zd, keep_plain, xb)
    shift = lax.rem(g.WY - (s * g.ny - g.start(s)), g.WY)
    for k in range(g.ns):
        partner = lax.rem(s - k + g.ns, g.ns)
        for o, ref in enumerate((xb, res)):

            def row(z, o=o, ref=ref, k=k, partner=partner):
                v = blocks(ref, pl.ds(partner * g.nz + z, g.nx, stride=g.NZ))
                at = (o * g.nz + z) * g.nx
                if not isinstance(at, int):
                    at = pl.multiple_of(at, 8)
                outs[k][pl.ds(at, g.nx), :] = pltpu.roll(v, shift, 1)[:, : g.PW]

            repeat(g, g.nz, row)


def unpack_kernel(g, idx, *refs):
    s = idx[0]
    recv, outs = refs[: g.ns], refs[g.ns :]
    for o in range(2):
        for z in range(g.nz):
            at = (o * g.nz + z) * g.nx
            total = None
            if g.ny % 128 == 0:
                wide = jnp.concatenate(
                    [recv[j][at : at + g.nx, : g.ny] for j in range(g.ns)], axis=1
                )
                total = pltpu.roll(wide, s * g.ny, 1)
            else:
                mine = iota((g.nx, g.NY), 1) < g.ny
                for j in range(g.ns):
                    src = lax.rem(s + j, g.ns)
                    v = recv[j][at : at + g.nx, :]
                    pad = jnp.zeros((g.nx, g.NY - g.PW), F32)
                    v = jnp.where(mine, jnp.concatenate([v, pad], axis=1), 0.0)
                    v = pltpu.roll(v, src * g.ny, 1)
                    total = v if total is None else total + v
            outs[o][z] = total


def ring(value, axis, by):
    peers = lax.axis_size(axis)
    if by % peers == 0:
        return value
    return lax.ppermute(value, axis, [(i, (i - by) % peers) for i in range(peers)])


def sweep_tables(degrees, lower, upper):
    centre = (upper + lower) * 0.5
    radius = (upper - lower) * 0.5
    ratio = centre / radius
    rho = 1.0 / ratio
    alphas, betas = [], []
    for j in range(1, MAXDEG):
        new = 1.0 / (2.0 * ratio - rho)
        active = j < degrees
        alphas.append(jnp.where(active, new * rho, 0.0))
        betas.append(jnp.where(active, 2.0 * new / radius, 0.0))
        rho = new
    zero = jnp.zeros_like(rho)
    return jnp.stack([1.0 / centre] + alphas + [zero] + betas, axis=1)


def shards(right_side, scale_field, mass_field, degrees, lower_bound, upper_bound):
    g = Geometry(right_side.shape, lax.axis_size("slab"), lax.axis_size("level"))
    place = jnp.stack([lax.axis_index("slab"), lax.axis_index("level")])
    place = place.astype(jnp.int32)
    idx = jnp.concatenate([place, degrees])
    tab = sweep_tables(degrees, lower_bound, upper_bound)

    def call(kernel, outs, scratch, smem, *args):
        return vmem_call(lambda *refs: kernel(g, *refs), outs, scratch, smem, args)

    shape = right_side.shape
    packs = call(
        pack_kernel, [(g.rows_1st, g.WY)] * g.ns + [(g.rows_2nd, g.WY)] * g.ns, [], 1,
        place, jnp.stack([right_side, scale_field, mass_field]),
    )
    packs_1st, packs_2nd = [], []
    for k in range(g.ns):
        packs_1st.append(ring(packs[k], "slab", k))
    for k in range(g.ns):
        packs_2nd.append(ring(packs[g.ns + k], "slab", k))

    fine = (g.PF * g.NZ, g.WY)
    own = (g.nx * g.NZ, g.WY)
    mid = (g.PM * g.NZm, g.WYm)
    low = (g.PL * g.NZl, g.NYl)
    own_blocks = (g.WY // 128, own[0], 128)
    scratch = [
        fine, fine, fine, (fine[0] + 2 * g.NZ, g.WY),
        mid, mid, mid, (mid[0] + 2 * g.NZm, g.WYm),
        low, low, low, (low[0] + 2 * g.NZl, g.NYl),
        (g.WY // 128, (g.nxm + 2) * g.NZ, 128), own_blocks,
    ]

    def assemble(count, packs):
        outs = [
            (count, *own), (count, g.nxm * g.NZm, g.WYm),
            (edge_rows(g, count), 128), (edge_rows(g, count), 128),
        ] + [(3, g.nxl * g.NZl, g.NYl)] * (count == 1)
        return vmem_call(
            lambda *refs: assemble_kernel(g, count, *refs),
            outs, [(count, *own_blocks)], 1, (place, *packs),
        )

    f, m, to_left, to_right, l = assemble(1, packs_1st)
    far = (LH - g.nxl) * g.NZl
    lanes = g.NYl // 128

    def far_rows(part):
        parts = part.reshape(3, part.shape[1], lanes, 128)
        return parts.transpose(0, 2, 1, 3).reshape(3 * lanes * far, 128)

    from_l = ring(to_right, "level", -1)
    from_r = ring(to_left, "level", 1)
    from_l2 = ring(far_rows(l[:, l.shape[1] - far :]), "level", -2)
    from_r2 = ring(far_rows(l[:, :far]), "level", 2)

    f2nd, m2nd, to_left, to_right = assemble(2, packs_2nd)
    from_l2nd = ring(to_right, "level", -1)
    from_r2nd = ring(to_left, "level", 1)

    x_shape = ((g.nx + 2) * g.NZ, g.WY)
    rm_shape, rl_shape = (g.nxm * g.NZm, g.WYm), (g.nxl * g.NZl, g.NYl)
    sent = (
        XH * g.NZ * (g.WY // 128) + MH * g.NZm * (g.WYm // 128) + rl_shape[0] * lanes,
        128,
    )
    sent2 = (lanes * far, 128)
    state = [x_shape, own, rm_shape, rl_shape, sent, sent, sent2, sent2]
    outs = call(
        first_kernel, [fine] * 3 + [own] * 2 + [mid] * 4 + [low] * 4 + state, scratch, 2,
        idx, tab, f, m, l, f2nd, m2nd,
        from_l, from_r, from_l2nd, from_r2nd, from_l2, from_r2,
    )
    coefs, outs = outs[:13], outs[13:]
    for cycle_no in range(1, CYCLES):
        x, gi, rm, rl, to_l, to_r, to_l2, to_r2 = outs
        received = (
            ring(to_r, "level", -1),
            ring(to_l, "level", 1),
            ring(to_r2, "level", -2),
            ring(to_l2, "level", 2),
        )
        if cycle_no < CYCLES - 1:
            shapes, more = state, []
        else:
            shapes, more = [(2 * g.nz * g.nx, g.PW)] * g.ns, [x_shape, own_blocks]
        outs = vmem_call(
            lambda *refs, n=len(shapes): cycle_kernel(g, n, *refs),
            shapes, scratch + more, 2,
            (idx, tab, gi, rm, rl, x, *received, *coefs),
        )
    packs = []
    for k, v in enumerate(outs):
        packs.append(ring(v, "slab", k))
    return tuple(call(unpack_kernel, [shape, shape], [], 1, place, *packs))


def solution(mesh):
    spread = P("slab", "level", None)
    return jax.shard_map(
        shards,
        mesh=mesh,
        in_specs=(spread, spread, spread, P(), P(), P()),
        out_specs=(spread, spread),
        check_vma=False,
    )
```

```python
import math

import jax
import jax.numpy as jnp
from jax import lax
from jax.experimental import pallas as pl
from jax.experimental.pallas import tpu as pltpu
from jax.sharding import PartitionSpec as P


CYCLES = 3
MAXDEG = 6
INTERPRET = False

F32 = jnp.float32
OUT = 8
XH = 6
MH = 6
LH = 6
YH = 64


def blocks(ref, rows):
    return jnp.concatenate([ref[b, rows, :] for b in range(ref.shape[0])], axis=1)


def put_blocks(ref, rows, value):
    for b in range(ref.shape[0]):
        ref[b, rows, :] = value[:, 128 * b : 128 * b + 128]


def thirds(v):
    high = v.astype(jnp.bfloat16)
    rest = v - high.astype(F32)
    mid = rest.astype(jnp.bfloat16)
    return high, mid, (rest - mid.astype(F32)).astype(jnp.bfloat16)


def spread(v, pick):
    parts = [jnp.dot(p, pick, preferred_element_type=F32) for p in thirds(v)]
    return parts[0] + (parts[1] + parts[2])


def gathered(pick, v):
    parts = [jnp.dot(pick, p, preferred_element_type=F32) for p in thirds(v)]
    return parts[0] + (parts[1] + parts[2])


def chosen(test, value=1.0):
    return jnp.where(test, value, 0.0).astype(F32).astype(jnp.bfloat16)


def iota(shape, dim):
    return lax.broadcasted_iota(jnp.int32, shape, dim)


def zy_sum(w, nz):
    rows, lanes = w.shape
    if nz % 8 == 0:
        v = w.reshape(rows // nz, nz // 8, 8, lanes)
        at = iota(v.shape, 2)
        edge = jnp.zeros_like(v[:, :1])
        up = pltpu.roll(w.reshape(rows // 8, 8, lanes), 1, 1).reshape(v.shape)
        down = pltpu.roll(w.reshape(rows // 8, 8, lanes), 7, 1).reshape(v.shape)
        up_over = down_over = edge
        if nz > 8:
            up_over = jnp.concatenate([edge, up[:, :-1]], axis=1)
            down_over = jnp.concatenate([down[:, 1:], edge], axis=1)
        s = v + jnp.where(at == 0, up_over, up) + jnp.where(at == 7, down_over, down)
        s = s.reshape(rows, lanes)
    else:
        at = iota(w.shape, 0) & (nz - 1)
        up = jnp.where(at == 0, 0.0, pltpu.roll(w, 1, 0))
        down = jnp.where(at == nz - 1, 0.0, pltpu.roll(w, rows - 1, 0))
        s = w + up + down
    at = iota((rows, 128), 1)
    n = lanes // 128
    part = [s[:, 128 * b : 128 * b + 128] for b in range(n)]
    left = [pltpu.roll(p, 1, 1) for p in part]
    right = [pltpu.roll(p, 127, 1) for p in part]
    out = []
    for b in range(n):
        before = left[b - 1] if b else 0.0
        after = right[b + 1] if b < n - 1 else 0.0
        out.append(
            part[b] + jnp.where(at == 0, before, left[b]) + jnp.where(at == 127, after, right[b])
        )
    return jnp.concatenate(out, axis=1)


class Geometry:
    def __init__(self, shape, ns, nl):
        self.nz, self.nx, self.NY = shape
        self.ns, self.nl = ns, nl
        self.NZ = self.nz * ns
        self.ny = self.NY // ns
        self.WY = min(self.NY, -(-(self.ny + 2 * YH) // 128) * 128)
        self.PW = -(-self.ny // 128) * 128
        self.nxm, self.nxl = self.nx // 2, self.nx // 4
        self.NZm, self.NZl = self.NZ // 2, self.NZ // 4
        self.WYm, self.NYm, self.NYl = self.WY // 2, self.NY // 2, self.NY // 4
        self.CH = max(1, min(4, 64 // self.NZ))
        self.unrolled = self.NZ <= 16
        self.PF = self.nx + 2 * OUT
        self.PM = self.nxm + 2 * MH
        self.PL = self.nxl + 2 * LH
        assert self.nx % self.CH == 0 and OUT % self.CH == 0 and XH <= self.nx
        assert self.nxl < LH <= 2 * self.nxl and MH <= self.nxm
        assert (self.nxl * self.nz // 4) % 4 == 0 and self.WYm % 128 == 0 and self.NYl % 128 == 0
        self.lowrows = self.nxl * (self.nz // 4)
        self.rows_1st = self.nz * self.nx + -(-3 * self.lowrows // 8) * 8
        self.rows_2nd = 2 * self.nz * self.nx

    def start(self, s):
        return jnp.clip(s * self.ny - (self.WY - self.ny) // 2, 0, self.NY - self.WY)


def vmem_call(kernel, outs, scratch, smem, args):
    specs = [pl.BlockSpec(memory_space=pltpu.SMEM)] * smem
    specs += [pl.BlockSpec(memory_space=pltpu.VMEM)] * (len(args) - smem)
    shapes = list(outs) + list(scratch) + [a.shape for a in args[smem:]]
    held = sum(4 * math.prod(o) for o in shapes)
    return pl.pallas_call(
        kernel,
        out_shape=[jax.ShapeDtypeStruct(o, F32) for o in outs],
        in_specs=specs,
        out_specs=[pl.BlockSpec(memory_space=pltpu.VMEM)] * len(outs),
        scratch_shapes=[pltpu.VMEM(o, F32) for o in scratch],
        compiler_params=pltpu.CompilerParams(vmem_limit_bytes=min(held * 3 // 2 + (4 << 20), 60 << 20)),
        interpret=INTERPRET,
    )(*args)


def repeat(g, n, body):
    if g.ns <= 4:
        for i in range(n):
            body(i)
    else:
        lax.fori_loop(0, n, lambda i, carry: (body(i), carry)[1], 0)


def pack_kernel(g, idx, near, *outs):
    s = idx[0]
    lane_pick = chosen(iota((g.NY, g.NYl), 0) // 4 == iota((g.NY, g.NYl), 1))
    row_pick = chosen(iota((g.nxl, g.nx), 1) // 4 == iota((g.nxl, g.nx), 0), 1.0 / 64.0)
    base = g.nz * g.nx
    first, second = outs[: g.ns], outs[g.ns :]
    turns = []
    for k in range(g.ns):
        first[k][base:, :] = jnp.zeros((g.rows_1st - base, g.WY), F32)
        partner = lax.rem(s - k + g.ns, g.ns)
        turns.append(lax.rem(g.NY - g.start(partner), g.NY))
    for a, (group, at_a) in enumerate(((first, 0), (second, 0), (second, 1))):
        arr = near.at[a]
        for k in range(g.ns):

            def row(z, at_a=at_a, k=k, arr=arr, group=group):
                at = (at_a * g.nz + z) * g.nx
                if not isinstance(at, int):
                    at = pl.multiple_of(at, 8)
                v = pltpu.roll(arr[z], turns[k], 1)[:, : g.WY]
                group[k][pl.ds(at, g.nx), :] = v

            repeat(g, g.nz, row)
        for zl in range(g.nz // 4):
            col = arr[4 * zl] + arr[4 * zl + 1] + arr[4 * zl + 2] + arr[4 * zl + 3]
            low = gathered(row_pick, spread(col, lane_pick))
            at = base + a * g.lowrows + zl * g.nxl
            for k in range(g.ns):
                first[k][at : at + g.nxl, : g.NYl] = low


def pair_sums(src, planes, nz):
    n = planes * nz // 2
    lanes = src.shape[0] * 128
    v = blocks(src, pl.ds(0, n, stride=2)) + blocks(src, pl.ds(1, n, stride=2))
    v = v.reshape(planes // 2, 2, nz // 2, lanes)
    return (v[:, 0] + v[:, 1]).reshape(planes // 2 * (nz // 2), lanes)


def to_mid(v, scale):
    half = (v.shape[1], v.shape[1] // 2)
    return spread(v, chosen(iota(half, 0) // 2 == iota(half, 1), scale / 8.0))


def assemble_kernel(g, count, idx, *refs):
    s = idx[0]
    recv, refs = refs[: g.ns], refs[g.ns :]
    f_out, m_out, to_left, to_right = refs[:4]
    l_out, fs = refs[4] if count == 1 else None, refs[-1]
    base = count * g.nz * g.nx
    for j in range(g.ns):
        src = lax.rem(s + j, g.ns)
        for a in range(count):

            def row(z, a=a, j=j, src=src):
                at = (a * g.nz + z) * g.nx
                if not isinstance(at, int):
                    at = pl.multiple_of(at, 8)
                rows = pl.ds(src * g.nz + z, g.nx, stride=g.NZ)
                put_blocks(fs.at[a], rows, recv[j][pl.ds(at, g.nx), :])

            repeat(g, g.nz, row)
        for i in range(3 if count == 1 else 0):
            for zl in range(g.nz // 4):
                at = base + i * g.lowrows + zl * g.nxl
                for x in range(g.nxl):
                    l_out[i, pl.ds(x * g.NZl + src * (g.nz // 4) + zl, 1), :] = recv[j][
                        at + x : at + x + 1, : g.NYl
                    ]
    nxz = g.nx * g.NZ
    at, n = 0, XH * g.NZ
    for a in range(count):
        f_out[a] = blocks(fs.at[a], slice(0, nxz))
        m_out[a] = to_mid(pair_sums(fs.at[a], g.nx, g.NZ), 1.0)
        for b in range(g.WY // 128):
            to_left[at : at + n, :] = fs[a, b, 0:n, :]
            to_right[at : at + n, :] = fs[a, b, nxz - n :, :]
            at += n
    n, total = MH * g.NZm, g.nxm * g.NZm
    for a in range(count):
        for y in range(0, g.WYm, 128):
            to_left[at : at + n, :] = m_out[a, 0:n, y : y + 128]
            to_right[at : at + n, :] = m_out[a, total - n :, y : y + 128]
            at += n
    n = g.nxl * g.NZl
    for i in range(3 if count == 1 else 0):
        for y in range(0, g.NYl, 128):
            to_left[at : at + n, :] = l_out[i, :, y : y + 128]
            to_right[at : at + n, :] = l_out[i, :, y : y + 128]
            at += n


def edge_rows(g, count):
    rows = count * XH * g.NZ * (g.WY // 128) + count * MH * g.NZm * (g.WYm // 128)
    return rows + (3 * g.nxl * g.NZl * (g.NYl // 128) if count == 1 else 0)


def coefficients(b, c, q):
    diag = c * c + q
    inv = 1.0 / diag
    scaled = (27.0 / 26.0 * (c * c) + q) * inv
    return diag, inv, scaled, c * inv / 26.0


def coarse_smooth(g, idx, tab, mid, low):
    for level, (gi, c, D, K, y, d, t) in ((1, mid), (2, low)):
        y[...] = gi[...] * tab[level, 0]
        d[...] = y[...]

    def turn(j, carry):
        for nz, (gi, c, D, K, y, d, t) in ((g.NZm, mid), (g.NZl, low)):
            rows = c.shape[0]
            t[nz : nz + rows, :] = zy_sum(c[...] * y[...], nz)
        for level, nz, (gi, c, D, K, y, d, t) in ((1, g.NZm, mid), (2, g.NZl, low)):
            rows = c.shape[0]
            box = t[0:rows, :] + t[nz : nz + rows, :] + t[2 * nz : 2 * nz + rows, :]
            e = gi[...] - D[...] * y[...] + K[...] * box
            nd = tab[level, j] * d[...] + tab[level, MAXDEG + j] * e
            d[...] = nd
            y[...] = y[...] + nd
        return carry

    lax.fori_loop(1, jnp.maximum(idx[3], idx[4]), turn, 0)


def small_sweep(tab, j, grids):
    for level, nz, (gi, c, D, K, y, d, t) in grids:
        rows = c.shape[0]
        t[nz : nz + rows, :] = zy_sum(c[...] * y[...], nz)
    for level, nz, (gi, c, D, K, y, d, t) in grids:
        rows = c.shape[0]
        box = t[0:rows, :] + t[nz : nz + rows, :] + t[2 * nz : 2 * nz + rows, :]
        e = gi[...] - D[...] * y[...] + K[...] * box
        nd = tab[level, j] * d[...] + tab[level, MAXDEG + j] * e
        d[...] = nd
        y[...] = y[...] + nd


def all_sweeps(g, idx, tab, gi_at, fine, mid, low, zd):
    _, c, D, K, y, d, _ = fine
    nz = g.NZ
    grids = ((1, g.NZm, mid), (2, g.NZl, low))
    for level, _, (gi, _, _, _, ys, ds, _) in grids:
        ys[...] = gi[...] * tab[level, 0]
        ds[...] = ys[...]

    def rows(p):
        return slice((OUT + p) * nz, (OUT + p + 1) * nz)

    def fine_sweep(j):
        alpha, beta = tab[0, j], tab[0, MAXDEG + j]
        reach = MAXDEG - j
        first, last = -reach - 1, g.nx + reach
        held, sums = {}, {}
        for p in range(first, last + 1):
            held[p] = gi_at(p) * tab[0, 0] if j == 1 else y[rows(p), :]
            sums[p] = zy_sum(c[rows(p), :] * held[p], nz)
            q = p - 1
            if q <= first:
                continue
            r = rows(q)
            box = sums[q - 1] + sums[q] + sums[p]
            e = gi_at(q) - D[r, :] * held[q] + K[r, :] * box
            nd = alpha * (held[q] if j == 1 else d[r, :]) + beta * e
            if j < MAXDEG - 1:
                d[r, :] = nd
            y[r, :] = held[q] + nd

    ahead = {j: () for j in range(1, MAXDEG)}
    ahead[1], ahead[2] = (1, 2), (3, 4, 5)

    def beside(j):
        for k in ahead[j]:
            small_sweep(tab, k, grids)
        if j == 3:
            coarse_correction(g, idx[0], mid[4], low[4], zd)

    fine_sweep(1)
    beside(1)
    for j in range(2, MAXDEG):

        @pl.when(j < idx[2])
        def _(j=j):
            fine_sweep(j)
            beside(j)

        if j < 4:

            @pl.when(j >= idx[2])
            def _(j=j):
                beside(j)


def fine_smooth(g, idx, tab, gi, c, D, K, y, d, t):
    n = g.CH * g.NZ
    side, own = OUT // g.CH, g.nx // g.CH
    y[...] = gi[...] * tab[0, 0]
    d[...] = y[...]

    def turn(j, carry):
        radius = idx[2] - j
        ht = (radius + 1 + g.CH - 1) // g.CH
        h = (radius + g.CH - 1) // g.CH
        fine_boxes(g, side - ht, side + own + ht, c, y, t)

        def chunk(k, inner_carry):
            r = pl.ds(pl.multiple_of(k * n, n), n)
            old = y[r, :]
            e = gi[r, :] - D[r, :] * old + K[r, :] * box_at(g, t, k)
            nd = tab[0, j] * d[r, :] + tab[0, MAXDEG + j] * e
            d[r, :] = nd
            y[r, :] = old + nd
            return inner_carry

        lax.fori_loop(side - h, side + own + h, chunk, 0)
        return carry

    lax.fori_loop(1, idx[2], turn, 0)


def clear_box_edges(g, t, tm, tl):
    for ref, nz in ((t, g.NZ), (tm, g.NZm), (tl, g.NZl)):
        zeros = jnp.zeros((nz, ref.shape[1]), F32)
        ref[0:nz, :] = zeros
        ref[ref.shape[0] - nz :, :] = zeros


def fine_boxes(g, first, last, c, x, t):
    n = g.CH * g.NZ

    def turn(k, carry):
        r = pl.ds(pl.multiple_of(k * n, n), n)
        t[pl.ds(pl.multiple_of(g.NZ + k * n, g.NZ), n), :] = zy_sum(c[r, :] * x[r, :], g.NZ)
        return carry

    lax.fori_loop(first, last, turn, 0)


def box_at(g, t, k):
    n = g.CH * g.NZ
    parts = [t[pl.ds(pl.multiple_of(k * n + o * g.NZ, g.NZ), n), :] for o in range(3)]
    return parts[0] + parts[1] + parts[2]


def coarse_correction(g, s, ym, yl, zd):
    planes = g.nxm + 2
    shape = (g.WYm, g.WY)
    mid_lanes = chosen(iota(shape, 0) == iota(shape, 1) // 2)
    shape = (g.NYl, g.WY)
    low_lanes = chosen(iota(shape, 0) == g.start(s) // 4 + iota(shape, 1) // 4)
    first = (MH - 1) * g.NZm
    mid = spread(ym[first : first + planes * g.NZm, :], mid_lanes)
    low = spread(yl[...], low_lanes)
    shape = (planes * g.NZm, g.PL * g.NZl)
    row, col = iota(shape, 0), iota(shape, 1)
    plane = row // g.NZm + (2 * LH - 1)
    want = (plane // 2) * g.NZl + (row % g.NZm) // 2
    v = mid + gathered(chosen(col == want), low)
    n = planes * g.NZm
    put_blocks(zd, pl.ds(0, n, stride=2), v)
    put_blocks(zd, pl.ds(1, n, stride=2), v)


def doubled(g, zd, plane, planes):
    at = (plane + 2) // 2 * g.NZ
    if planes == 1:
        return blocks(zd, slice(at, at + g.NZ))
    v = blocks(zd, slice(at, at + planes // 2 * g.NZ)).reshape(planes // 2, 1, g.NZ, g.WY)
    v = jnp.broadcast_to(v, (planes // 2, 2, g.NZ, g.WY))
    return v.reshape(planes * g.NZ, g.WY)


def pieces(g):
    return [(-1, 1)] + [(p, g.CH) for p in range(0, g.nx, g.CH)] + [(g.nx, 1)]


def cycle(g, idx, tab, gi_at, fine, mid, low, x_old, x, bi, diag, zd, keep, xb=None):
    _, c, D, K, y, _, t = fine
    if g.unrolled:
        all_sweeps(g, idx, tab, gi_at, fine, mid, low, zd)
    else:
        fine_smooth(g, idx, tab, *fine)
        coarse_smooth(g, idx, tab, mid, low)
        coarse_correction(g, idx[0], mid[4], low[4], zd)
    for p, planes in pieces(g):
        n = planes * g.NZ
        rr = slice((OUT + p) * g.NZ, (OUT + p) * g.NZ + n)
        r = slice((1 + p) * g.NZ, (1 + p) * g.NZ + n)
        v = 0.5 * (y[rr, :] + doubled(g, zd, p, planes))
        if x_old is not None:
            v = x_old[r, :] + v
        x[r, :] = v
        if xb is not None and planes == g.CH and 0 <= p < g.nx:
            put_blocks(xb, slice(p * g.NZ, p * g.NZ + n), v)
        t[r, :] = zy_sum(c[rr, :] * v, g.NZ)
    step = g.CH * g.NZ
    for p in range(0, g.nx, g.CH):
        at = p * g.NZ
        box = (
            t[at : at + step, :]
            + t[at + g.NZ : at + g.NZ + step, :]
            + t[at + 2 * g.NZ : at + 2 * g.NZ + step, :]
        )
        r = slice(at, at + step)
        rr = slice(OUT * g.NZ + at, OUT * g.NZ + at + step)
        v = bi[r, :] - D[rr, :] * x[at + g.NZ : at + g.NZ + step, :] + K[rr, :] * box
        keep(r, v, v * diag[r, :])


def send_defect(g, s, gi, rm, rl, res, to_l, to_r, to_l2, to_r2):
    sums = pair_sums(res, g.nx, g.NZ)
    rm[...] = to_mid(sums, 4.0)
    shape = (g.nxl * g.NZl, g.nxm * g.NZm)
    row, col = iota(shape, 0), iota(shape, 1)
    same_x = col // (2 * g.NZm) == row // g.NZl
    same_z = (col % g.NZm) // 2 == row % g.NZl
    rows = chosen(same_x & same_z, 0.25)
    shape = (g.WY, g.NYl)
    lanes = chosen(iota(shape, 0) // 4 + g.start(s) // 4 == iota(shape, 1))
    rl[...] = spread(gathered(rows, sums), lanes)
    at = 0
    for ref, n in ((gi, XH * g.NZ), (rm, MH * g.NZm), (rl, g.nxl * g.NZl)):
        total = ref.shape[0]
        for y in range(0, ref.shape[1], 128):
            to_l[at : at + n, :] = ref[0:n, y : y + 128]
            to_r[at : at + n, :] = ref[total - n :, y : y + 128]
            at += n
    far = (LH - g.nxl) * g.NZl
    total = rl.shape[0]
    for b in range(g.NYl // 128):
        lanes = slice(128 * b, 128 * b + 128)
        to_l2[b * far : b * far + far, :] = rl[0:far, lanes]
        to_r2[b * far : b * far + far, :] = rl[total - far :, lanes]


def first_kernel(g, idx, tab, *refs):
    f, m, l, f2nd, m2nd, from_l, from_r, from_l2nd, from_r2nd, from_l2, from_r2 = refs[:11]
    refs = refs[11:]
    (c, D, K, bi, diag, cm, Dm, Km, im, cl, Dl, Kl, il) = refs[:13]
    x, gi_own, rm, rl, to_l, to_r, to_l2, to_r2 = refs[13:21]
    (gi, y, d, t, gm, ym, dm, tm, gl, yl, dl, tl, zd, res) = refs[21:]
    s, li = idx[0], idx[1]
    clear_box_edges(g, t, tm, tl)
    fill = (0.0, 0.0, 1.0)

    def kept(ok, v, a):
        return jnp.where(ok, v, fill[a])

    n = XH * g.NZ
    lo, hi = OUT * g.NZ, (OUT + g.nx) * g.NZ
    at = {0: 0, 1: 0}
    region = (gi, c, y)
    for a in range(3):
        left, right = (from_l2nd, from_r2nd) if a else (from_l, from_r)
        q = min(a, 1)
        region[a][0 : lo - n, :] = jnp.full((lo - n, g.WY), fill[a], F32)
        region[a][hi + n :, :] = jnp.full((lo - n, g.WY), fill[a], F32)
        region[a][lo:hi, :] = f2nd[a - 1] if a else f[0]
        for yy in range(0, g.WY, 128):
            rows = slice(at[q], at[q] + n)
            region[a][lo - n : lo, yy : yy + 128] = kept(li > 0, left[rows, :], a)
            region[a][hi : hi + n, yy : yy + 128] = kept(
                li < g.nl - 1, right[rows, :], a
            )
            at[q] += n
    step = g.CH * g.NZ

    def build(k, carry):
        r = pl.ds(pl.multiple_of(k * step, step), step)
        b0 = gi[r, :]
        dg, inv, sc, kk = coefficients(b0, c[r, :], y[r, :])
        gi[r, :] = b0 * inv
        D[r, :] = sc
        K[r, :] = kk
        y[r, :] = dg
        return carry

    lax.fori_loop(0, g.PF // g.CH, build, 0)
    bi[...] = gi[lo:hi, :]
    diag[...] = y[lo:hi, :]

    n = MH * g.NZm
    parts = []
    for a in range(3):
        halves = []
        left, right = (from_l2nd, from_r2nd) if a else (from_l, from_r)
        q = min(a, 1)
        for _ in range(0, g.WYm, 128):
            rows = slice(at[q], at[q] + n)
            halves.append(
                (kept(li > 0, left[rows, :], a), kept(li < g.nl - 1, right[rows, :], a))
            )
            at[q] += n
        left = jnp.concatenate([v[0] for v in halves], axis=1)
        right = jnp.concatenate([v[1] for v in halves], axis=1)
        own_mid = m2nd[a - 1] if a else m[0]
        parts.append(jnp.concatenate([left, own_mid, right], axis=0))
    _, inv, sc, kk = coefficients(*parts)
    cm[...] = parts[1]
    Dm[...] = sc
    Km[...] = kk
    im[...] = inv
    gm[...] = 4.0 * parts[0] * inv

    n = g.nxl * g.NZl
    far = (LH - g.nxl) * g.NZl
    store = (gl, cl, il)
    at, at2 = at[0], 0
    for a in range(3):
        for yy in range(0, g.NYl, 128):
            lanes = slice(yy, yy + 128)
            ref = store[a]
            ref[0:far, lanes] = kept(li > 1, from_l2[at2 : at2 + far, :], a)
            ref[far : far + n, lanes] = kept(li > 0, from_l[at : at + n, :], a)
            ref[far + n : far + 2 * n, lanes] = l[a, :, lanes]
            ref[far + 2 * n : far + 3 * n, lanes] = kept(
                li < g.nl - 1, from_r[at : at + n, :], a
            )
            ref[far + 3 * n :, lanes] = kept(li < g.nl - 2, from_r2[at2 : at2 + far, :], a)
            at += n
            at2 += far
    _, inv, sc, kk = coefficients(gl[...], cl[...], il[...])
    Dl[...] = sc
    Kl[...] = kk
    il[...] = inv
    gl[...] = 16.0 * gl[...] * inv

    def keep(r, scaled, plain):
        gi_own[r, :] = scaled
        put_blocks(res, r, plain)

    fine = (gi, c, D, K, y, d, t)
    mid = (gm, cm, Dm, Km, ym, dm, tm)
    low = (gl, cl, Dl, Kl, yl, dl, tl)

    def gi_at(p):
        return gi[(OUT + p) * g.NZ : (OUT + p + 1) * g.NZ, :]

    cycle(g, idx, tab, gi_at, fine, mid, low, None, x, bi, diag, zd, keep)
    send_defect(g, s, gi_own, rm, rl, res, to_l, to_r, to_l2, to_r2)


def gather_defect(g, gi_own, rm, rl, from_l, from_r, from_l2, from_r2, gi, gm, im, gl, il):
    lo, hi = OUT * g.NZ, (OUT + g.nx) * g.NZ
    n = XH * g.NZ
    at = 0 if not g.unrolled else g.WY // 128 * n
    if not g.unrolled:
        zeros = jnp.zeros((lo - n, g.WY), F32)
        gi[0 : lo - n, :] = zeros
        gi[hi + n :, :] = zeros
        gi[lo:hi, :] = gi_own[...]
        for y in range(0, g.WY, 128):
            gi[lo - n : lo, y : y + 128] = from_l[at : at + n, :]
            gi[hi : hi + n, y : y + 128] = from_r[at : at + n, :]
            at += n
    n, own = MH * g.NZm, rm.shape[0]
    for y in range(0, g.WYm, 128):
        lanes = slice(y, y + 128)
        gm[0:n, lanes] = from_l[at : at + n, :] * im[0:n, lanes]
        gm[n + own :, lanes] = from_r[at : at + n, :] * im[n + own :, lanes]
        at += n
    gm[n : n + own, :] = rm[...] * im[n : n + own, :]
    n = g.nxl * g.NZl
    far = (LH - g.nxl) * g.NZl
    for b in range(g.NYl // 128):
        lanes = slice(128 * b, 128 * b + 128)
        rows = slice(b * far, b * far + far)
        gl[0:far, lanes] = from_l2[rows, :]
        gl[far : far + n, lanes] = from_l[at : at + n, :]
        gl[far + n : far + 2 * n, lanes] = rl[:, lanes]
        gl[far + 2 * n : far + 3 * n, lanes] = from_r[at : at + n, :]
        gl[far + 3 * n :, lanes] = from_r2[rows, :]
        at += n
    gl[...] = gl[...] * il[...]


def cycle_kernel(g, n_outs, idx, tab, *refs):
    gi_own, rm, rl, x_old = refs[:4]
    received = refs[4:8]
    (c, D, K, bi, diag, cm, Dm, Km, im, cl, Dl, Kl, il) = refs[8:21]
    outs = refs[21 : 21 + n_outs]
    scr = refs[21 + n_outs :]
    (gi, y, d, t, gm, ym, dm, tm, gl, yl, dl, tl, zd, res) = scr[:14]
    clear_box_edges(g, t, tm, tl)
    gather_defect(g, gi_own, rm, rl, *received, gi, gm, im, gl, il)
    fine = (gi, c, D, K, y, d, t)
    mid = (gm, cm, Dm, Km, ym, dm, tm)
    low = (gl, cl, Dl, Kl, yl, dl, tl)
    s = idx[0]

    def gi_at(p):
        if 0 <= p < g.nx:
            return gi_own[p * g.NZ : (p + 1) * g.NZ, :]
        part = received[0] if p < 0 else received[1]
        at = (p + XH if p < 0 else p - g.nx) * g.NZ
        step = XH * g.NZ
        return jnp.concatenate(
            [part[at + b * step : at + b * step + g.NZ, :] for b in range(g.WY // 128)],
            axis=1,
        )

    if len(scr) == 14:
        x, gi_new, rm_new, rl_new = outs[:4]

        def keep(r, scaled, plain):
            gi_new[r, :] = scaled
            put_blocks(res, r, plain)

        cycle(g, idx, tab, gi_at, fine, mid, low, x_old, x, bi, diag, zd, keep)
        send_defect(g, s, gi_new, rm_new, rl_new, res, *outs[4:])
        return
    x, xb = scr[14:]

    def keep_plain(r, scaled, plain):
        put_blocks(res, r, plain)

    cycle(g, idx, tab, gi_at, fine, mid, low, x_old, x, bi, diag, zd, keep_plain, xb)
    shift = lax.rem(g.WY - (s * g.ny - g.start(s)), g.WY)
    for k in range(g.ns):
        partner = lax.rem(s - k + g.ns, g.ns)
        for o, ref in enumerate((xb, res)):

            def row(z, o=o, ref=ref, k=k, partner=partner):
                v = blocks(ref, pl.ds(partner * g.nz + z, g.nx, stride=g.NZ))
                at = (o * g.nz + z) * g.nx
                if not isinstance(at, int):
                    at = pl.multiple_of(at, 8)
                outs[k][pl.ds(at, g.nx), :] = pltpu.roll(v, shift, 1)[:, : g.PW]

            repeat(g, g.nz, row)


def unpack_kernel(g, idx, *refs):
    s = idx[0]
    recv, outs = refs[: g.ns], refs[g.ns :]
    for o in range(2):
        for z in range(g.nz):
            at = (o * g.nz + z) * g.nx
            total = None
            if g.ny % 128 == 0:
                wide = jnp.concatenate(
                    [recv[j][at : at + g.nx, : g.ny] for j in range(g.ns)], axis=1
                )
                total = pltpu.roll(wide, s * g.ny, 1)
            else:
                mine = iota((g.nx, g.NY), 1) < g.ny
                for j in range(g.ns):
                    src = lax.rem(s + j, g.ns)
                    v = recv[j][at : at + g.nx, :]
                    pad = jnp.zeros((g.nx, g.NY - g.PW), F32)
                    v = jnp.where(mine, jnp.concatenate([v, pad], axis=1), 0.0)
                    v = pltpu.roll(v, src * g.ny, 1)
                    total = v if total is None else total + v
            outs[o][z] = total


def ring(value, axis, by):
    peers = lax.axis_size(axis)
    if by % peers == 0:
        return value
    return lax.ppermute(value, axis, [(i, (i - by) % peers) for i in range(peers)])


def sweep_tables(degrees, lower, upper):
    centre = (upper + lower) * 0.5
    radius = (upper - lower) * 0.5
    ratio = centre / radius
    rho = 1.0 / ratio
    alphas, betas = [], []
    for j in range(1, MAXDEG):
        new = 1.0 / (2.0 * ratio - rho)
        active = j < degrees
        alphas.append(jnp.where(active, new * rho, 0.0))
        betas.append(jnp.where(active, 2.0 * new / radius, 0.0))
        rho = new
    zero = jnp.zeros_like(rho)
    return jnp.stack([1.0 / centre] + alphas + [zero] + betas, axis=1)


def shards(right_side, scale_field, mass_field, degrees, lower_bound, upper_bound):
    g = Geometry(right_side.shape, lax.axis_size("slab"), lax.axis_size("level"))
    place = jnp.stack([lax.axis_index("slab"), lax.axis_index("level")])
    place = place.astype(jnp.int32)
    idx = jnp.concatenate([place, degrees])
    tab = sweep_tables(degrees, lower_bound, upper_bound)

    def call(kernel, outs, scratch, smem, *args):
        return vmem_call(lambda *refs: kernel(g, *refs), outs, scratch, smem, args)

    shape = right_side.shape
    packs = call(
        pack_kernel, [(g.rows_1st, g.WY)] * g.ns + [(g.rows_2nd, g.WY)] * g.ns, [], 1,
        place, jnp.stack([right_side, scale_field, mass_field]),
    )
    packs_1st, packs_2nd = [], []
    for k in range(g.ns):
        packs_1st.append(ring(packs[k], "slab", k))
    for k in range(g.ns):
        packs_2nd.append(ring(packs[g.ns + k], "slab", k))

    fine = (g.PF * g.NZ, g.WY)
    own = (g.nx * g.NZ, g.WY)
    mid = (g.PM * g.NZm, g.WYm)
    low = (g.PL * g.NZl, g.NYl)
    own_blocks = (g.WY // 128, own[0], 128)
    scratch = [
        fine, fine, fine, (fine[0] + 2 * g.NZ, g.WY),
        mid, mid, mid, (mid[0] + 2 * g.NZm, g.WYm),
        low, low, low, (low[0] + 2 * g.NZl, g.NYl),
        (g.WY // 128, (g.nxm + 2) * g.NZ, 128), own_blocks,
    ]

    def assemble(count, packs):
        outs = [
            (count, *own), (count, g.nxm * g.NZm, g.WYm),
            (edge_rows(g, count), 128), (edge_rows(g, count), 128),
        ] + [(3, g.nxl * g.NZl, g.NYl)] * (count == 1)
        return vmem_call(
            lambda *refs: assemble_kernel(g, count, *refs),
            outs, [(count, *own_blocks)], 1, (place, *packs),
        )

    f, m, to_left, to_right, l = assemble(1, packs_1st)
    far = (LH - g.nxl) * g.NZl
    lanes = g.NYl // 128

    def far_rows(part):
        parts = part.reshape(3, part.shape[1], lanes, 128)
        return parts.transpose(0, 2, 1, 3).reshape(3 * lanes * far, 128)

    from_l = ring(to_right, "level", -1)
    from_r = ring(to_left, "level", 1)
    from_l2 = ring(far_rows(l[:, l.shape[1] - far :]), "level", -2)
    from_r2 = ring(far_rows(l[:, :far]), "level", 2)

    f2nd, m2nd, to_left, to_right = assemble(2, packs_2nd)
    from_l2nd = ring(to_right, "level", -1)
    from_r2nd = ring(to_left, "level", 1)

    x_shape = ((g.nx + 2) * g.NZ, g.WY)
    rm_shape, rl_shape = (g.nxm * g.NZm, g.WYm), (g.nxl * g.NZl, g.NYl)
    sent = (
        XH * g.NZ * (g.WY // 128) + MH * g.NZm * (g.WYm // 128) + rl_shape[0] * lanes,
        128,
    )
    sent2 = (lanes * far, 128)
    state = [x_shape, own, rm_shape, rl_shape, sent, sent, sent2, sent2]
    outs = call(
        first_kernel, [fine] * 3 + [own] * 2 + [mid] * 4 + [low] * 4 + state, scratch, 2,
        idx, tab, f, m, l, f2nd, m2nd,
        from_l, from_r, from_l2nd, from_r2nd, from_l2, from_r2,
    )
    coefs, outs = outs[:13], outs[13:]
    for cycle_no in range(1, CYCLES):
        x, gi, rm, rl, to_l, to_r, to_l2, to_r2 = outs
        received = (
            ring(to_r, "level", -1),
            ring(to_l, "level", 1),
            ring(to_r2, "level", -2),
            ring(to_l2, "level", 2),
        )
        if cycle_no < CYCLES - 1:
            shapes, more = state, []
        else:
            shapes, more = [(2 * g.nz * g.nx, g.PW)] * g.ns, [x_shape, own_blocks]
        outs = vmem_call(
            lambda *refs, n=len(shapes): cycle_kernel(g, n, *refs),
            shapes, scratch + more, 2,
            (idx, tab, gi, rm, rl, x, *received, *coefs),
        )
    packs = []
    for k, v in enumerate(outs):
        packs.append(ring(v, "slab", k))
    return tuple(call(unpack_kernel, [shape, shape], [], 1, place, *packs))


def solution(mesh):
    spread = P("slab", "level", None)
    return jax.shard_map(
        shards,
        mesh=mesh,
        in_specs=(spread, spread, spread, P(), P(), P()),
        out_specs=(spread, spread),
        check_vma=False,
    )
```
